32 devices in a mesh: batch: 8 (over z, core), seq: 4 (over y, x).
Axes of the slice: x: 2, y: 2, z: 4, core: 2. Of those that a mesh axis runs over, the one named last changes fastest.
Arguments:
- inputs: bfloat16 [16, 2080, 1152], P('batch', 'seq'), may hold values from -6 to 6
- skip_inputs: bfloat16 [16, 2080, 1152], P('batch', 'seq'), may hold values from -6 to 6
- out_cotangent: bfloat16 [16, 2080, 1152], P('batch', 'seq'), may hold values from -6 to 6
- segments: int32 [16, 2080], P('batch'), may hold values from 0 to 8, as said below
- occupied: int32 [16, 2080], P('batch'), may hold values from 0 to 1, as said below
- skip_weight: bfloat16 [2304, 1152], P('batch', 'seq'), may hold values from -0.125 to 0.125
- skip_bias: bfloat16 [1152], P('seq'), may hold values from -3 to 3
- first_gain: bfloat16 [1152], P('seq'), may hold values from 0.25 to 1.75
- first_shift: bfloat16 [1152], P('seq'), may hold values from -3 to 3
- qkv_weight: bfloat16 [1152, 3456], P('batch', 'seq'), may hold values from -0.25 to 0.25
- proj_weight: bfloat16 [1152, 1152], P('batch', 'seq'), may hold values from -1.5 to 1.5
- proj_bias: bfloat16 [1152], P('seq'), may hold values from -3 to 3
- second_gain: bfloat16 [1152], P('seq'), may hold values from 0.25 to 1.75
- second_shift: bfloat16 [1152], P('seq'), may hold values from -3 to 3
- hidden_weight: bfloat16 [1152, 4608], P('batch', 'seq'), may hold values from -0.1875 to 0.1875
- hidden_bias: bfloat16 [4608], P('seq'), may hold values from -3 to 3
- down_weight: bfloat16 [4608, 1152], P('batch', 'seq'), may hold values from -0.125 to 0.125
- down_bias: bfloat16 [1152], P('seq'), may hold values from -3 to 3
Outputs:
- output: bfloat16 [16, 2080, 1152], P('batch', 'seq')
- input_grad: float32 [16, 2080, 1152], P('batch', 'seq')
- skip_grad: float32 [16, 2080, 1152], P('batch', 'seq')
- skip_weight_grad: float32 [2304, 1152], P('batch', 'seq')
- skip_bias_grad: float32 [1152], P('seq')
- first_gain_grad: float32 [1152], P('seq')
- first_shift_grad: float32 [1152], P('seq')
- qkv_weight_grad: float32 [1152, 3456], P('batch', 'seq')
- proj_weight_grad: float32 [1152, 1152], P('batch', 'seq')
- proj_bias_grad: float32 [1152], P('seq')
- second_gain_grad: float32 [1152], P('seq')
- second_shift_grad: float32 [1152], P('seq')
- hidden_weight_grad: float32 [1152, 4608], P('batch', 'seq')
- hidden_bias_grad: float32 [4608], P('seq')
- down_weight_grad: float32 [4608, 1152], P('batch', 'seq')
- down_bias_grad: float32 [1152], P('seq')
The draws below stay inside these ranges and needn't reach their ends.
Inputs may be any that keep to these rules, and one draw needn't show every extreme that they name: `segments`: each row holds whole items numbered 0, 1, 2, ... in order from slot 0: eight items of 258 slots, two of 1026, one of 1026 then four of 258, or one of 1026 then one of 258; each of these four kinds is some row's. The slots after the last item have id 8. `occupied`: 1 exactly on the slots of items, 0 on the slots after them.
All inputs are finite; a program needn't handle non-finite values.
Results may differ from the reference program's by a relative error of at most 0.02.
Values may be sent and summed in bfloat16 or wider, within the bound.
No kernel may reach another device: no remote copies, remote signals or barrier semaphores. Data moves between devices by JAX's collectives and lax.ppermute only.
A program may use at most 384 MiB of HBM per device.

```python
import jax
import jax.numpy as jnp
from jax import lax

MODEL = 1152
HEADS = 16
HEAD_DIM = 72
HIDDEN_SIZE = 4608
SLOTS = 2080
BIG = 1026
SMALL = 258
ITEMS_MAX = 8
ROWS = 16


def row_layout(key):
    row_order = jax.random.permutation(jax.random.fold_in(key, 7), ROWS)
    row_kind = (row_order % 4).astype(jnp.int32)[:, None]
    slot_index = jnp.arange(SLOTS, dtype=jnp.int32)[None, :]
    after_big = slot_index - BIG
    item_zero = slot_index // SMALL
    item_one = slot_index // BIG
    item_two = jnp.where(slot_index < BIG, 0, 1 + after_big // SMALL)
    item_three = jnp.where(slot_index < BIG, 0, 1)
    used_slots = jnp.where(row_kind == 0, 8 * SMALL, jnp.where(row_kind == 1, 2 * BIG, jnp.where(row_kind == 2, BIG + 4 * SMALL, BIG + SMALL)))
    item_index = jnp.where(row_kind == 0, item_zero, jnp.where(row_kind == 1, item_one, jnp.where(row_kind == 2, item_two, item_three)))
    return jnp.where(slot_index < used_slots, item_index, ITEMS_MAX).astype(jnp.int32)


def draw_segments(key, part):
    return row_layout(key)


def draw_occupied(key, part):
    return (row_layout(key) < ITEMS_MAX).astype(jnp.int32)


def shard_levels(own_key, dims, cuts, low, largest):
    def one(axis_at, blocks):
        steps = jax.random.uniform(jax.random.fold_in(jax.random.fold_in(own_key, 6), axis_at), (blocks,), jnp.float32, low / len(cuts), largest / len(cuts))
        return jnp.repeat(jnp.exp(steps), dims[axis_at] // blocks).reshape((-1,) + (1,) * (len(dims) - axis_at - 1))

    loudness = one(*cuts[0])
    for cut in cuts[1:]:
        loudness = loudness * one(*cut)
    return loudness


def normal_values(stream_key, dims, width, limit, cuts=(), kind=jnp.bfloat16):
    values = width * jax.random.normal(stream_key, dims, jnp.float32)
    if cuts:
        values = values * shard_levels(stream_key, dims, cuts, -0.22, 0.18)
    return jnp.clip(values, -limit, limit).astype(kind)


def setup_inputs(seed: int = 0) -> dict:
    arg_keys = jax.random.split(jax.random.key(seed), 19)
    return {
        "inputs": normal_values(arg_keys[0], (ROWS, SLOTS, MODEL), 1.0, 6.0, ((0, 8), (1, 4))),
        "skip_inputs": normal_values(arg_keys[1], (ROWS, SLOTS, MODEL), 1.0, 6.0, ((0, 8), (1, 4))),
        "out_cotangent": normal_values(arg_keys[2], (ROWS, SLOTS, MODEL), 1.0, 6.0, ((0, 8), (1, 4))),
        "segments": draw_segments(jax.random.fold_in(arg_keys[18], 71), 0),
        "occupied": draw_occupied(jax.random.fold_in(arg_keys[18], 71), 0),
        "skip_weight": normal_values(arg_keys[5], (2 * MODEL, MODEL), (2 * MODEL) ** -0.5, 0.125, ((0, 8), (1, 4))),
        "skip_bias": normal_values(arg_keys[6], (MODEL,), 0.5, 3.0, ((0, 4),)),
        "first_gain": jnp.clip(1.0 + 0.15 * jax.random.normal(arg_keys[7], (MODEL,), jnp.float32), 0.25, 1.75).astype(jnp.bfloat16),
        "first_shift": normal_values(arg_keys[8], (MODEL,), 0.3, 3.0, ((0, 4),)),
        "qkv_weight": normal_values(arg_keys[9], (MODEL, 3 * MODEL), (MODEL // 2) ** -0.5, 0.25, ((0, 8), (1, 4))),
        "proj_weight": normal_values(arg_keys[10], (MODEL, MODEL), (MODEL // 64) ** -0.5, 1.5, ((0, 8), (1, 4))),
        "proj_bias": normal_values(arg_keys[11], (MODEL,), 0.3, 3.0, ((0, 4),)),
        "second_gain": jnp.clip(1.0 + 0.15 * jax.random.normal(arg_keys[12], (MODEL,), jnp.float32), 0.25, 1.75).astype(jnp.bfloat16),
        "second_shift": normal_values(arg_keys[13], (MODEL,), 0.3, 3.0, ((0, 4),)),
        "hidden_weight": normal_values(arg_keys[14], (MODEL, HIDDEN_SIZE), MODEL ** -0.5, 0.1875, ((0, 8), (1, 4))),
        "hidden_bias": normal_values(arg_keys[15], (HIDDEN_SIZE,), 0.5, 3.0, ((0, 4),)),
        "down_weight": normal_values(arg_keys[16], (HIDDEN_SIZE, MODEL), (HIDDEN_SIZE // 2) ** -0.5, 0.125, ((0, 8), (1, 4))),
        "down_bias": normal_values(arg_keys[17], (MODEL,), 0.3, 3.0, ((0, 4),)),
    }


@jax.custom_vjp
def low(v):
    return lax.optimization_barrier(v.astype(jnp.bfloat16)).astype(jnp.float32)

@jax.custom_vjp
def low_back(v):
    return v

def low_keep(v):
    return (low(v), None)

def low_pass(kept, grad):
    return (grad,)

def back_keep(v):
    return (v, None)

def back_low(kept, grad):
    return (low(grad),)
low.defvjp(low_keep, low_pass)
low_back.defvjp(back_keep, back_low)
epsilon = 1e-05
masked_score = -1e+30

def high_dot(left_side, right_side):
    return jnp.dot(left_side, right_side, precision=lax.Precision.HIGHEST)

def layer_norm(stream, norm_gain, norm_shift):
    centred = stream - lax.optimization_barrier(jnp.mean(stream, axis=-1, keepdims=True))
    spread = lax.optimization_barrier(jnp.mean(centred * centred, axis=-1, keepdims=True))
    return centred * lax.rsqrt(spread + epsilon) * norm_gain + norm_shift

def block_row(weight_list, row_input, row_skip, segment_row, occupied_row):
    skip_weight, skip_bias, first_gain, first_shift, qkv_weight, proj_weight, proj_bias, second_gain, second_shift, hidden_weight, hidden_bias, down_weight, down_bias = weight_list
    joined = jnp.concatenate([row_input, row_skip], axis=-1)
    stream = low_back(high_dot(joined, skip_weight) + skip_bias)
    first_low = low(layer_norm(stream, first_gain, first_shift))
    mixed_qkv = low(low_back(high_dot(first_low, qkv_weight)))
    shaped = mixed_qkv.reshape(SLOTS, 3, HEADS, HEAD_DIM).transpose(1, 2, 0, 3)
    scores = jnp.einsum('hqd,hkd->hqk', shaped[0], shaped[1], precision=lax.Precision.HIGHEST) * HEAD_DIM ** (-0.5)
    scores = low_back(scores)
    slot_index = jnp.arange(SLOTS)
    allowed = (segment_row[:, None] == segment_row[None, :]) & (occupied_row[None, :] > 0) | (slot_index[:, None] == slot_index[None, :])
    scores = jnp.where(allowed[None], scores, masked_score)
    soft_low = low(jax.nn.softmax(scores, axis=-1))
    attended = jnp.einsum('hqk,hkd->hqd', soft_low, shaped[2], precision=lax.Precision.HIGHEST)
    attended = low(low_back(attended)).transpose(1, 0, 2).reshape(SLOTS, HEADS * HEAD_DIM)
    middle = stream + low_back(high_dot(attended, proj_weight) + proj_bias)
    second_low = low(layer_norm(middle, second_gain, second_shift))
    activated = low(jax.nn.gelu(low_back(high_dot(second_low, hidden_weight) + hidden_bias), approximate=False))
    return middle + low_back(high_dot(activated, down_weight) + down_bias)

def add_pair(first_sum, second_sum):
    return first_sum + second_sum

def reference(inputs, skip_inputs, out_cotangent, segments, occupied, skip_weight, skip_bias, first_gain, first_shift, qkv_weight, proj_weight, proj_bias, second_gain, second_shift, hidden_weight, hidden_bias, down_weight, down_bias):
    weights = tuple((weight_arg.astype(jnp.float32) for weight_arg in (skip_weight, skip_bias, first_gain, first_shift, qkv_weight, proj_weight, proj_bias, second_gain, second_shift, hidden_weight, hidden_bias, down_weight, down_bias)))

    def one_row(totals, row_parts):
        row_input, row_skip, row_cotangent, segment_row, occupied_row = row_parts

        def forward(weight_list, first_input, second_input):
            return block_row(weight_list, first_input, second_input, segment_row, occupied_row)
        result, pullback = jax.vjp(forward, weights, row_input.astype(jnp.float32), row_skip.astype(jnp.float32))
        masked_cot = row_cotangent.astype(jnp.float32) * occupied_row[:, None].astype(jnp.float32)
        weight_grads, input_grad, skip_grad = pullback(masked_cot)
        totals = jax.tree.map(add_pair, totals, weight_grads)
        return (totals, (result.astype(jnp.bfloat16), input_grad, skip_grad))
    zeros_start = tuple((jnp.zeros(weight_arg.shape, jnp.float32) for weight_arg in weights))
    totals, (output, input_grad, skip_grad) = lax.scan(one_row, zeros_start, (inputs, skip_inputs, out_cotangent, segments, occupied))
    return (output, input_grad, skip_grad, totals[0], totals[1], totals[2], totals[3], totals[4], totals[5], totals[6], totals[7], totals[8], totals[9], totals[10], totals[11], totals[12])
```

```python
import jax
import jax.numpy as jnp
from jax import lax
from jax.experimental import pallas as pl
from jax.experimental.pallas import tpu as pltpu
from jax.sharding import PartitionSpec as P

HEADS = 16
HEAD_DIM = 72
LANES = 128
epsilon = 1e-05
masked_score = -1e30
VMEM_BYTES = 60 * 1024 * 1024
def nt_dot(left_side, right_side):
    return lax.dot_general(
        left_side, right_side, (((1,), (1,)), ((), ())), preferred_element_type=jnp.float32
    )


def tn_dot(left_side, right_side):
    return lax.dot_general(
        left_side, right_side, (((0,), (0,)), ((), ())), preferred_element_type=jnp.float32
    )


def nn_dot(left_side, right_side):
    return lax.dot_general(
        left_side, right_side, (((1,), (0,)), ((), ())), preferred_element_type=jnp.float32
    )


def split_heads(wide, head_ref, start=0):
    rows = wide.shape[0]
    pad = jnp.zeros((rows, LANES - HEAD_DIM), wide.dtype)
    for head in range(HEADS):
        piece = wide[:, head * HEAD_DIM : (head + 1) * HEAD_DIM]
        head_ref[head, start : start + rows] = jnp.concatenate([piece, pad], axis=1)


def split_keys(own_ref, far_ref, kh, vh):
    features = own_ref.shape[2] // 2
    start = 0
    for ref in (own_ref, far_ref):
        split_heads(ref[0, :, :features], kh, start)
        split_heads(ref[0, :, features:], vh, start)
        start += ref.shape[1]


def join_heads(head_ref):
    return jnp.concatenate([head_ref[head][:, :HEAD_DIM] for head in range(HEADS)], axis=1)


def chunk_of(rows):
    for count in (4, 2, 1):
        if rows % (count * 16) == 0:
            return rows // count
    return rows


def attend_kernel(
    q_ref, own_ref, far_ref, qid_ref, kid_ref, old_out, old_lse, out_ref, lse_ref,
    qh, kh, vh, score, prob,
):
    split_heads(q_ref[0], qh)
    split_keys(own_ref, far_ref, kh, vh)
    key_rows = kh.shape[1]
    step = chunk_of(key_rows)
    scale = HEAD_DIM ** (-0.5)
    query_ids = qid_ref[0]

    def one_head(head, carry):
        query = qh[head]
        top = jnp.full((1, query.shape[0]), masked_score, jnp.float32)
        for start in range(0, key_rows, step):
            part = nt_dot(kh[head, start : start + step], query) * scale
            part = jnp.where(kid_ref[0, start : start + step] == query_ids, part, masked_score)
            score[start : start + step] = part
            top = jnp.maximum(top, jnp.max(part, axis=0, keepdims=True))
        total = jnp.zeros_like(top)
        for start in range(0, key_rows, step):
            part = jnp.exp(score[start : start + step] - top)
            total = total + jnp.sum(part, axis=0, keepdims=True)
            prob[start : start + step] = part.astype(jnp.bfloat16)
        mixed = tn_dot(vh[head], prob[...]) / total
        qh[head] = mixed.T.astype(jnp.bfloat16)
        lse_ref[0, pl.ds(head, 1)] = top + jnp.log(total)
        return carry

    lax.fori_loop(0, HEADS, one_head, 0)
    out_ref[0] = join_heads(qh)


def attend(query, own, far, query_ids, key_ids, row, out, level):
    rows, width, features = query.shape
    far_rows = far.shape[1]
    key_rows = width + far_rows
    here = lambda i: (row, 0, 0)
    only = lambda i: (0, 0, 0)
    wide = pl.BlockSpec((1, width, features), here)
    levels = pl.BlockSpec((1, HEADS, width), here)
    return pl.pallas_call(
        attend_kernel,
        grid=(1,),
        in_specs=[
            wide,
            pl.BlockSpec((1, width, 2 * features), here),
            pl.BlockSpec((1, far_rows, 2 * features), only),
            pl.BlockSpec((1, 1, width), here),
            pl.BlockSpec((1, key_rows, 1), here),
            pl.BlockSpec(memory_space=pl.ANY),
            pl.BlockSpec(memory_space=pl.ANY),
        ],
        out_specs=[wide, levels],
        out_shape=[
            jax.ShapeDtypeStruct((rows, width, features), jnp.bfloat16),
            jax.ShapeDtypeStruct((rows, HEADS, width), jnp.float32),
        ],
        scratch_shapes=[
            pltpu.VMEM((HEADS, width, LANES), jnp.bfloat16),
            pltpu.VMEM((HEADS, key_rows, LANES), jnp.bfloat16),
            pltpu.VMEM((HEADS, key_rows, LANES), jnp.bfloat16),
            pltpu.VMEM((key_rows, width), jnp.float32),
            pltpu.VMEM((key_rows, width), jnp.bfloat16),
        ],
        input_output_aliases={5: 0, 6: 1},
        compiler_params=pltpu.CompilerParams(vmem_limit_bytes=VMEM_BYTES),
        cost_estimate=pl.CostEstimate(
            flops=4 * HEADS * width * key_rows * LANES,
            transcendentals=HEADS * width * key_rows,
            bytes_accessed=4 * features * (width + key_rows),
        ),
        name="attend",
    )(query, own, far, query_ids[:, None, :], key_ids[:, :, None], out, level)


def attend_back_kernel(
    q_ref, own_ref, far_ref, o_ref, g_ref, lse_ref, qid_ref, kid_ref, old_dq, old_dkv,
    dq_ref, dkv_ref, qh, kh, vh, oh, gh, prob, slope,
):
    split_heads(q_ref[0], qh)
    features = q_ref.shape[2]
    split_keys(own_ref, far_ref, kh, vh)
    split_heads(o_ref[0], oh)
    split_heads(g_ref[0], gh)
    key_rows = kh.shape[1]
    step = chunk_of(key_rows)
    scale = HEAD_DIM ** (-0.5)
    query_ids = qid_ref[0]

    def one_head(head, carry):
        query = qh[head]
        grad = gh[head]
        level = lse_ref[0, pl.ds(head, 1)]
        overlap = oh[head].astype(jnp.float32) * grad.astype(jnp.float32)
        row_dot = jnp.sum(overlap.T, axis=0, keepdims=True)
        for start in range(0, key_rows, step):
            part = nt_dot(kh[head, start : start + step], query) * scale
            part = jnp.where(kid_ref[0, start : start + step] == query_ids, part, masked_score)
            soft = jnp.exp(part - level)
            prob[start : start + step] = soft.astype(jnp.bfloat16)
            turn = nt_dot(vh[head, start : start + step], grad)
            slope[start : start + step] = (soft * (turn - row_dot)).astype(jnp.bfloat16)
        value_grad = nn_dot(prob[...], grad)
        query_grad = tn_dot(kh[head], slope[...]) * scale
        key_grad = nn_dot(slope[...], query) * scale
        vh[head] = value_grad.astype(jnp.bfloat16)
        kh[head] = key_grad.astype(jnp.bfloat16)
        qh[head] = query_grad.T.astype(jnp.bfloat16)
        return carry

    lax.fori_loop(0, HEADS, one_head, 0)
    dq_ref[0] = join_heads(qh)
    dkv_ref[0, :, :features] = join_heads(kh)
    dkv_ref[0, :, features:] = join_heads(vh)


def attend_back(
    query, own, far, mixed, grad, level, query_ids, key_ids, row, query_grad, both_grad
):
    rows, width, features = query.shape
    far_rows = far.shape[1]
    key_rows = width + far_rows
    here = lambda i: (row, 0, 0)
    only = lambda i: (0, 0, 0)
    wide = pl.BlockSpec((1, width, features), here, pipeline_mode=pl.Buffered(1))
    return pl.pallas_call(
        attend_back_kernel,
        grid=(1,),
        in_specs=[
            wide,
            pl.BlockSpec((1, width, 2 * features), here, pipeline_mode=pl.Buffered(1)),
            pl.BlockSpec((1, far_rows, 2 * features), only, pipeline_mode=pl.Buffered(1)),
            wide,
            wide,
            pl.BlockSpec((1, HEADS, width), here),
            pl.BlockSpec((1, 1, width), here),
            pl.BlockSpec((1, key_rows, 1), here),
            pl.BlockSpec(memory_space=pl.ANY),
            pl.BlockSpec(memory_space=pl.ANY),
        ],
        out_specs=[
            pl.BlockSpec((1, width, features), here),
            pl.BlockSpec((1, key_rows, 2 * features), here),
        ],
        out_shape=[
            jax.ShapeDtypeStruct((rows, width, features), jnp.bfloat16),
            jax.ShapeDtypeStruct((rows, key_rows, 2 * features), jnp.bfloat16),
        ],
        scratch_shapes=[
            pltpu.VMEM((HEADS, width, LANES), jnp.bfloat16),
            pltpu.VMEM((HEADS, key_rows, LANES), jnp.bfloat16),
            pltpu.VMEM((HEADS, key_rows, LANES), jnp.bfloat16),
            pltpu.VMEM((HEADS, width, LANES), jnp.bfloat16),
            pltpu.VMEM((HEADS, width, LANES), jnp.bfloat16),
            pltpu.VMEM((key_rows, width), jnp.bfloat16),
            pltpu.VMEM((key_rows, width), jnp.bfloat16),
        ],
        input_output_aliases={8: 0, 9: 1},
        compiler_params=pltpu.CompilerParams(vmem_limit_bytes=VMEM_BYTES),
        cost_estimate=pl.CostEstimate(
            flops=10 * HEADS * width * key_rows * LANES,
            transcendentals=HEADS * width * key_rows,
            bytes_accessed=8 * features * (width + key_rows),
        ),
        name="attend_back",
    )(
        query,
        own,
        far,
        mixed,
        grad,
        level,
        query_ids[:, None, :],
        key_ids[:, :, None],
        query_grad,
        both_grad,
    )


def weight_grad_kernel(outer, here_ref, left_ref, right_ref, keep_ref, give_ref, total):
    total[...] = tn_dot(left_ref[...], right_ref[...]).astype(jnp.bfloat16)
    inner = total.shape[0] // (2 * outer)
    here = here_ref[0]
    for group in range(outer):
        start = group * 2 * inner
        mine = pl.multiple_of(start + here * inner, 16)
        other = pl.multiple_of(start + (1 - here) * inner, 16)
        span = slice(group * inner, (group + 1) * inner)
        keep_ref[span] = total[pl.ds(mine, inner)]
        give_ref[span] = total[pl.ds(other, inner)]


def weight_grad(left, right, here, outer, row_blocks, column_blocks, name):
    tokens = left.shape[0]
    model = left.shape[1] // row_blocks
    width = right.shape[1] // column_blocks
    half = jax.ShapeDtypeStruct((left.shape[1] // 2, right.shape[1]), jnp.bfloat16)
    spec = pl.BlockSpec((model // 2, width), lambda i, j, here: (i, j))
    return pl.pallas_call(
        lambda *refs: weight_grad_kernel(outer, *refs),
        grid_spec=pltpu.PrefetchScalarGridSpec(
            num_scalar_prefetch=1,
            grid=(row_blocks, column_blocks),
            in_specs=[
                pl.BlockSpec((tokens, model), lambda i, j, here: (0, i)),
                pl.BlockSpec((tokens, width), lambda i, j, here: (0, j)),
            ],
            out_specs=[spec, spec],
            scratch_shapes=[pltpu.VMEM((model, width), jnp.bfloat16)],
        ),
        out_shape=[half, half],
        compiler_params=pltpu.CompilerParams(vmem_limit_bytes=VMEM_BYTES),
        cost_estimate=pl.CostEstimate(
            flops=2 * tokens * left.shape[1] * right.shape[1],
            transcendentals=0,
            bytes_accessed=2 * (tokens + right.shape[1]) * (left.shape[1] + right.shape[1]),
        ),
        name=name,
    )(here.astype(jnp.int32).reshape(1), left, right)


def column_chunks(width):
    cut = width // 256 // 2 * 256
    return ((0, cut), (cut, width)) if cut else ((0, width),)


def middle_kernel(
    stream_ref, att_ref, cot_ref, used_ref, proj_ref, hidden_ref, down_ref,
    proj_bias_ref, gain_ref, shift_ref, hidden_bias_ref, down_bias_ref,
    out_ref, second_ref, act_ref, pre_ref, middle_grad_ref, proj_grad_ref, att_grad_ref,
    hidden_sum_ref, sums_ref,
    low, normal, scale, branch, total, back,
):
    step = pl.program_id(1)
    steps = pl.num_programs(1)

    @pl.when(step == 0)
    def _():
        middle = stream_ref[...] + nn_dot(att_ref[...], proj_ref[...]) + proj_bias_ref[...]
        centred = middle - jnp.mean(middle, axis=-1, keepdims=True)
        inverse = lax.rsqrt(jnp.mean(centred * centred, axis=-1, keepdims=True) + epsilon)
        unit = centred * inverse
        normal[...] = unit
        scale[...] = inverse
        second = (unit * gain_ref[...] + shift_ref[...]).astype(jnp.bfloat16)
        low[...] = second
        second_ref[...] = second
        branch[...] = (cot_ref[...].astype(jnp.float32) * used_ref[...]).astype(jnp.bfloat16)
        total[...] = middle + down_bias_ref[...]
        back[...] = jnp.zeros_like(back)

    for start, stop in column_chunks(hidden_ref.shape[2]):
        pre_act = nn_dot(low[...], hidden_ref[0, :, start:stop]) + hidden_bias_ref[0, :, start:stop]
        grad_act = nt_dot(branch[...], down_ref[0, start:stop])
        below = 0.5 + 0.5 * lax.erf(pre_act * (0.5**0.5))
        density = jnp.exp(-0.5 * pre_act * pre_act) * ((2.0 * jnp.pi) ** -0.5)
        act = (pre_act * below).astype(jnp.bfloat16)
        grad_pre = (grad_act * (below + pre_act * density)).astype(jnp.bfloat16)
        act_ref[:, start:stop] = act
        pre_ref[:, start:stop] = grad_pre
        hidden_sum_ref[0, 0, :, start:stop] = jnp.sum(
            grad_pre.astype(jnp.float32), axis=0, keepdims=True
        )
        total[...] += nn_dot(act, down_ref[0, start:stop])
        back[...] += nt_dot(grad_pre, hidden_ref[0, :, start:stop])

    @pl.when(step == steps - 1)
    def _():
        out_ref[...] = total[...].astype(jnp.bfloat16)
        grad = back[...]
        unit = normal[...]
        part = grad * gain_ref[...]
        mean_part = jnp.mean(part, axis=-1, keepdims=True)
        mean_both = jnp.mean(part * unit, axis=-1, keepdims=True)
        grad_out = cot_ref[...].astype(jnp.float32) * used_ref[...]
        grad_middle = grad_out + (part - mean_part - unit * mean_both) * scale[...]
        middle_grad_ref[...] = grad_middle
        grad_low = grad_middle.astype(jnp.bfloat16)
        proj_grad_ref[...] = grad_low
        att_grad_ref[...] = nt_dot(grad_low, proj_ref[...]).astype(jnp.bfloat16)
        sums_ref[0, 0:1] = jnp.sum(grad * unit, axis=0, keepdims=True)
        sums_ref[0, 1:2] = jnp.sum(grad, axis=0, keepdims=True)
        sums_ref[0, 2:3] = jnp.sum(grad_low.astype(jnp.float32), axis=0, keepdims=True)
        sums_ref[0, 3:4] = jnp.sum(grad_out, axis=0, keepdims=True)


def token_block(tokens):
    return tokens // 4 if tokens % 64 == 0 else tokens


def middle_block(
    stream, attended, cotangent, used, proj, hidden, down, proj_bias, gain, shift, hidden_bias,
    down_bias,
):
    tokens, model = stream.shape
    steps = hidden.shape[0]
    rows = token_block(tokens)
    blocks = tokens // rows
    by_rows = pl.BlockSpec((rows, model), lambda i, s: (i, 0))
    by_step = pl.BlockSpec((rows, model), lambda i, s: (i, s))
    vector = pl.BlockSpec((1, model), lambda i, s: (0, 0))
    low_rows = jax.ShapeDtypeStruct((tokens, model), jnp.bfloat16)
    low_steps = jax.ShapeDtypeStruct((tokens, steps * model), jnp.bfloat16)
    flops = 2 * tokens * model * model * (4 * steps + 2)
    return pl.pallas_call(
        middle_kernel,
        grid=(blocks, steps),
        in_specs=[
            by_rows,
            by_rows,
            by_rows,
            pl.BlockSpec((rows, 1), lambda i, s: (i, 0)),
            pl.BlockSpec((model, model), lambda i, s: (0, 0), pipeline_mode=pl.Buffered(1)),
            pl.BlockSpec((1, model, model), lambda i, s: (s, 0, 0)),
            pl.BlockSpec((1, model, model), lambda i, s: (s, 0, 0)),
            vector,
            vector,
            vector,
            pl.BlockSpec((1, 1, model), lambda i, s: (s, 0, 0)),
            vector,
        ],
        out_specs=[
            by_rows,
            by_rows,
            by_step,
            by_step,
            by_rows,
            by_rows,
            by_rows,
            pl.BlockSpec((1, 1, 1, model), lambda i, s: (i, s, 0, 0)),
            pl.BlockSpec((1, 4, model), lambda i, s: (i, 0, 0)),
        ],
        out_shape=[
            low_rows,
            low_rows,
            low_steps,
            low_steps,
            jax.ShapeDtypeStruct((tokens, model), jnp.float32),
            low_rows,
            low_rows,
            jax.ShapeDtypeStruct((blocks, steps, 1, model), jnp.float32),
            jax.ShapeDtypeStruct((blocks, 4, model), jnp.float32),
        ],
        scratch_shapes=[
            pltpu.VMEM((rows, model), jnp.bfloat16),
            pltpu.VMEM((rows, model), jnp.float32),
            pltpu.VMEM((rows, 1), jnp.float32),
            pltpu.VMEM((rows, model), jnp.bfloat16),
            pltpu.VMEM((rows, model), jnp.float32),
            pltpu.VMEM((rows, model), jnp.float32),
        ],
        compiler_params=pltpu.CompilerParams(vmem_limit_bytes=VMEM_BYTES),
        cost_estimate=pl.CostEstimate(
            flops=flops,
            transcendentals=2 * tokens * model * steps,
            bytes_accessed=2 * tokens * model * (2 * steps + 12) + 4 * model * model * steps * blocks,
        ),
        name="middle_block",
    )(
        stream,
        attended,
        cotangent,
        used,
        proj,
        hidden,
        down,
        proj_bias[None],
        gain[None],
        shift[None],
        hidden_bias.reshape(steps, 1, model),
        down_bias[None],
    )


def layer_norm(stream, norm_gain, norm_shift):
    centred = stream - jnp.mean(stream, axis=-1, keepdims=True)
    scale = lax.rsqrt(jnp.mean(centred * centred, axis=-1, keepdims=True) + epsilon)
    normal = centred * scale
    return (normal * norm_gain + norm_shift).astype(jnp.bfloat16), normal, scale


def layer_norm_back(grad, normal, scale, norm_gain):
    part = grad * norm_gain
    mean_part = jnp.mean(part, axis=-1, keepdims=True)
    mean_both = jnp.mean(part * normal, axis=-1, keepdims=True)
    gain_grad = jnp.sum(grad * normal, axis=(0, 1))
    shift_grad = jnp.sum(grad, axis=(0, 1))
    return (part - mean_part - normal * mean_both) * scale, gain_grad, shift_grad


def outer_dot(left_side, right_side):
    return lax.dot_general(
        left_side, right_side, (((0,), (0,)), ((), ())), preferred_element_type=jnp.bfloat16
    )


def dot_last(left_side, right_side):
    return lax.dot_general(
        left_side, right_side, (((2,), (0,)), ((), ())), preferred_element_type=jnp.float32
    )


def dot_back(left_side, right_side):
    return lax.dot_general(
        left_side, right_side, (((2,), (1,)), ((), ())), preferred_element_type=jnp.float32
    )


def dot_tokens(left_side, right_side):
    return lax.dot_general(
        left_side, right_side, (((0, 1), (0, 1)), ((), ())), preferred_element_type=jnp.bfloat16
    )


class Grid:
    def __init__(self):
        self.batch_count = lax.axis_size("batch")
        self.seq_count = lax.axis_size("seq")
        self.seq_index = lax.axis_index("seq")
        batch_index = lax.axis_index("batch")
        self.outer_count = self.batch_count // 2
        self.square = self.seq_count == 4 and self.outer_count == 4
        self.at = {
            "z": batch_index // 2,
            "c": batch_index % 2,
            "y": self.seq_index // 2,
            "x": self.seq_index % 2,
        }

    def index(self, z, c, s):
        return (z * 2 + c) * self.seq_count + s

    def send(self, value, axis, turn=1):
        pairs = []
        for z in range(self.outer_count):
            for c in range(2):
                for s in range(self.seq_count):
                    far_z, far_c, far_s = z, c, s
                    if axis == "z":
                        far_z = (z + turn) % self.outer_count
                    elif axis == "c":
                        far_c = 1 - c
                    elif axis == "y":
                        far_s = s ^ 2
                    else:
                        far_s = s ^ 1
                    pairs.append((self.index(z, c, s), self.index(far_z, far_c, far_s)))
        return lax.ppermute(value, ("batch", "seq"), pairs)

    def shift(self, value, source, target):
        pairs = [
            (b * self.seq_count + source, b * self.seq_count + target)
            for b in range(self.batch_count)
        ]
        return lax.ppermute(value, ("batch", "seq"), pairs)


def tie(value, *others):
    return lax.optimization_barrier((value, others))[0]


def square_gather(grid, shard):
    over_x = grid.send(shard, "x")
    found = jnp.stack([shard, over_x, grid.send(shard, "y"), grid.send(over_x, "y")])
    return jnp.stack(
        [
            lax.dynamic_index_in_dim(found, grid.seq_index ^ place, 0, keepdims=False)
            for place in range(4)
        ]
    )


def pack_lanes(shard):
    rows, columns = shard.shape
    whole = columns // LANES
    rest = columns - whole * LANES
    pieces = [shard[:, k * LANES : (k + 1) * LANES] for k in range(whole)]
    if rest:
        fold = LANES // rest
        step = rows // fold
        last = [shard[k * step : (k + 1) * step, whole * LANES :] for k in range(fold)]
        pieces.append(jnp.concatenate(last, axis=1))
    return jnp.concatenate(pieces, axis=0)


def unpack_lanes(packed, rows, columns):
    whole = columns // LANES
    rest = columns - whole * LANES
    pieces = [packed[k * rows : (k + 1) * rows] for k in range(whole)]
    if rest:
        fold = LANES // rest
        last = packed[whole * rows : whole * rows + rows // fold]
        pieces.append(
            jnp.concatenate([last[:, k * rest : (k + 1) * rest] for k in range(fold)], axis=0)
        )
    return jnp.concatenate(pieces, axis=1)


def rows_kernel(rows, columns, turn_ref, to_ref, *refs):
    blocks, out_ref, found = refs[:8], refs[8], refs[9]
    for block in range(8):
        found[to_ref[block]] = blocks[block][...]
    for core in range(2):
        wide = [unpack_lanes(found[core * 4 + place], rows, columns) for place in range(4)]
        out_ref[core * rows : (core + 1) * rows] = jnp.concatenate(wide, axis=1)


def mixed_kernel(columns, turn_ref, to_ref, *refs):
    blocks, query_ref, both_ref, proj_ref, found = refs[:8], refs[8], refs[9], refs[10], refs[11]
    rows, model = found.shape[1:]
    for block in range(8):
        found[to_ref[block]] = blocks[block][...]
    for core in range(2):
        span = slice(core * rows, (core + 1) * rows)
        parts = [found[core * 4 + place] for place in range(4)]
        wide = jnp.concatenate([part[:, :columns] for part in parts], axis=1)
        query_ref[span] = wide[:, :model]
        both_ref[span] = wide[:, model:]
        proj_ref[span] = jnp.concatenate([part[:, columns:] for part in parts], axis=1)


def assemble(grid, blocks, piece, kernel, widths, rows, name):
    outer = grid.outer_count
    turns = jnp.stack([(grid.at["z"] - z + outer) % outer for z in range(outer)])
    places = [
        (grid.at["c"] ^ (block >> 2)) * 4 + (grid.seq_index ^ (block & 3)) for block in range(8)
    ]
    shapes = [jax.ShapeDtypeStruct((outer * 2 * rows, w), jnp.bfloat16) for w in widths]
    result = pl.pallas_call(
        kernel,
        grid_spec=pltpu.PrefetchScalarGridSpec(
            num_scalar_prefetch=2,
            grid=(outer,),
            in_specs=[pl.BlockSpec(piece, lambda z, turn, to: (turn[z], 0))] * 8,
            out_specs=[pl.BlockSpec((2 * rows, w), lambda z, turn, to: (z, 0)) for w in widths],
            scratch_shapes=[pltpu.VMEM((8,) + piece, jnp.bfloat16)],
        ),
        out_shape=shapes,
        compiler_params=pltpu.CompilerParams(vmem_limit_bytes=VMEM_BYTES),
        cost_estimate=pl.CostEstimate(
            flops=0,
            transcendentals=0,
            bytes_accessed=8 * outer * rows * sum(widths),
        ),
        name=name,
    )(turns.astype(jnp.int32), jnp.stack(places).astype(jnp.int32), *blocks)
    return result


def place_kernel(block_count, outer_count, to_ref, *refs):
    blocks, out_ref, sems = refs[:block_count], refs[block_count], refs[block_count + 1]
    rows = out_ref.shape[1]
    copies = []
    for block in range(block_count):
        for turn in range(outer_count):
            slot = block * outer_count + turn
            copies.append(
                pltpu.make_async_copy(
                    blocks[block].at[pl.ds(turn * rows, rows)], out_ref.at[to_ref[slot]], sems.at[slot]
                )
            )
    for copy in copies:
        copy.start()
    for copy in copies:
        copy.wait()


def place_blocks(grid, blocks):
    outer = grid.outer_count
    rows, columns = blocks[0].shape[0] // outer, blocks[0].shape[1]
    slots = []
    for block in range(8):
        core, place = grid.at["c"] ^ (block >> 2), grid.seq_index ^ (block & 3)
        for turn in range(outer):
            far = (grid.at["z"] - turn + outer) % outer
            slots.append((place * outer + far) * 2 + core)
    count = 8 * outer
    return pl.pallas_call(
        lambda *refs: place_kernel(8, outer, *refs),
        grid_spec=pltpu.PrefetchScalarGridSpec(
            num_scalar_prefetch=1,
            grid=(1,),
            in_specs=[pl.BlockSpec(memory_space=pl.ANY)] * 8,
            out_specs=pl.BlockSpec((count, rows, columns), lambda i, to: (0, 0, 0)),
            scratch_shapes=[pltpu.SemaphoreType.DMA((count,))],
        ),
        compiler_params=pltpu.CompilerParams(vmem_limit_bytes=VMEM_BYTES),
        out_shape=jax.ShapeDtypeStruct((count, rows, columns), blocks[0].dtype),
        cost_estimate=pl.CostEstimate(
            flops=0, transcendentals=0, bytes_accessed=4 * count * rows * columns
        ),
        name="place_blocks",
    )(jnp.stack(slots).astype(jnp.int32), *blocks)


def column_gather(grid, piece, *extra):
    parts = [piece] + [grid.send(piece, "z", turn) for turn in range(1, grid.outer_count)]
    return jnp.concatenate(parts + list(extra), axis=0)


def seq_gather(grid, column, first):
    if first == "x":
        over_x = grid.send(column, "x")
        return [column, over_x, grid.send(column, "y"), grid.send(over_x, "y")]
    over_y = grid.send(column, "y")
    return [column, grid.send(column, "x"), over_y, grid.send(over_y, "x")]


def core_gather(grid, blocks):
    return blocks + [grid.send(block, "c") for block in blocks]


def columns_of_seq(grid, piece):
    rows, columns = piece.shape
    split = piece.reshape(rows, 4, columns // 4).transpose(1, 0, 2)
    mixed = lax.all_to_all(split, "seq", 0, 0)
    return mixed.reshape(4 * rows, columns // 4)


def split_vectors(joint, widths):
    result, start = [], 0
    for width in widths:
        result.append(joint[:, start : start + width].reshape(-1).astype(jnp.float32))
        start += width
    return result


def gather_all(grid, matrices, vectors):
    skip_weight, qkv_weight, proj_weight, hidden_weight, down_weight = matrices
    widths = [vector.shape[0] for vector in vectors]
    joint = jnp.concatenate(vectors)
    if not grid.square:
        wide = [
            lax.all_gather(
                lax.all_gather(shard, "batch", axis=0, tiled=True), "seq", axis=1, tiled=True
            )
            for shard in matrices
        ]
        skip_full, qkv_full, proj_full, hidden_full, down_full = wide
        model = skip_full.shape[1]
        hidden_blocks = jnp.stack(jnp.split(hidden_full, hidden_full.shape[1] // model, axis=1))
        down_blocks = down_full.reshape(-1, model, model)
        joint = lax.all_gather(joint, "seq", axis=0)
        return (
            split_vectors(joint, widths),
            skip_full,
            qkv_full[:, :model],
            qkv_full[:, model:],
            proj_full,
            hidden_blocks,
            down_blocks,
        )
    model = proj_weight.shape[1] * 4
    short = -joint.shape[0] % (8 * LANES)
    extra = jnp.pad(joint, (0, short)).reshape(-1, LANES)
    skip_rows, skip_columns = skip_weight.shape
    skip_piece = pack_lanes(skip_weight)
    skip_column = column_gather(grid, skip_piece, extra)
    skip_blocks = seq_gather(grid, skip_column, "x")
    found = jnp.stack([block[-extra.shape[0] :].reshape(-1) for block in skip_blocks])
    joint = jnp.stack(
        [
            lax.dynamic_index_in_dim(found, grid.seq_index ^ place, 0, keepdims=False)
            for place in range(4)
        ]
    )
    (skip_full,) = assemble(
        grid,
        core_gather(grid, skip_blocks),
        skip_piece.shape,
        lambda *refs: rows_kernel(skip_rows, skip_columns, *refs),
        [model],
        skip_rows,
        "join_skip",
    )
    mixed_piece = jnp.concatenate([qkv_weight, proj_weight], axis=1)
    mixed_piece = tie(mixed_piece, skip_blocks[1], skip_blocks[2])
    mixed_column = column_gather(grid, mixed_piece)
    mixed_blocks = seq_gather(grid, mixed_column, "x")
    query_full, both_full, proj_full = assemble(
        grid,
        core_gather(grid, mixed_blocks),
        mixed_piece.shape,
        lambda *refs: mixed_kernel(qkv_weight.shape[1], *refs),
        [model, 2 * model, model],
        mixed_piece.shape[0],
        "join_mixed",
    )
    hidden_piece = tie(hidden_weight, mixed_column)
    hidden_column = column_gather(grid, hidden_piece)
    hidden_blocks = seq_gather(grid, hidden_column, "y")
    hidden_full = place_blocks(grid, core_gather(grid, hidden_blocks)).reshape(4, -1, model)
    down_rows, down_columns = down_weight.shape
    down_piece = tie(pack_lanes(down_weight), hidden_column)
    down_blocks = seq_gather(grid, column_gather(grid, down_piece), "x")
    (down_full,) = assemble(
        grid,
        core_gather(grid, down_blocks),
        down_piece.shape,
        lambda *refs: rows_kernel(down_rows, down_columns, *refs),
        [model],
        down_rows,
        "join_down",
    )
    return (
        split_vectors(joint, widths),
        skip_full,
        query_full,
        both_full,
        proj_full,
        hidden_full,
        down_full.reshape(-1, model, model),
    )


def add_low(mine, other):
    return (mine.astype(jnp.float32) + other.astype(jnp.float32)).astype(jnp.bfloat16)


class Scatter:
    def __init__(self, grid, keep, give):
        self.grid, self.mine, self.sent = grid, keep, give
        self.got = [grid.send(value, "c") for value in give]

    def push(self, axis, choose):
        here = self.grid.at[axis]
        self.mine = choose(self.values, here)
        self.sent = choose(self.values, 1 - here)
        self.got = [self.grid.send(value, axis) for value in self.sent]

    def pull(self, *after):
        mine, got = self.mine, self.got
        if after:
            mine = tie(mine, *after)
        self.values = [add_low(m, g) for m, g in zip(mine, got, strict=True)]

    def push_outer(self):
        grid = self.grid
        (value,) = self.values
        pick = lambda at: lax.dynamic_index_in_dim(value, at, 0, keepdims=False)
        self.mine = pick(grid.at["z"])
        self.sent = [
            pick((grid.at["z"] + turn) % grid.outer_count) for turn in range(1, grid.outer_count)
        ]
        self.got = [grid.send(value, "z", turn + 1) for turn, value in enumerate(self.sent)]

    def pull_outer(self, *after):
        mine = tie(self.mine, *after) if after else self.mine
        total = mine.astype(jnp.float32)
        for value in self.got:
            total = total + value.astype(jnp.float32)
        return total


def choose_dim(dim):
    return lambda values, at: [
        lax.dynamic_index_in_dim(value, at, dim, keepdims=False) for value in values
    ]


def choose_lanes(values, at):
    half = values[0].shape[-1] // 2
    return [lax.dynamic_slice_in_dim(value, at * half, half, value.ndim - 1) for value in values]


def choose_pair(values, at):
    half = len(values) // 2
    return [jnp.where(at == 0, values[k], values[half + k]) for k in range(half)]


def mixed_shards(grid, part):
    part = part.astype(jnp.bfloat16)
    rows, columns = part.shape
    whole = square_gather(grid, part).reshape(4, rows, 4, columns // 4)
    whole = whole.transpose(0, 2, 1, 3).reshape(16, rows, columns // 4)
    qkv = lax.dynamic_slice_in_dim(whole, 3 * grid.seq_index, 3, 0)
    qkv = qkv.transpose(1, 0, 2).reshape(rows, 3 * columns // 4)
    proj = lax.dynamic_index_in_dim(whole, 12 + grid.seq_index, 0, keepdims=False)
    return qkv.astype(jnp.float32), proj.astype(jnp.float32)


def seq_scatter(value):
    value = lax.psum_scatter(value, "seq", scatter_dimension=1, tiled=True)
    return lax.psum_scatter(value, "batch", scatter_dimension=0, tiled=True).astype(jnp.float32)


def scatter_vectors(grid, vectors):
    if not grid.square:
        totals = lax.psum(tuple(vectors), ("batch", "seq"))
    else:
        sizes = [vector.shape[0] for vector in vectors]
        joint = jnp.concatenate(vectors).reshape(-1, LANES)
        for axis in ("c", "x", "y"):
            joint = joint + grid.send(joint, axis)
        others = [grid.send(joint, "z", turn) for turn in range(1, grid.outer_count)]
        for other in others:
            joint = joint + other
        joint = joint.reshape(-1)
        totals, start = [], 0
        for size in sizes:
            totals.append(joint[start : start + size])
            start += size
    return [
        lax.dynamic_slice_in_dim(
            total, grid.seq_index * (total.shape[0] // grid.seq_count), total.shape[0] // grid.seq_count
        )
        for total in totals
    ]


class Items:
    def __init__(self, grid, segments, occupied, own_rows, all_rows):
        self.grid = grid
        self.segments, self.occupied = segments, occupied
        self.own_rows, self.all_rows = own_rows, all_rows
        self.halo_rows = all_rows - own_rows
        self.border = own_rows * (grid.seq_count // 2)
        tail = slice(self.border - self.halo_rows, self.border)
        self.moved = (segments[:, tail] == segments[:, self.border : self.border + 1]) & (
            occupied[:, tail] > 0
        )

    def of(self, seq_index):
        half = self.grid.seq_count // 2
        start = seq_index * self.own_rows
        rows = self.segments.shape[0]
        segment = lax.dynamic_slice(self.segments, (0, start), (rows, self.own_rows))
        used = lax.dynamic_slice(self.occupied, (0, start), (rows, self.own_rows)) > 0
        gone = jnp.pad(self.moved, ((0, 0), (self.own_rows - self.halo_rows, 0)))
        used = used & ~(gone & (seq_index == half - 1))
        halo_used = self.moved & (seq_index == half)
        halo_segment = self.segments[:, self.border - self.halo_rows : self.border]
        segment = jnp.concatenate([segment, halo_segment], axis=1)
        used = jnp.concatenate([used, halo_used], axis=1)
        alone = 1024 + seq_index * self.all_rows + jnp.arange(self.all_rows, dtype=jnp.int32)
        return jnp.where(used, segment, alone[None]), used


def far_gather(grid, value):
    rows, width, features = value.shape
    half = grid.seq_count // 2
    if half == 2:
        return [grid.send(value[row : row + 1], "x") for row in range(rows)]
    whole = lax.all_gather(value, "seq", axis=0)
    start = grid.seq_index // half * half
    whole = lax.dynamic_slice_in_dim(whole, start, half, 0)
    whole = whole.transpose(1, 0, 2, 3).reshape(rows, half * width, features)
    return [whole[row : row + 1] for row in range(rows)]


def far_ids(grid, items):
    half = grid.seq_count // 2
    if half == 2:
        return items.of(grid.seq_index ^ 1)[0]
    start = grid.seq_index // half * half
    ids = [
        jnp.where(start + part == grid.seq_index, -1, items.of(start + part)[0])
        for part in range(half)
    ]
    return jnp.concatenate(ids, axis=1)


def far_reduce(grid, value):
    half = grid.seq_count // 2
    value = value.astype(jnp.bfloat16)
    if half == 2:
        return grid.send(value, "x").astype(jnp.float32)
    split = value.reshape(half, -1, value.shape[2])
    whole = jnp.zeros((grid.seq_count,) + split.shape[1:], jnp.bfloat16)
    start = grid.seq_index // half * half
    whole = lax.dynamic_update_slice_in_dim(whole, split, start, 0)
    return lax.psum_scatter(whole, "seq", scatter_dimension=0).astype(jnp.float32)[None]


def body(
    inputs,
    skip_inputs,
    out_cotangent,
    segments,
    occupied,
    skip_weight,
    skip_bias,
    first_gain,
    first_shift,
    qkv_weight,
    proj_weight,
    proj_bias,
    second_gain,
    second_shift,
    hidden_weight,
    hidden_bias,
    down_weight,
    down_bias,
):
    grid = Grid()
    own_rows, model = inputs.shape[1], inputs.shape[2]
    all_rows = -(-(own_rows + 16) // 32) * 32
    halo_rows = all_rows - own_rows
    half = grid.seq_count // 2
    vectors, skip_full, query_full, both_full, proj_full, hidden_blocks, down_blocks = gather_all(
        grid,
        [skip_weight, qkv_weight, proj_weight, hidden_weight, down_weight],
        [
            skip_bias,
            first_gain,
            first_shift,
            proj_bias,
            second_gain,
            second_shift,
            hidden_bias,
            down_bias,
        ],
    )
    (
        skip_bias_full,
        gain_one,
        shift_one,
        proj_bias_full,
        gain_two,
        shift_two,
        hidden_bias_full,
        down_bias_full,
    ) = vectors
    items = Items(grid, segments, occupied, own_rows, all_rows)
    query_ids, used = items.of(grid.seq_index)
    key_ids = jnp.concatenate([query_ids, far_ids(grid, items)], axis=1)
    tails = jnp.stack([v[:, own_rows - halo_rows :] for v in (inputs, skip_inputs, out_cotangent)])
    halo = grid.shift(tails, half - 1, half)
    first_tokens = jnp.concatenate([inputs, halo[0]], axis=1)
    second_tokens = jnp.concatenate([skip_inputs, halo[1]], axis=1)
    joined = jnp.concatenate([first_tokens, second_tokens], axis=2)
    cotangent = jnp.concatenate([out_cotangent, halo[2]], axis=1)

    stream = dot_last(joined, skip_full) + skip_bias_full
    first_low, first_normal, first_scale = layer_norm(stream, gain_one, shift_one)
    rows = inputs.shape[0]
    first_far = far_gather(grid, first_low)
    query = dot_last(first_low, query_full).astype(jnp.bfloat16)
    own = dot_last(first_low, both_full).astype(jnp.bfloat16)
    attended = jnp.zeros(query.shape, jnp.bfloat16)
    level = jnp.zeros((rows, HEADS, all_rows), jnp.float32)
    far = []
    for row in range(rows):
        far.append(dot_last(first_far[row], both_full).astype(jnp.bfloat16))
        attended, level = attend(
            query, own, far[row], query_ids, key_ids, row, attended, level
        )
    used_rows = used.astype(jnp.float32).reshape(-1, 1)
    flat = (-1, model)
    (
        output,
        second_low,
        act_low,
        grad_pre,
        grad_middle,
        grad_proj,
        grad_attended,
        hidden_sums,
        middle_sums,
    ) = middle_block(
        stream.reshape(flat),
        attended.reshape(flat),
        cotangent.reshape(flat),
        used_rows,
        proj_full,
        hidden_blocks,
        down_blocks,
        proj_bias_full,
        gain_two,
        shift_two,
        hidden_bias_full,
        down_bias_full,
    )
    hidden_bias_grad = jnp.sum(hidden_sums, axis=0).reshape(-1)
    middle_sums = jnp.sum(middle_sums, axis=0)
    gain_two_grad, shift_two_grad = middle_sums[0], middle_sums[1]
    proj_bias_grad, down_bias_grad = middle_sums[2], middle_sums[3]
    grad_branch = jnp.where(used[..., None], cotangent, 0).reshape(flat)
    here, outer = grid.at["c"], grid.outer_count
    core_rows = lambda value, *lead: value.reshape((outer,) + lead + (-1, value.shape[-1]))
    if grid.square:
        keep, give = weight_grad(act_low, grad_branch, here, outer // 4, 4, 1, "down_weight_grad")
        down_way = Scatter(
            grid, [core_rows(keep, 2, 2)], [core_rows(give, 2, 2)]
        )
        second_low = tie(second_low, give)
        keep, give = weight_grad(second_low, grad_pre, here, outer, 1, 4, "hidden_weight_grad")
        hidden_way = Scatter(grid, [core_rows(keep)], [core_rows(give)])
        down_way.pull(give)
        down_way.push("x", choose_dim(2))
        hidden_way.pull(*down_way.sent)
        hidden_way.push("y", choose_lanes)
        grad_attended = tie(grad_attended, *hidden_way.sent)
    else:
        down_grad = outer_dot(act_low, grad_branch)
        hidden_grad = outer_dot(second_low, grad_pre)
    output = output.reshape(stream.shape)
    grad_middle = grad_middle.reshape(stream.shape)
    grad_attended = grad_attended.reshape(stream.shape)

    query_grad = jnp.zeros(query.shape, jnp.bfloat16)
    both_grad = jnp.zeros((rows, key_ids.shape[1], 2 * model), jnp.bfloat16)
    grad_far = []
    for row in range(rows):
        query_grad, both_grad = attend_back(
            query,
            own,
            far[row],
            attended,
            grad_attended,
            level,
            query_ids,
            key_ids,
            row,
            query_grad,
            both_grad,
        )
        share = dot_back(both_grad[row : row + 1, all_rows:], both_full).astype(jnp.bfloat16)
        grad_far.append(far_reduce(grid, share))
        if row == 0 and grid.square:
            down_way.pull(share)
            down_way.push("y", choose_dim(1))
            hidden_way.pull(*down_way.sent)
            hidden_way.push("x", choose_lanes)
            both_grad = tie(both_grad, share, *hidden_way.sent)
    if grid.square:
        down_way.pull(share)
        down_way.push_outer()
        hidden_way.pull(*down_way.sent)
        hidden_way.push_outer()
        both_grad = tie(both_grad, *hidden_way.sent)
    both_flat = both_grad.reshape(-1, 2 * model)
    first_all = [jnp.concatenate([first_low[row], first_far[row][0]]) for row in range(rows)]
    first_all = jnp.concatenate(first_all)
    query_flat = query_grad.reshape(flat)
    if grid.square:
        both_keep, both_give = weight_grad(
            first_all, both_flat, here, outer, 1, 2, "both_weight_grad"
        )
        query_keep, query_give = weight_grad(
            first_low.reshape(flat), query_flat, here, outer, 1, 1, "query_weight_grad"
        )
        proj_keep, proj_give = weight_grad(
            attended.reshape(flat), grad_proj, here, outer, 1, 1, "proj_weight_grad"
        )
        mixed_way = Scatter(
            grid,
            [core_rows(value) for value in (query_keep, both_keep, proj_keep)],
            [core_rows(value) for value in (query_give, both_give, proj_give)],
        )
        query_grad = tie(query_grad, query_give, both_give, proj_give)
    else:
        both_weight_grad = outer_dot(first_all, both_flat)
        query_weight_grad = outer_dot(first_low.reshape(flat), query_flat)
        proj_grad = outer_dot(attended.reshape(flat), grad_proj)
    grad_first = dot_back(both_grad[:, :all_rows], both_full) + dot_back(query_grad, query_full)
    if grid.square:
        mixed_way.pull(grad_first)
        query_part, both_part, proj_part = mixed_way.values
        mixed_way.values = [
            query_part, both_part[..., :model], both_part[..., model:], proj_part
        ]
        mixed_way.push("y", choose_pair)
        grad_first = tie(grad_first, *mixed_way.sent)
    grad_first = grad_first + jnp.concatenate(grad_far)
    grad_norm, gain_one_grad, shift_one_grad = layer_norm_back(
        grad_first, first_normal, first_scale, gain_one
    )
    grad_stream = (grad_middle + grad_norm).astype(jnp.bfloat16)
    skip_bias_grad = jnp.sum(grad_stream.astype(jnp.float32), axis=(0, 1))
    joined_flat, stream_flat = joined.reshape(-1, 2 * model), grad_stream.reshape(flat)
    if grid.square:
        keep, give = weight_grad(joined_flat, stream_flat, here, outer // 2, 2, 1, "skip_weight_grad")
        skip_way = Scatter(grid, [core_rows(keep, 2, 2)], [core_rows(give, 2, 2)])
        grad_stream = tie(grad_stream, give)
    else:
        skip_weight_grad = outer_dot(joined_flat, stream_flat)
    input_grad = dot_back(grad_stream, skip_full[:model])
    if grid.square:
        skip_way.pull(input_grad)
        skip_way.push("x", choose_dim(2))
        grad_stream = tie(grad_stream, *skip_way.sent)
    skip_grad = dot_back(grad_stream, skip_full[model:])
    if grid.square:
        skip_way.pull(skip_grad)
        skip_way.push("y", choose_dim(1))
        mixed_way.pull(*skip_way.sent)
        mixed_way.push("x", choose_pair)
        skip_way.pull(*mixed_way.sent)
        skip_way.push_outer()
        mixed_way.pull(*skip_way.sent)
        mixed_way.push_outer()
        down_shard = columns_of_seq(grid, down_way.pull_outer().astype(jnp.bfloat16))
        down_shard = down_shard.astype(jnp.float32)
        hidden_shard = hidden_way.pull_outer()
        skip_shard = columns_of_seq(grid, skip_way.pull_outer().astype(jnp.bfloat16))
        skip_shard = skip_shard.astype(jnp.float32)
        qkv_shard, proj_shard = mixed_shards(grid, mixed_way.pull_outer())
    else:
        down_shard = seq_scatter(down_grad)
        hidden_shard = seq_scatter(hidden_grad)
        skip_shard = seq_scatter(skip_weight_grad)
        proj_shard = seq_scatter(proj_grad)
        qkv_shard = seq_scatter(jnp.concatenate([query_weight_grad, both_weight_grad], axis=1))

    moved = items.moved[..., None] & (grid.seq_index == half - 1)

    def settle(value):
        own, far = value[:, :own_rows], grid.shift(value[:, own_rows:], half, half - 1)
        tail = jnp.where(moved, far, own[:, own_rows - halo_rows :])
        return lax.dynamic_update_slice_in_dim(own, tail, own_rows - halo_rows, 1)

    vectors = scatter_vectors(
        grid,
        [
            skip_bias_grad,
            gain_one_grad,
            shift_one_grad,
            proj_bias_grad,
            gain_two_grad,
            shift_two_grad,
            hidden_bias_grad,
            down_bias_grad,
        ],
    )
    return (
        settle(output),
        settle(input_grad),
        settle(skip_grad),
        skip_shard,
        vectors[0],
        vectors[1],
        vectors[2],
        qkv_shard,
        proj_shard,
        vectors[3],
        vectors[4],
        vectors[5],
        hidden_shard,
        vectors[6],
        down_shard,
        vectors[7],
    )


def solution(mesh):
    return jax.shard_map(
        body,
        mesh=mesh,
        in_specs=(
            P("batch", "seq", None),
            P("batch", "seq", None),
            P("batch", "seq", None),
            P("batch", None),
            P("batch", None),
            P("batch", "seq"),
            P("seq"),
            P("seq"),
            P("seq"),
            P("batch", "seq"),
            P("batch", "seq"),
            P("seq"),
            P("seq"),
            P("seq"),
            P("batch", "seq"),
            P("seq"),
            P("batch", "seq"),
            P("seq"),
        ),
        out_specs=(
            P("batch", "seq", None),
            P("batch", "seq", None),
            P("batch", "seq", None),
            P("batch", "seq"),
            P("seq"),
            P("seq"),
            P("seq"),
            P("batch", "seq"),
            P("batch", "seq"),
            P("seq"),
            P("seq"),
            P("seq"),
            P("batch", "seq"),
            P("seq"),
            P("batch", "seq"),
            P("seq"),
        ),
        check_vma=False,
    )
```

```python
import jax
import jax.numpy as jnp
from jax import lax
from jax.experimental import pallas as pl
from jax.experimental.pallas import tpu as pltpu
from jax.sharding import PartitionSpec as P

HEADS = 16
HEAD_DIM = 72
LANES = 128
epsilon = 1e-05
masked_score = -1e30
VMEM_BYTES = 60 * 1024 * 1024
def nt_dot(left_side, right_side):
    return lax.dot_general(
        left_side, right_side, (((1,), (1,)), ((), ())), preferred_element_type=jnp.float32
    )


def tn_dot(left_side, right_side):
    return lax.dot_general(
        left_side, right_side, (((0,), (0,)), ((), ())), preferred_element_type=jnp.float32
    )


def nn_dot(left_side, right_side):
    return lax.dot_general(
        left_side, right_side, (((1,), (0,)), ((), ())), preferred_element_type=jnp.float32
    )


def split_heads(wide, head_ref, start=0):
    rows = wide.shape[0]
    pad = jnp.zeros((rows, LANES - HEAD_DIM), wide.dtype)
    for head in range(HEADS):
        piece = wide[:, head * HEAD_DIM : (head + 1) * HEAD_DIM]
        head_ref[head, start : start + rows] = jnp.concatenate([piece, pad], axis=1)


def split_keys(own_ref, far_ref, kh, vh):
    features = own_ref.shape[2] // 2
    start = 0
    for ref in (own_ref, far_ref):
        split_heads(ref[0, :, :features], kh, start)
        split_heads(ref[0, :, features:], vh, start)
        start += ref.shape[1]


def join_heads(head_ref):
    return jnp.concatenate([head_ref[head][:, :HEAD_DIM] for head in range(HEADS)], axis=1)


def chunk_of(rows):
    for count in (4, 2, 1):
        if rows % (count * 16) == 0:
            return rows // count
    return rows


def attend_kernel(
    q_ref, own_ref, far_ref, qid_ref, kid_ref, *refs
):
    out_ref, lse_ref, qh, kh, vh, score, prob = refs[-7:]
    split_heads(q_ref[0], qh)
    split_keys(own_ref, far_ref, kh, vh)
    key_rows = kh.shape[1]
    step = chunk_of(key_rows)
    scale = HEAD_DIM ** (-0.5)
    query_ids = qid_ref[0]

    def one_head(head, carry):
        query = qh[head]
        top = jnp.full((1, query.shape[0]), masked_score, jnp.float32)
        for start in range(0, key_rows, step):
            part = nt_dot(kh[head, start : start + step], query) * scale
            part = jnp.where(kid_ref[0, start : start + step] == query_ids, part, masked_score)
            score[start : start + step] = part
            top = jnp.maximum(top, jnp.max(part, axis=0, keepdims=True))
        total = jnp.zeros_like(top)
        for start in range(0, key_rows, step):
            part = jnp.exp(score[start : start + step] - top)
            total = total + jnp.sum(part, axis=0, keepdims=True)
            prob[start : start + step] = part.astype(jnp.bfloat16)
        mixed = tn_dot(vh[head], prob[...]) / total
        qh[head] = mixed.T.astype(jnp.bfloat16)
        lse_ref[0, pl.ds(head, 1)] = top + jnp.log(total)
        return carry

    lax.fori_loop(0, HEADS, one_head, 0)
    out_ref[0] = join_heads(qh)


def attend(query, own, far, query_ids, key_ids, row, *old):
    rows, width, features = query.shape
    far_rows = far.shape[1]
    key_rows = width + far_rows
    here = lambda i: (row, 0, 0)
    only = lambda i: (0, 0, 0)
    wide = pl.BlockSpec((1, width, features), here)
    levels = pl.BlockSpec((1, HEADS, width), here)
    return pl.pallas_call(
        attend_kernel,
        grid=(1,),
        in_specs=[
            wide,
            pl.BlockSpec((1, width, 2 * features), here),
            pl.BlockSpec((1, far_rows, 2 * features), only),
            pl.BlockSpec((1, 1, width), here),
            pl.BlockSpec((1, key_rows, 1), here),
        ]
        + [pl.BlockSpec(memory_space=pl.ANY)] * len(old),
        out_specs=[wide, levels],
        out_shape=[
            jax.ShapeDtypeStruct((rows, width, features), jnp.bfloat16),
            jax.ShapeDtypeStruct((rows, HEADS, width), jnp.float32),
        ],
        scratch_shapes=[
            pltpu.VMEM((HEADS, width, LANES), jnp.bfloat16),
            pltpu.VMEM((HEADS, key_rows, LANES), jnp.bfloat16),
            pltpu.VMEM((HEADS, key_rows, LANES), jnp.bfloat16),
            pltpu.VMEM((key_rows, width), jnp.float32),
            pltpu.VMEM((key_rows, width), jnp.bfloat16),
        ],
        input_output_aliases={5: 0, 6: 1} if old else {},
        compiler_params=pltpu.CompilerParams(vmem_limit_bytes=VMEM_BYTES),
        cost_estimate=pl.CostEstimate(
            flops=4 * HEADS * width * key_rows * LANES,
            transcendentals=HEADS * width * key_rows,
            bytes_accessed=4 * features * (width + key_rows),
        ),
        name="attend",
    )(query, own, far, query_ids[:, None, :], key_ids[:, :, None], *old)


def attend_back_kernel(
    q_ref, own_ref, far_ref, o_ref, g_ref, lse_ref, qid_ref, kid_ref, *refs
):
    dq_ref, dkv_ref, qh, kh, vh, oh, gh, prob, slope = refs[-9:]
    split_heads(q_ref[0], qh)
    features = q_ref.shape[2]
    split_keys(own_ref, far_ref, kh, vh)
    split_heads(o_ref[0], oh)
    split_heads(g_ref[0], gh)
    key_rows = kh.shape[1]
    step = chunk_of(key_rows)
    scale = HEAD_DIM ** (-0.5)
    query_ids = qid_ref[0]

    def one_head(head, carry):
        query = qh[head]
        grad = gh[head]
        level = lse_ref[0, pl.ds(head, 1)]
        overlap = oh[head].astype(jnp.float32) * grad.astype(jnp.float32)
        row_dot = jnp.sum(overlap.T, axis=0, keepdims=True)
        for start in range(0, key_rows, step):
            part = nt_dot(kh[head, start : start + step], query) * scale
            part = jnp.where(kid_ref[0, start : start + step] == query_ids, part, masked_score)
            soft = jnp.exp(part - level)
            prob[start : start + step] = soft.astype(jnp.bfloat16)
            turn = nt_dot(vh[head, start : start + step], grad)
            slope[start : start + step] = (soft * (turn - row_dot)).astype(jnp.bfloat16)
        value_grad = nn_dot(prob[...], grad)
        query_grad = tn_dot(kh[head], slope[...]) * scale
        key_grad = nn_dot(slope[...], query) * scale
        vh[head] = value_grad.astype(jnp.bfloat16)
        kh[head] = key_grad.astype(jnp.bfloat16)
        qh[head] = query_grad.T.astype(jnp.bfloat16)
        return carry

    lax.fori_loop(0, HEADS, one_head, 0)
    dq_ref[0] = join_heads(qh)
    dkv_ref[0, :, :features] = join_heads(kh)
    dkv_ref[0, :, features:] = join_heads(vh)


def attend_back(
    query, own, far, mixed, grad, level, query_ids, key_ids, row, *old
):
    rows, width, features = query.shape
    far_rows = far.shape[1]
    key_rows = width + far_rows
    here = lambda i: (row, 0, 0)
    only = lambda i: (0, 0, 0)
    wide = pl.BlockSpec((1, width, features), here, pipeline_mode=pl.Buffered(1))
    return pl.pallas_call(
        attend_back_kernel,
        grid=(1,),
        in_specs=[
            wide,
            pl.BlockSpec((1, width, 2 * features), here, pipeline_mode=pl.Buffered(1)),
            pl.BlockSpec((1, far_rows, 2 * features), only, pipeline_mode=pl.Buffered(1)),
            wide,
            wide,
            pl.BlockSpec((1, HEADS, width), here),
            pl.BlockSpec((1, 1, width), here),
            pl.BlockSpec((1, key_rows, 1), here),
        ]
        + [pl.BlockSpec(memory_space=pl.ANY)] * len(old),
        out_specs=[
            pl.BlockSpec((1, width, features), here),
            pl.BlockSpec((1, key_rows, 2 * features), here),
        ],
        out_shape=[
            jax.ShapeDtypeStruct((rows, width, features), jnp.bfloat16),
            jax.ShapeDtypeStruct((rows, key_rows, 2 * features), jnp.bfloat16),
        ],
        scratch_shapes=[
            pltpu.VMEM((HEADS, width, LANES), jnp.bfloat16),
            pltpu.VMEM((HEADS, key_rows, LANES), jnp.bfloat16),
            pltpu.VMEM((HEADS, key_rows, LANES), jnp.bfloat16),
            pltpu.VMEM((HEADS, width, LANES), jnp.bfloat16),
            pltpu.VMEM((HEADS, width, LANES), jnp.bfloat16),
            pltpu.VMEM((key_rows, width), jnp.bfloat16),
            pltpu.VMEM((key_rows, width), jnp.bfloat16),
        ],
        input_output_aliases={8: 0, 9: 1} if old else {},
        compiler_params=pltpu.CompilerParams(vmem_limit_bytes=VMEM_BYTES),
        cost_estimate=pl.CostEstimate(
            flops=10 * HEADS * width * key_rows * LANES,
            transcendentals=HEADS * width * key_rows,
            bytes_accessed=8 * features * (width + key_rows),
        ),
        name="attend_back",
    )(
        query,
        own,
        far,
        mixed,
        grad,
        level,
        query_ids[:, None, :],
        key_ids[:, :, None],
        *old,
    )


def split_rows(total_ref, here, outer, keep_ref, give_ref):
    inner = total_ref.shape[0] // (2 * outer)
    for group in range(outer):
        start = group * 2 * inner
        span = slice(group * inner, (group + 1) * inner)
        keep_ref[span] = total_ref[pl.ds(pl.multiple_of(start + here * inner, 16), inner)]
        give_ref[span] = total_ref[pl.ds(pl.multiple_of(start + (1 - here) * inner, 16), inner)]


def wide_grad_kernel(outer, here_ref, left_ref, right_ref, keep_ref, give_ref, total):
    total[...] = tn_dot(left_ref[...], right_ref[...]).astype(jnp.bfloat16)
    split_rows(total, here_ref[0], outer, keep_ref, give_ref)


def wide_grad(left, right, here, outer, name):
    tokens, rows = left.shape
    blocks = right.shape[1] // rows
    half = jax.ShapeDtypeStruct((rows // 2, right.shape[1]), jnp.bfloat16)
    spec = pl.BlockSpec((rows // 2, rows), lambda j, here: (0, j))
    return pl.pallas_call(
        lambda *refs: wide_grad_kernel(outer, *refs),
        grid_spec=pltpu.PrefetchScalarGridSpec(
            num_scalar_prefetch=1,
            grid=(blocks,),
            in_specs=[
                pl.BlockSpec((tokens, rows), lambda j, here: (0, 0)),
                pl.BlockSpec((tokens, rows), lambda j, here: (0, j)),
            ],
            out_specs=[spec, spec],
            scratch_shapes=[pltpu.VMEM((rows, rows), jnp.bfloat16)],
        ),
        out_shape=[half, half],
        compiler_params=pltpu.CompilerParams(vmem_limit_bytes=VMEM_BYTES),
        cost_estimate=pl.CostEstimate(
            flops=2 * tokens * rows * right.shape[1],
            transcendentals=0,
            bytes_accessed=2 * (tokens + right.shape[1]) * rows,
        ),
        name=name,
    )(here, left, right)


def tall_grad_kernel(groups, here_ref, left_ref, right_ref, keep_ref, give_ref, total):
    total[...] = tn_dot(left_ref[...], right_ref[...]).astype(jnp.bfloat16)
    here = here_ref[0]
    inner = total.shape[0] // (2 * groups)
    columns = total.shape[1] // 4
    for group in range(groups):
        start = group * 2 * inner
        for core, out_ref in ((here, keep_ref), (1 - here, give_ref)):
            rows = total[pl.ds(pl.multiple_of(start + core * inner, 16), inner)]
            for place in range(4):
                out_ref[group, place] = pack_lanes(rows[:, place * columns : (place + 1) * columns])


def tall_grad(left, right, here, outer, name):
    tokens, model = right.shape
    blocks = left.shape[1] // model
    groups = outer // blocks
    packed = left.shape[1] // (2 * outer) * (model // 4) // LANES
    half = jax.ShapeDtypeStruct((outer, 4, packed, LANES), jnp.bfloat16)
    spec = pl.BlockSpec((groups, 4, packed, LANES), lambda i, here: (i, 0, 0, 0))
    return pl.pallas_call(
        lambda *refs: tall_grad_kernel(groups, *refs),
        grid_spec=pltpu.PrefetchScalarGridSpec(
            num_scalar_prefetch=1,
            grid=(blocks,),
            in_specs=[
                pl.BlockSpec((tokens, model), lambda i, here: (0, i)),
                pl.BlockSpec((tokens, model), lambda i, here: (0, 0)),
            ],
            out_specs=[spec, spec],
            scratch_shapes=[pltpu.VMEM((model, model), jnp.bfloat16)],
        ),
        out_shape=[half, half],
        compiler_params=pltpu.CompilerParams(vmem_limit_bytes=VMEM_BYTES),
        cost_estimate=pl.CostEstimate(
            flops=2 * tokens * model * left.shape[1],
            transcendentals=0,
            bytes_accessed=2 * (tokens + model) * left.shape[1],
        ),
        name=name,
    )(here, left, right)


def mixed_grad_kernel(
    outer, here_ref, first_ref, far_a, far_b, att_ref, query_ref, both_ref, proj_ref,
    keep_ref, give_ref, total, sums,
):
    step = pl.program_id(0)
    width = far_a.shape[0]
    span = far_a.shape[0] + first_ref.shape[0] // 2
    own = first_ref.shape[0] // 2

    @pl.when(step == 0)
    def _():
        total[0] = tn_dot(first_ref[...], query_ref[...]).astype(jnp.bfloat16)

    @pl.when((step == 1) | (step == 2))
    def _():
        sums[...] = tn_dot(first_ref[0:own], both_ref[0:own])
        sums[...] += tn_dot(far_a[...], both_ref[own:span])
        sums[...] += tn_dot(first_ref[own:], both_ref[span : span + own])
        total[step] = (sums[...] + tn_dot(far_b[...], both_ref[span + own :])).astype(jnp.bfloat16)

    @pl.when(step == 3)
    def _():
        total[3] = tn_dot(att_ref[...], proj_ref[...]).astype(jnp.bfloat16)
        here = here_ref[0]
        model = total.shape[2]
        inner = model // (2 * outer)
        cut = model * 3 // 4
        for group in range(outer):
            rows = slice(group * inner, (group + 1) * inner)
            for core, out_ref in ((here, keep_ref), (1 - here, give_ref)):
                start = pl.multiple_of((group * 2 + core) * inner, 16)
                wide = jnp.concatenate([total[k, pl.ds(start, inner)] for k in range(3)], axis=1)
                last = total[3, pl.ds(start, inner)]
                for place in range(4):
                    out_ref[rows, place * model : (place + 1) * model] = jnp.concatenate(
                        [
                            wide[:, place * cut : (place + 1) * cut],
                            last[:, place * (model - cut) : (place + 1) * (model - cut)],
                        ],
                        axis=1,
                    )


def mixed_grad(first, far, attended, query_grad, both_grad, proj_grad, here, outer):
    tokens, model = first.shape
    half = jax.ShapeDtypeStruct((model // 2, 4 * model), jnp.bfloat16)
    fixed = lambda *shape: pl.BlockSpec(
        shape, lambda j, here: (0, 0), pipeline_mode=pl.Buffered(1)
    )
    return pl.pallas_call(
        lambda *refs: mixed_grad_kernel(outer, *refs),
        grid_spec=pltpu.PrefetchScalarGridSpec(
            num_scalar_prefetch=1,
            grid=(4,),
            in_specs=[
                fixed(tokens, model),
                fixed(*far[0].shape),
                fixed(*far[1].shape),
                fixed(tokens, model),
                fixed(tokens, model),
                pl.BlockSpec(
                    (both_grad.shape[0], model),
                    lambda j, here: (0, jnp.minimum(jnp.maximum(j - 1, 0), 1)),
                ),
                fixed(tokens, model),
            ],
            out_specs=[fixed(model // 2, 4 * model), fixed(model // 2, 4 * model)],
            scratch_shapes=[
                pltpu.VMEM((4, model, model), jnp.bfloat16),
                pltpu.VMEM((model, model), jnp.float32),
            ],
        ),
        out_shape=[half, half],
        compiler_params=pltpu.CompilerParams(vmem_limit_bytes=VMEM_BYTES),
        cost_estimate=pl.CostEstimate(
            flops=2 * model * model * (2 * tokens + 2 * both_grad.shape[0]),
            transcendentals=0,
            bytes_accessed=2 * model * (6 * tokens + 2 * both_grad.shape[0] + 4 * model),
        ),
        name="mixed_weight_grad",
    )(here, first, far[0], far[1], attended, query_grad, both_grad, proj_grad)


def column_chunks(width):
    cut = width // 256 // 2 * 256
    return ((0, cut), (cut, width)) if cut else ((0, width),)


def middle_kernel(
    stream_ref, att_ref, cot_ref, used_ref, proj_ref, hidden_ref, down_ref,
    proj_bias_ref, gain_ref, shift_ref, hidden_bias_ref, down_bias_ref,
    out_ref, second_ref, act_ref, pre_ref, middle_grad_ref, proj_grad_ref, att_grad_ref,
    hidden_sum_ref, sums_ref,
    low, normal, scale, branch, total, back,
):
    step = pl.program_id(1)
    steps = pl.num_programs(1)

    @pl.when(step == 0)
    def _():
        middle = stream_ref[...] + nn_dot(att_ref[...], proj_ref[...]) + proj_bias_ref[...]
        centred = middle - jnp.mean(middle, axis=-1, keepdims=True)
        inverse = lax.rsqrt(jnp.mean(centred * centred, axis=-1, keepdims=True) + epsilon)
        unit = centred * inverse
        normal[...] = unit
        scale[...] = inverse
        second = (unit * gain_ref[...] + shift_ref[...]).astype(jnp.bfloat16)
        low[...] = second
        second_ref[...] = second
        branch[...] = (cot_ref[...].astype(jnp.float32) * used_ref[...]).astype(jnp.bfloat16)
        total[...] = middle + down_bias_ref[...]
        back[...] = jnp.zeros_like(back)

    for start, stop in column_chunks(hidden_ref.shape[2]):
        pre_act = nn_dot(low[...], hidden_ref[0, :, start:stop]) + hidden_bias_ref[0, :, start:stop]
        grad_act = nt_dot(branch[...], down_ref[0, start:stop])
        below = 0.5 + 0.5 * lax.erf(pre_act * (0.5**0.5))
        density = jnp.exp(-0.5 * pre_act * pre_act) * ((2.0 * jnp.pi) ** -0.5)
        act = (pre_act * below).astype(jnp.bfloat16)
        grad_pre = (grad_act * (below + pre_act * density)).astype(jnp.bfloat16)
        act_ref[:, start:stop] = act
        pre_ref[:, start:stop] = grad_pre
        hidden_sum_ref[0, 0, :, start:stop] = jnp.sum(
            grad_pre.astype(jnp.float32), axis=0, keepdims=True
        )
        total[...] += nn_dot(act, down_ref[0, start:stop])
        back[...] += nt_dot(grad_pre, hidden_ref[0, :, start:stop])

    @pl.when(step == steps - 1)
    def _():
        out_ref[...] = total[...].astype(jnp.bfloat16)
        grad = back[...]
        unit = normal[...]
        part = grad * gain_ref[...]
        mean_part = jnp.mean(part, axis=-1, keepdims=True)
        mean_both = jnp.mean(part * unit, axis=-1, keepdims=True)
        grad_out = cot_ref[...].astype(jnp.float32) * used_ref[...]
        grad_middle = grad_out + (part - mean_part - unit * mean_both) * scale[...]
        middle_grad_ref[...] = grad_middle
        grad_low = grad_middle.astype(jnp.bfloat16)
        proj_grad_ref[...] = grad_low
        att_grad_ref[...] = nt_dot(grad_low, proj_ref[...]).astype(jnp.bfloat16)
        sums_ref[0, 0:1] = jnp.sum(grad * unit, axis=0, keepdims=True)
        sums_ref[0, 1:2] = jnp.sum(grad, axis=0, keepdims=True)
        sums_ref[0, 2:3] = jnp.sum(grad_low.astype(jnp.float32), axis=0, keepdims=True)
        sums_ref[0, 3:4] = jnp.sum(grad_out, axis=0, keepdims=True)


def token_block(tokens):
    return tokens // 4 if tokens % 64 == 0 else tokens


def middle_block(
    stream, attended, cotangent, used, proj, hidden, down, proj_bias, gain, shift, hidden_bias,
    down_bias,
):
    tokens, model = stream.shape
    steps = hidden.shape[0]
    rows = token_block(tokens)
    blocks = tokens // rows
    by_rows = pl.BlockSpec((rows, model), lambda i, s: (i, 0))
    by_step = pl.BlockSpec((rows, model), lambda i, s: (i, s))
    vector = pl.BlockSpec((1, model), lambda i, s: (0, 0))
    low_rows = jax.ShapeDtypeStruct((tokens, model), jnp.bfloat16)
    low_steps = jax.ShapeDtypeStruct((tokens, steps * model), jnp.bfloat16)
    flops = 2 * tokens * model * model * (4 * steps + 2)
    return pl.pallas_call(
        middle_kernel,
        grid=(blocks, steps),
        in_specs=[
            by_rows,
            by_rows,
            by_rows,
            pl.BlockSpec((rows, 1), lambda i, s: (i, 0)),
            pl.BlockSpec((model, model), lambda i, s: (0, 0), pipeline_mode=pl.Buffered(1)),
            pl.BlockSpec((1, model, model), lambda i, s: (s, 0, 0)),
            pl.BlockSpec((1, model, model), lambda i, s: (s, 0, 0)),
            vector,
            vector,
            vector,
            pl.BlockSpec((1, 1, model), lambda i, s: (s, 0, 0)),
            vector,
        ],
        out_specs=[
            by_rows,
            by_rows,
            by_step,
            by_step,
            by_rows,
            by_rows,
            by_rows,
            pl.BlockSpec((1, 1, 1, model), lambda i, s: (i, s, 0, 0)),
            pl.BlockSpec((1, 4, model), lambda i, s: (i, 0, 0)),
        ],
        out_shape=[
            low_rows,
            low_rows,
            low_steps,
            low_steps,
            jax.ShapeDtypeStruct((tokens, model), jnp.float32),
            low_rows,
            low_rows,
            jax.ShapeDtypeStruct((blocks, steps, 1, model), jnp.float32),
            jax.ShapeDtypeStruct((blocks, 4, model), jnp.float32),
        ],
        scratch_shapes=[
            pltpu.VMEM((rows, model), jnp.bfloat16),
            pltpu.VMEM((rows, model), jnp.float32),
            pltpu.VMEM((rows, 1), jnp.float32),
            pltpu.VMEM((rows, model), jnp.bfloat16),
            pltpu.VMEM((rows, model), jnp.float32),
            pltpu.VMEM((rows, model), jnp.float32),
        ],
        compiler_params=pltpu.CompilerParams(vmem_limit_bytes=VMEM_BYTES),
        cost_estimate=pl.CostEstimate(
            flops=flops,
            transcendentals=2 * tokens * model * steps,
            bytes_accessed=2 * tokens * model * (2 * steps + 12) + 4 * model * model * steps * blocks,
        ),
        name="middle_block",
    )(
        stream,
        attended,
        cotangent,
        used,
        proj,
        hidden,
        down,
        proj_bias[None],
        gain[None],
        shift[None],
        hidden_bias.reshape(steps, 1, model),
        down_bias[None],
    )


def layer_norm(stream, norm_gain, norm_shift):
    centred = stream - jnp.mean(stream, axis=-1, keepdims=True)
    scale = lax.rsqrt(jnp.mean(centred * centred, axis=-1, keepdims=True) + epsilon)
    normal = centred * scale
    return (normal * norm_gain + norm_shift).astype(jnp.bfloat16), normal, scale


def layer_norm_back(grad, normal, scale, norm_gain):
    part = grad * norm_gain
    mean_part = jnp.mean(part, axis=-1, keepdims=True)
    mean_both = jnp.mean(part * normal, axis=-1, keepdims=True)
    gain_grad = jnp.sum(grad * normal, axis=(0, 1))
    shift_grad = jnp.sum(grad, axis=(0, 1))
    return (part - mean_part - normal * mean_both) * scale, gain_grad, shift_grad


def outer_dot(left_side, right_side):
    return lax.dot_general(
        left_side, right_side, (((0,), (0,)), ((), ())), preferred_element_type=jnp.bfloat16
    )


def dot_last(left_side, right_side):
    return lax.dot_general(
        left_side, right_side, (((2,), (0,)), ((), ())), preferred_element_type=jnp.float32
    )


def dot_back(left_side, right_side):
    return lax.dot_general(
        left_side, right_side, (((2,), (1,)), ((), ())), preferred_element_type=jnp.float32
    )


def dot_tokens(left_side, right_side):
    return lax.dot_general(
        left_side, right_side, (((0, 1), (0, 1)), ((), ())), preferred_element_type=jnp.bfloat16
    )


class Grid:
    def __init__(self):
        self.batch_count = lax.axis_size("batch")
        self.seq_count = lax.axis_size("seq")
        self.seq_index = lax.axis_index("seq")
        batch_index = lax.axis_index("batch")
        self.outer_count = self.batch_count // 2
        self.square = self.seq_count == 4 and self.outer_count == 4
        self.at = {
            "z": batch_index // 2,
            "c": batch_index % 2,
            "y": self.seq_index // 2,
            "x": self.seq_index % 2,
        }

    def index(self, z, c, s):
        return (z * 2 + c) * self.seq_count + s

    def send(self, value, axis, turn=0):
        pairs = []
        for z in range(self.outer_count):
            for c in range(2):
                for s in range(self.seq_count):
                    far_z, far_c, far_s = z, c, s
                    if axis == "z":
                        far_z = z ^ turn
                    elif axis == "c":
                        far_c = 1 - c
                    elif axis == "y":
                        far_s = s ^ 2
                    else:
                        far_s = s ^ 1
                    pairs.append((self.index(z, c, s), self.index(far_z, far_c, far_s)))
        return lax.ppermute(value, ("batch", "seq"), pairs)

    def shift(self, value, source, target):
        pairs = [
            (b * self.seq_count + source, b * self.seq_count + target)
            for b in range(self.batch_count)
        ]
        return lax.ppermute(value, ("batch", "seq"), pairs)


def tie(value, *others):
    return lax.optimization_barrier((value, *others))[0]


def square_gather(grid, shard):
    over_x = grid.send(shard, "x")
    found = jnp.stack([shard, over_x, grid.send(shard, "y"), grid.send(over_x, "y")])
    return jnp.stack(
        [
            lax.dynamic_index_in_dim(found, grid.seq_index ^ place, 0, keepdims=False)
            for place in range(4)
        ]
    )


def pack_lanes(shard):
    rows, columns = shard.shape
    whole = columns // LANES
    rest = columns - whole * LANES
    pieces = [shard[:, k * LANES : (k + 1) * LANES] for k in range(whole)]
    if rest:
        fold = LANES // rest
        step = rows // fold
        last = [shard[k * step : (k + 1) * step, whole * LANES :] for k in range(fold)]
        pieces.append(jnp.concatenate(last, axis=1))
    return jnp.concatenate(pieces, axis=0)


def unpack_lanes(packed, rows, columns):
    whole = columns // LANES
    rest = columns - whole * LANES
    pieces = [packed[k * rows : (k + 1) * rows] for k in range(whole)]
    if rest:
        fold = LANES // rest
        last = packed[whole * rows : whole * rows + rows // fold]
        pieces.append(
            jnp.concatenate([last[:, k * rest : (k + 1) * rest] for k in range(fold)], axis=0)
        )
    return jnp.concatenate(pieces, axis=1)


def rows_kernel(rows, columns, turn_ref, to_ref, *refs):
    blocks, out_ref, found = refs[:8], refs[8], refs[9]
    for block in range(8):
        found[to_ref[block]] = blocks[block][...]
    for core in range(2):
        wide = [unpack_lanes(found[core * 4 + place], rows, columns) for place in range(4)]
        out_ref[core * rows : (core + 1) * rows] = jnp.concatenate(wide, axis=1)


def mixed_kernel(columns, turn_ref, to_ref, *refs):
    blocks, query_ref, both_ref, proj_ref, found = refs[:8], refs[8], refs[9], refs[10], refs[11]
    rows, model = found.shape[1:]
    for block in range(8):
        found[to_ref[block]] = blocks[block][...]
    for core in range(2):
        span = slice(core * rows, (core + 1) * rows)
        parts = [found[core * 4 + place] for place in range(4)]
        wide = jnp.concatenate([part[:, :columns] for part in parts], axis=1)
        query_ref[span] = wide[:, :model]
        both_ref[span] = wide[:, model:]
        proj_ref[span] = jnp.concatenate([part[:, columns:] for part in parts], axis=1)


def assemble(grid, blocks, order, piece, kernel, widths, rows, name):
    outer = grid.outer_count
    spots = jnp.array([order.index(turn) for turn in range(outer)], jnp.int32)
    turns = jnp.stack(
        [lax.dynamic_index_in_dim(spots, grid.at["z"] ^ z, keepdims=False) for z in range(outer)]
    )
    places = [
        (grid.at["c"] ^ (block >> 2)) * 4 + (grid.seq_index ^ (block & 3)) for block in range(8)
    ]
    shapes = [jax.ShapeDtypeStruct((outer * 2 * rows, w), jnp.bfloat16) for w in widths]
    return pl.pallas_call(
        kernel,
        grid_spec=pltpu.PrefetchScalarGridSpec(
            num_scalar_prefetch=2,
            grid=(outer,),
            in_specs=[pl.BlockSpec(piece, lambda z, turn, to: (turn[z], 0))] * 8,
            out_specs=[pl.BlockSpec((2 * rows, w), lambda z, turn, to: (z, 0)) for w in widths],
            scratch_shapes=[pltpu.VMEM((8,) + piece, jnp.bfloat16)],
        ),
        out_shape=shapes,
        compiler_params=pltpu.CompilerParams(vmem_limit_bytes=VMEM_BYTES),
        cost_estimate=pl.CostEstimate(
            flops=0,
            transcendentals=0,
            bytes_accessed=8 * outer * rows * sum(widths),
        ),
        name=name,
    )(turns.astype(jnp.int32), jnp.stack(places).astype(jnp.int32), *blocks)


def place_kernel(block_count, outer_count, to_ref, *refs):
    blocks, out_ref, sems = refs[:block_count], refs[block_count], refs[block_count + 1]
    rows = out_ref.shape[1]
    copies = []
    for block in range(block_count):
        for turn in range(outer_count):
            slot = block * outer_count + turn
            copies.append(
                pltpu.make_async_copy(
                    blocks[block].at[pl.ds(turn * rows, rows)], out_ref.at[to_ref[slot]], sems.at[slot]
                )
            )
    for copy in copies:
        copy.start()
    for copy in copies:
        copy.wait()


def place_blocks(grid, blocks, order):
    outer = grid.outer_count
    rows, columns = blocks[0].shape[0] // outer, blocks[0].shape[1]
    slots = []
    for block in range(8):
        core, place = grid.at["c"] ^ (block >> 2), grid.seq_index ^ (block & 3)
        for turn in order:
            slots.append((place * outer + (grid.at["z"] ^ turn)) * 2 + core)
    count = 8 * outer
    return pl.pallas_call(
        lambda *refs: place_kernel(8, outer, *refs),
        grid_spec=pltpu.PrefetchScalarGridSpec(
            num_scalar_prefetch=1,
            grid=(1,),
            in_specs=[pl.BlockSpec(memory_space=pl.ANY)] * 8,
            out_specs=pl.BlockSpec((count, rows, columns), lambda i, to: (0, 0, 0)),
            scratch_shapes=[pltpu.SemaphoreType.DMA((count,))],
        ),
        compiler_params=pltpu.CompilerParams(vmem_limit_bytes=VMEM_BYTES),
        out_shape=jax.ShapeDtypeStruct((count, rows, columns), blocks[0].dtype),
        cost_estimate=pl.CostEstimate(
            flops=0, transcendentals=0, bytes_accessed=4 * count * rows * columns
        ),
        name="place_blocks",
    )(jnp.stack(slots).astype(jnp.int32), *blocks)


class Gather:
    def __init__(self, grid, piece, *extra, direct=False):
        self.grid = grid
        if direct:
            self.order = [0, 1, 2, 3]
            parts = [piece] + [grid.send(piece, "z", turn) for turn in (1, 2, 3)]
        else:
            self.order = [0, 2, 1, 3]
            self.pair = jnp.concatenate([piece, grid.send(piece, "z", 2)], axis=0)
            parts = [self.pair, grid.send(self.pair, "z", 1)]
        self.column = jnp.concatenate(parts + list(extra), axis=0)

    def spread(self):
        self.over_x = self.grid.send(self.column, "x")
        self.over_y = self.grid.send(self.column, "y")

    def forward(self, axis, *after):
        value = self.over_x if axis == "y" else self.over_y
        if after:
            value = tie(value, *after)
            if axis == "y":
                self.over_x = value
            else:
                self.over_y = value
        self.blocks = [self.column, self.over_x, self.over_y, self.grid.send(value, axis)]

    def core(self, *after):
        blocks = list(self.blocks)
        if after:
            blocks[3] = tie(blocks[3], *after)
        return blocks + [self.grid.send(block, "c") for block in blocks]


def split_vectors(joint, widths):
    result, start = [], 0
    for width in widths:
        result.append(joint[:, start : start + width].reshape(-1).astype(jnp.float32))
        start += width
    return result


def gather_plain(matrices, vectors):
    joint = lax.all_gather(jnp.concatenate(vectors), "seq", axis=0)
    wide = [
        lax.all_gather(
            lax.all_gather(shard, "batch", axis=0, tiled=True), "seq", axis=1, tiled=True
        )
        for shard in matrices
    ]
    return split_vectors(joint, [vector.shape[0] for vector in vectors]), wide


def hidden_columns(hidden_full, model):
    return jnp.stack(jnp.split(hidden_full, hidden_full.shape[1] // model, axis=1))


def gather_skip(grid, skip_weight, vectors):
    joint = jnp.concatenate(vectors)
    short = -joint.shape[0] % (8 * LANES)
    extra = jnp.pad(joint, (0, short)).reshape(-1, LANES)
    rows, columns = skip_weight.shape
    piece = pack_lanes(skip_weight)
    way = Gather(grid, piece, extra, direct=True)
    way.spread()
    way.forward("y")
    found = jnp.stack([block[-extra.shape[0] :].reshape(-1) for block in way.blocks])
    joint = jnp.stack(
        [
            lax.dynamic_index_in_dim(found, grid.seq_index ^ place, 0, keepdims=False)
            for place in range(4)
        ]
    )
    (skip_full,) = assemble(
        grid,
        way.core(),
        way.order,
        piece.shape,
        lambda *refs: rows_kernel(rows, columns, *refs),
        [4 * columns],
        rows,
        "join_skip",
    )
    return way, split_vectors(joint, [vector.shape[0] for vector in vectors]), skip_full


def join_mixed(grid, blocks, order, rows, columns, model):
    return assemble(
        grid,
        blocks,
        order,
        (rows, model),
        lambda *refs: mixed_kernel(columns, *refs),
        [model, 2 * model, model],
        rows,
        "join_mixed",
    )


def join_down(grid, blocks, order, rows, columns):
    packed = rows * columns // LANES
    (full,) = assemble(
        grid,
        blocks,
        order,
        (packed, LANES),
        lambda *refs: rows_kernel(rows, columns, *refs),
        [4 * columns],
        rows,
        "join_down",
    )
    return full.reshape(-1, 4 * columns, 4 * columns)


def add_low(mine, other):
    return (mine.astype(jnp.float32) + other.astype(jnp.float32)).astype(jnp.bfloat16)


class Scatter:
    def __init__(self, grid, keep, give, view):
        self.grid, self.mine, self.sent, self.view = grid, keep, give, view
        self.got = grid.send(give, "c")

    def push(self, axis, choose, turn=0):
        here = self.grid.at[axis]
        if turn:
            here = here // turn % 2
        self.mine, self.sent = choose(self.value, here), choose(self.value, 1 - here)
        self.got = self.grid.send(self.sent, axis, turn)

    def pull(self, *after):
        mine = tie(self.mine, *after) if after else self.mine
        self.value = add_low(mine, self.got)
        if self.view is not None:
            self.value, self.view = self.value.reshape(self.view), None
        return self.value


def fork(way):
    rows = way.value.shape[1] // 2
    ways = []
    for part in range(2):
        branch = object.__new__(Scatter)
        branch.grid, branch.view = way.grid, None
        branch.value = way.value[:, part * rows : (part + 1) * rows]
        ways.append(branch)
    return ways


def choose_dim(dim):
    return lambda value, at: lax.dynamic_index_in_dim(value, at, dim, keepdims=False)


def choose_half(value, at):
    half = value.shape[0] // 2
    return lax.dynamic_slice_in_dim(value, at * half, half, 0)


def choose_odd(value, at):
    pairs = value.reshape((2, 2) + value.shape[1:])
    return lax.dynamic_index_in_dim(pairs, at, 1, keepdims=False)


def choose_lanes(value, at):
    half = value.shape[-1] // 2
    return lax.dynamic_slice_in_dim(value, at * half, half, value.ndim - 1)


def choose_odd_lanes(value, at):
    part = value.shape[-1] // 4
    pieces = [
        lax.dynamic_slice_in_dim(value, (2 * k + at) * part, part, value.ndim - 1) for k in range(2)
    ]
    return jnp.concatenate(pieces, axis=-1)


def seq_scatter(value):
    value = lax.psum_scatter(value, "seq", scatter_dimension=1, tiled=True)
    return lax.psum_scatter(value, "batch", scatter_dimension=0, tiled=True).astype(jnp.float32)


def scatter_vectors(grid, vectors):
    joint = jnp.concatenate(vectors)
    if grid.square:
        joint = lax.all_gather(joint.reshape(-1, LANES), ("batch", "seq"))
    else:
        joint = lax.psum(joint, ("batch", "seq"))[None]
    return lambda *after: own_columns(grid, tie(joint, *after), vectors)


def own_columns(grid, joint, vectors):
    joint = jnp.sum(joint, axis=0).reshape(-1)
    result, start = [], 0
    for vector in vectors:
        width = vector.shape[0] // grid.seq_count
        result.append(lax.dynamic_slice_in_dim(joint, start + grid.seq_index * width, width))
        start += vector.shape[0]
    return result


class Items:
    def __init__(self, grid, segments, occupied, own_rows, all_rows):
        self.grid = grid
        self.segments, self.occupied = segments, occupied
        self.own_rows, self.all_rows = own_rows, all_rows
        self.halo_rows = all_rows - own_rows
        self.border = own_rows * (grid.seq_count // 2)
        tail = slice(self.border - self.halo_rows, self.border)
        self.moved = (segments[:, tail] == segments[:, self.border : self.border + 1]) & (
            occupied[:, tail] > 0
        )

    def of(self, seq_index):
        half = self.grid.seq_count // 2
        start = seq_index * self.own_rows
        rows = self.segments.shape[0]
        segment = lax.dynamic_slice(self.segments, (0, start), (rows, self.own_rows))
        used = lax.dynamic_slice(self.occupied, (0, start), (rows, self.own_rows)) > 0
        gone = jnp.pad(self.moved, ((0, 0), (self.own_rows - self.halo_rows, 0)))
        used = used & ~(gone & (seq_index == half - 1))
        halo_used = self.moved & (seq_index == half)
        halo_segment = self.segments[:, self.border - self.halo_rows : self.border]
        segment = jnp.concatenate([segment, halo_segment], axis=1)
        used = jnp.concatenate([used, halo_used], axis=1)
        alone = 1024 + seq_index * self.all_rows + jnp.arange(self.all_rows, dtype=jnp.int32)
        return jnp.where(used, segment, alone[None]), used


def far_gather(grid, value):
    rows, width, features = value.shape
    half = grid.seq_count // 2
    if half == 2:
        return [grid.send(value[row : row + 1], "x") for row in range(rows)]
    whole = lax.all_gather(value, "seq", axis=0)
    start = grid.seq_index // half * half
    whole = lax.dynamic_slice_in_dim(whole, start, half, 0)
    whole = whole.transpose(1, 0, 2, 3).reshape(rows, half * width, features)
    return [whole[row : row + 1] for row in range(rows)]


def far_ids(grid, items):
    half = grid.seq_count // 2
    if half == 2:
        return items.of(grid.seq_index ^ 1)[0]
    start = grid.seq_index // half * half
    ids = [
        jnp.where(start + part == grid.seq_index, -1, items.of(start + part)[0])
        for part in range(half)
    ]
    return jnp.concatenate(ids, axis=1)


def far_send(grid, value):
    half = grid.seq_count // 2
    if half == 2:
        return grid.send(value, "x")
    split = value.reshape(half, -1, value.shape[2])
    whole = jnp.zeros((grid.seq_count,) + split.shape[1:], jnp.bfloat16)
    start = grid.seq_index // half * half
    whole = lax.dynamic_update_slice_in_dim(whole, split, start, 0)
    return lax.psum_scatter(whole, "seq", scatter_dimension=0)[None]


def body(
    inputs,
    skip_inputs,
    out_cotangent,
    segments,
    occupied,
    skip_weight,
    skip_bias,
    first_gain,
    first_shift,
    qkv_weight,
    proj_weight,
    proj_bias,
    second_gain,
    second_shift,
    hidden_weight,
    hidden_bias,
    down_weight,
    down_bias,
):
    grid = Grid()
    own_rows, model = inputs.shape[1], inputs.shape[2]
    all_rows = -(-(own_rows + 16) // 32) * 32
    halo_rows = all_rows - own_rows
    half = grid.seq_count // 2
    vectors = [
        skip_bias,
        first_gain,
        first_shift,
        proj_bias,
        second_gain,
        second_shift,
        hidden_bias,
        down_bias,
    ]
    if grid.square:
        skip_way, vectors, skip_full = gather_skip(grid, skip_weight, vectors)
        mixed_piece = jnp.concatenate([qkv_weight, proj_weight], axis=1)
        mixed_way = Gather(grid, tie(mixed_piece, skip_way.column))
        mixed_way.spread()
        mixed_way.forward("y")
    else:
        vectors, wide = gather_plain(
            [skip_weight, qkv_weight, proj_weight, hidden_weight, down_weight], vectors
        )
        skip_full, qkv_full, proj_full, hidden_full, down_full = wide
        query_full, both_full = qkv_full[:, :model], qkv_full[:, model:]
        hidden_blocks = hidden_columns(hidden_full, model)
        down_blocks = down_full.reshape(-1, model, model)
    (
        skip_bias_full,
        gain_one,
        shift_one,
        proj_bias_full,
        gain_two,
        shift_two,
        hidden_bias_full,
        down_bias_full,
    ) = vectors
    joined_inputs = inputs
    if grid.square:
        joined_inputs = tie(inputs, skip_way.over_x, skip_way.over_y)
    items = Items(grid, segments, occupied, own_rows, all_rows)
    query_ids, used = items.of(grid.seq_index)
    key_ids = jnp.concatenate([query_ids, far_ids(grid, items)], axis=1)
    tails = jnp.stack([v[:, own_rows - halo_rows :] for v in (inputs, skip_inputs, out_cotangent)])
    halo = grid.shift(tails, half - 1, half)
    first_tokens = jnp.concatenate([joined_inputs, halo[0]], axis=1)
    second_tokens = jnp.concatenate([skip_inputs, halo[1]], axis=1)
    joined = tie(jnp.concatenate([first_tokens, second_tokens], axis=2))
    cotangent = jnp.concatenate([out_cotangent, halo[2]], axis=1)

    stream = dot_last(joined, skip_full) + skip_bias_full
    first_low, first_normal, first_scale = layer_norm(stream, gain_one, shift_one)
    rows = inputs.shape[0]
    first_far = far_gather(grid, first_low)
    if grid.square:
        hidden_way = Gather(grid, tie(hidden_weight, mixed_way.column, stream))
        down_way = Gather(grid, tie(pack_lanes(down_weight), hidden_way.pair))
        hidden_way.column = tie(hidden_way.column, mixed_way.blocks[3])
        hidden_way.spread()
        mixed_blocks = mixed_way.core(first_far[0], hidden_way.column, down_way.column)
        query_full, both_full, proj_full = join_mixed(
            grid, mixed_blocks, mixed_way.order, *qkv_weight.shape, model
        )
        query_full = tie(query_full, first_far[1])
        both_full = tie(both_full, first_far[1])
    query = dot_last(first_low, query_full).astype(jnp.bfloat16)
    own = dot_last(first_low, both_full).astype(jnp.bfloat16)
    if grid.square:
        down_way.spread()
        hidden_way.forward("y")
        first_far[0] = tie(first_far[0], query, own, hidden_way.over_x, hidden_way.over_y)
    far, done = [], ()
    for row in range(rows):
        far.append(dot_last(first_far[row], both_full).astype(jnp.bfloat16))
        done = attend(query, own, far[row], query_ids, key_ids, row, *done)
        if row == 0 and grid.square:
            down_way.forward("y", done[0])
            first_far[1] = tie(
                first_far[1], *hidden_way.blocks, down_way.over_x, down_way.over_y
            )
    attended, level = done
    if grid.square:
        hidden_blocks = place_blocks(grid, hidden_way.core(), hidden_way.order)
        hidden_blocks = hidden_blocks.reshape(-1, model, model)
        down_blocks = join_down(grid, down_way.core(attended), down_way.order, *down_weight.shape)
    used_rows = used.astype(jnp.float32).reshape(-1, 1)
    flat = (-1, model)
    (
        output,
        second_low,
        act_low,
        grad_pre,
        grad_middle,
        grad_proj,
        grad_attended,
        hidden_sums,
        middle_sums,
    ) = middle_block(
        stream.reshape(flat),
        attended.reshape(flat),
        cotangent.reshape(flat),
        used_rows,
        proj_full,
        hidden_blocks,
        down_blocks,
        proj_bias_full,
        gain_two,
        shift_two,
        hidden_bias_full,
        down_bias_full,
    )
    hidden_bias_grad = jnp.sum(hidden_sums, axis=0).reshape(-1)
    middle_sums = jnp.sum(middle_sums, axis=0)
    gain_two_grad, shift_two_grad = middle_sums[0], middle_sums[1]
    proj_bias_grad, down_bias_grad = middle_sums[2], middle_sums[3]
    grad_branch = jnp.where(used[..., None], cotangent, 0).reshape(flat)
    here, outer = grid.at["c"].astype(jnp.int32).reshape(1), grid.outer_count
    if grid.square:
        keep, give = tall_grad(act_low, grad_branch, here, outer, "down_weight_grad")
        down_way = Scatter(grid, keep, give, (outer, 2, 2) + keep.shape[2:])
        second_low = tie(second_low, give)
        keep, give = wide_grad(second_low, grad_pre, here, outer, "hidden_weight_grad")
        hidden_way = Scatter(grid, keep, give, (outer, -1, keep.shape[1]))
        down_way.pull(give)
        down_way.push("x", choose_dim(2))
        hidden_way.pull(down_way.sent)
        hidden_way.push("y", choose_lanes)
        grad_attended = tie(grad_attended, hidden_way.sent)
    else:
        down_grad = outer_dot(act_low, grad_branch)
        hidden_grad = outer_dot(second_low, grad_pre)
    output = output.reshape(stream.shape)
    grad_middle = grad_middle.reshape(stream.shape)
    grad_attended = grad_attended.reshape(stream.shape)

    grad_far, done = [], ()
    for row in range(rows):
        done = attend_back(
            query,
            own,
            far[row],
            attended,
            grad_attended,
            level,
            query_ids,
            key_ids,
            row,
            *done,
        )
        both_grad = done[1]
        if grid.square:
            down_way.pull(both_grad)
            hidden_way.pull(down_way.value)
            if row == 0:
                down_way.push("y", choose_dim(1))
                hidden_way.push("x", choose_lanes)
            else:
                down_way.push("z", choose_half, 2)
                hidden_way.push("z", choose_odd, 1)
            both_grad = tie(both_grad, down_way.sent, hidden_way.sent, *grad_far)
        share = dot_back(both_grad[row : row + 1, all_rows:], both_full).astype(jnp.bfloat16)
        grad_far.append(far_send(grid, share))
        done = (done[0], tie(both_grad, share))
    query_grad, both_grad = done
    both_flat = both_grad.reshape(-1, 2 * model)
    query_flat = query_grad.reshape(flat)
    if grid.square:
        keep, give = mixed_grad(
            first_low.reshape(flat),
            [value[0] for value in first_far],
            attended.reshape(flat),
            query_flat,
            both_flat,
            grad_proj,
            here,
            outer,
        )
        mixed_way = Scatter(grid, keep, give, (outer, -1, keep.shape[1]))
        down_way.pull(give)
        down_way.push("z", choose_half, 1)
        hidden_way.pull(give)
        hidden_way.push("z", choose_half, 2)
        query_grad = tie(query_grad, hidden_way.sent, down_way.sent, *grad_far)
        both_grad = tie(both_grad, hidden_way.sent, down_way.sent, *grad_far)
    else:
        first_all = [jnp.concatenate([first_low[row], first_far[row][0]]) for row in range(rows)]
        both_weight_grad = outer_dot(jnp.concatenate(first_all), both_flat)
        query_weight_grad = outer_dot(first_low.reshape(flat), query_flat)
        proj_grad = outer_dot(attended.reshape(flat), grad_proj)
    grad_first = dot_back(query_grad, query_full) + dot_back(both_grad[:, :all_rows], both_full)
    if grid.square:
        mixed_way.pull(grad_first)
        way_a, way_b = fork(mixed_way)
        way_a.push("y", choose_lanes)
        way_b.push("x", choose_odd_lanes)
        grad_first = tie(grad_first, way_a.sent, way_b.sent)
    grad_first = grad_first + jnp.concatenate(grad_far).astype(jnp.float32)
    grad_norm, gain_one_grad, shift_one_grad = layer_norm_back(
        grad_first, first_normal, first_scale, gain_one
    )
    grad_stream = (grad_middle + grad_norm).astype(jnp.bfloat16)
    skip_bias_grad = jnp.sum(grad_stream.astype(jnp.float32), axis=(0, 1))
    joined_flat, stream_flat = joined.reshape(-1, 2 * model), grad_stream.reshape(flat)
    if grid.square:
        keep, give = tall_grad(joined_flat, stream_flat, here, outer, "skip_weight_grad")
        skip_way = Scatter(grid, keep, give, (outer, 2, 2) + keep.shape[2:])
        grad_stream = tie(grad_stream, give)
    else:
        skip_weight_grad = outer_dot(joined_flat, stream_flat)
    vectors = scatter_vectors(
        grid,
        [
            skip_bias_grad,
            gain_one_grad,
            shift_one_grad,
            proj_bias_grad,
            gain_two_grad,
            shift_two_grad,
            hidden_bias_grad,
            down_bias_grad,
        ],
    )
    input_grad = dot_back(grad_stream, skip_full[:model])
    if grid.square:
        skip_way.pull(input_grad)
        skip_way.push("x", choose_dim(2))
        grad_stream = tie(grad_stream, skip_way.sent)
    skip_grad = dot_back(grad_stream, skip_full[model:])
    if grid.square:
        way_a.pull(skip_grad)
        way_b.pull(skip_grad)
        way_a.push("x", choose_lanes)
        way_b.push("y", choose_lanes)
        skip_way.pull(way_a.sent, way_b.sent)
        skip_way.push("y", choose_dim(1))
        way_a.pull(skip_way.sent)
        way_b.pull(skip_way.sent)
        mixed_way.value = jnp.concatenate([way_a.value, way_b.value], axis=1)
        mixed_way.push("z", choose_half, 2)
        skip_way.pull(mixed_way.sent)
        skip_way.push("z", choose_odd, 1)
        mixed_way.pull(skip_way.sent)
        mixed_way.push("z", choose_half, 1)
        skip_way.pull(mixed_way.sent)
        skip_way.push("z", choose_half, 2)
        vectors = vectors(skip_way.sent)

        def tall_shard(way, shape):
            total = way.mine.astype(jnp.float32) + way.got.astype(jnp.float32)
            return unpack_lanes(total[0], *shape)

        def wide_shard(way):
            return (way.mine.astype(jnp.float32) + way.got.astype(jnp.float32))[0]

        down_shard = tall_shard(down_way, down_weight.shape)
        hidden_shard = wide_shard(hidden_way)
        skip_shard = tall_shard(skip_way, skip_weight.shape)
        mixed_shard = wide_shard(mixed_way)
        qkv_shard = mixed_shard[:, : qkv_weight.shape[1]]
        proj_shard = mixed_shard[:, qkv_weight.shape[1] :]
    else:
        down_shard = seq_scatter(down_grad)
        hidden_shard = seq_scatter(hidden_grad)
        skip_shard = seq_scatter(skip_weight_grad)
        proj_shard = seq_scatter(proj_grad)
        qkv_shard = seq_scatter(jnp.concatenate([query_weight_grad, both_weight_grad], axis=1))
        vectors = vectors()

    moved = items.moved[..., None] & (grid.seq_index == half - 1)
    results = [output, input_grad, skip_grad]
    tails = jnp.stack([value[:, own_rows:].astype(jnp.float32) for value in results])
    tails = grid.shift(tails, half, half - 1)

    def settle(place):
        own = results[place][:, :own_rows]
        tail = own[:, own_rows - halo_rows :]
        tail = jnp.where(moved, tails[place].astype(own.dtype), tail)
        return lax.dynamic_update_slice_in_dim(own, tail, own_rows - halo_rows, 1)

    return (
        settle(0),
        settle(1),
        settle(2),
        skip_shard,
        vectors[0],
        vectors[1],
        vectors[2],
        qkv_shard,
        proj_shard,
        vectors[3],
        vectors[4],
        vectors[5],
        hidden_shard,
        vectors[6],
        down_shard,
        vectors[7],
    )


def solution(mesh):
    return jax.shard_map(
        body,
        mesh=mesh,
        in_specs=(
            P("batch", "seq", None),
            P("batch", "seq", None),
            P("batch", "seq", None),
            P("batch", None),
            P("batch", None),
            P("batch", "seq"),
            P("seq"),
            P("seq"),
            P("seq"),
            P("batch", "seq"),
            P("batch", "seq"),
            P("seq"),
            P("seq"),
            P("seq"),
            P("batch", "seq"),
            P("seq"),
            P("batch", "seq"),
            P("seq"),
        ),
        out_specs=(
            P("batch", "seq", None),
            P("batch", "seq", None),
            P("batch", "seq", None),
            P("batch", "seq"),
            P("seq"),
            P("seq"),
            P("seq"),
            P("batch", "seq"),
            P("batch", "seq"),
            P("seq"),
            P("seq"),
            P("seq"),
            P("batch", "seq"),
            P("seq"),
            P("batch", "seq"),
            P("seq"),
        ),
        check_vma=False,
    )
```

```python
import jax
import jax.numpy as jnp
from jax import lax
from jax.experimental import pallas as pl
from jax.experimental.pallas import tpu as pltpu
from jax.sharding import PartitionSpec as P

HEADS = 16
HEAD_DIM = 72
LANES = 128
epsilon = 1e-05
masked_score = -1e30
VMEM_BYTES = 60 * 1024 * 1024
def nt_dot(left_side, right_side):
    return lax.dot_general(
        left_side, right_side, (((1,), (1,)), ((), ())), preferred_element_type=jnp.float32
    )


def tn_dot(left_side, right_side):
    return lax.dot_general(
        left_side, right_side, (((0,), (0,)), ((), ())), preferred_element_type=jnp.float32
    )


def nn_dot(left_side, right_side):
    return lax.dot_general(
        left_side, right_side, (((1,), (0,)), ((), ())), preferred_element_type=jnp.float32
    )


def split_heads(wide, head_ref, start=0):
    rows = wide.shape[0]
    pad = jnp.zeros((rows, LANES - HEAD_DIM), wide.dtype)
    for head in range(HEADS):
        piece = wide[:, head * HEAD_DIM : (head + 1) * HEAD_DIM]
        head_ref[head, start : start + rows] = jnp.concatenate([piece, pad], axis=1)


def split_keys(own_ref, far_ref, kh, vh):
    features = own_ref.shape[2] // 2
    start = 0
    for ref in (own_ref, far_ref):
        split_heads(ref[0, :, :features], kh, start)
        split_heads(ref[0, :, features:], vh, start)
        start += ref.shape[1]


def join_heads(head_ref):
    return jnp.concatenate([head_ref[head][:, :HEAD_DIM] for head in range(HEADS)], axis=1)


def chunk_of(rows):
    for count in (4, 2, 1):
        if rows % (count * 16) == 0:
            return rows // count
    return rows


def attend_kernel(
    q_ref, own_ref, far_ref, qid_ref, kid_ref, *refs
):
    out_ref, lse_ref, qh, kh, vh, score, prob = refs[-7:]
    split_heads(q_ref[0], qh)
    split_keys(own_ref, far_ref, kh, vh)
    key_rows = kh.shape[1]
    step = chunk_of(key_rows)
    scale = HEAD_DIM ** (-0.5)
    query_ids = qid_ref[0]

    def one_head(head, carry):
        query = qh[head]
        top = jnp.full((1, query.shape[0]), masked_score, jnp.float32)
        for start in range(0, key_rows, step):
            part = nt_dot(kh[head, start : start + step], query) * scale
            part = jnp.where(kid_ref[0, start : start + step] == query_ids, part, masked_score)
            score[start : start + step] = part
            top = jnp.maximum(top, jnp.max(part, axis=0, keepdims=True))
        total = jnp.zeros_like(top)
        for start in range(0, key_rows, step):
            part = jnp.exp(score[start : start + step] - top)
            total = total + jnp.sum(part, axis=0, keepdims=True)
            prob[start : start + step] = part.astype(jnp.bfloat16)
        mixed = tn_dot(vh[head], prob[...]) / total
        qh[head] = mixed.T.astype(jnp.bfloat16)
        lse_ref[0, pl.ds(head, 1)] = top + jnp.log(total)
        return carry

    lax.fori_loop(0, HEADS, one_head, 0)
    out_ref[0] = join_heads(qh)


def attend(query, own, far, query_ids, key_ids, row, *old):
    rows, width, features = query.shape
    far_rows = far.shape[1]
    key_rows = width + far_rows
    here = lambda i: (row, 0, 0)
    only = lambda i: (0, 0, 0)
    wide = pl.BlockSpec((1, width, features), here)
    levels = pl.BlockSpec((1, HEADS, width), here)
    return pl.pallas_call(
        attend_kernel,
        grid=(1,),
        in_specs=[
            wide,
            pl.BlockSpec((1, width, 2 * features), here),
            pl.BlockSpec((1, far_rows, 2 * features), only),
            pl.BlockSpec((1, 1, width), here),
            pl.BlockSpec((1, key_rows, 1), here),
        ]
        + [pl.BlockSpec(memory_space=pl.ANY)] * len(old),
        out_specs=[wide, levels],
        out_shape=[
            jax.ShapeDtypeStruct((rows, width, features), jnp.bfloat16),
            jax.ShapeDtypeStruct((rows, HEADS, width), jnp.float32),
        ],
        scratch_shapes=[
            pltpu.VMEM((HEADS, width, LANES), jnp.bfloat16),
            pltpu.VMEM((HEADS, key_rows, LANES), jnp.bfloat16),
            pltpu.VMEM((HEADS, key_rows, LANES), jnp.bfloat16),
            pltpu.VMEM((key_rows, width), jnp.float32),
            pltpu.VMEM((key_rows, width), jnp.bfloat16),
        ],
        input_output_aliases={5: 0, 6: 1} if old else {},
        compiler_params=pltpu.CompilerParams(vmem_limit_bytes=VMEM_BYTES),
        cost_estimate=pl.CostEstimate(
            flops=4 * HEADS * width * key_rows * LANES,
            transcendentals=HEADS * width * key_rows,
            bytes_accessed=4 * features * (width + key_rows),
        ),
        name="attend",
    )(query, own, far, query_ids, key_ids, *old)


def attend_back_kernel(
    q_ref, own_ref, far_ref, o_ref, g_ref, lse_ref, qid_ref, kid_ref, *refs
):
    dq_ref, dkv_ref, qh, kh, vh, oh, gh, prob, slope = refs[-9:]
    split_heads(q_ref[0], qh)
    features = q_ref.shape[2]
    split_keys(own_ref, far_ref, kh, vh)
    split_heads(o_ref[0], oh)
    split_heads(g_ref[0], gh)
    key_rows = kh.shape[1]
    step = chunk_of(key_rows)
    scale = HEAD_DIM ** (-0.5)
    query_ids = qid_ref[0]

    def one_head(head, carry):
        query = qh[head]
        grad = gh[head]
        level = lse_ref[0, pl.ds(head, 1)]
        overlap = oh[head].astype(jnp.float32) * grad.astype(jnp.float32)
        row_dot = jnp.sum(overlap.T, axis=0, keepdims=True)
        for start in range(0, key_rows, step):
            part = nt_dot(kh[head, start : start + step], query) * scale
            part = jnp.where(kid_ref[0, start : start + step] == query_ids, part, masked_score)
            soft = jnp.exp(part - level)
            prob[start : start + step] = soft.astype(jnp.bfloat16)
            turn = nt_dot(vh[head, start : start + step], grad)
            slope[start : start + step] = (soft * (turn - row_dot)).astype(jnp.bfloat16)
        value_grad = nn_dot(prob[...], grad)
        query_grad = tn_dot(kh[head], slope[...]) * scale
        key_grad = nn_dot(slope[...], query) * scale
        vh[head] = value_grad.astype(jnp.bfloat16)
        kh[head] = key_grad.astype(jnp.bfloat16)
        qh[head] = query_grad.T.astype(jnp.bfloat16)
        return carry

    lax.fori_loop(0, HEADS, one_head, 0)
    dq_ref[0] = join_heads(qh)
    dkv_ref[0, :, :features] = join_heads(kh)
    dkv_ref[0, :, features:] = join_heads(vh)


def attend_back(
    query, own, far, mixed, grad, level, query_ids, key_ids, row, *old
):
    rows, width, features = query.shape
    far_rows = far.shape[1]
    key_rows = width + far_rows
    here = lambda i: (row, 0, 0)
    only = lambda i: (0, 0, 0)
    wide = pl.BlockSpec((1, width, features), here, pipeline_mode=pl.Buffered(1))
    return pl.pallas_call(
        attend_back_kernel,
        grid=(1,),
        in_specs=[
            wide,
            pl.BlockSpec((1, width, 2 * features), here, pipeline_mode=pl.Buffered(1)),
            pl.BlockSpec((1, far_rows, 2 * features), only, pipeline_mode=pl.Buffered(1)),
            wide,
            wide,
            pl.BlockSpec((1, HEADS, width), here),
            pl.BlockSpec((1, 1, width), here),
            pl.BlockSpec((1, key_rows, 1), here),
        ]
        + [pl.BlockSpec(memory_space=pl.ANY)] * len(old),
        out_specs=[
            pl.BlockSpec((1, width, features), here),
            pl.BlockSpec((1, key_rows, 2 * features), here),
        ],
        out_shape=[
            jax.ShapeDtypeStruct((rows, width, features), jnp.bfloat16),
            jax.ShapeDtypeStruct((rows, key_rows, 2 * features), jnp.bfloat16),
        ],
        scratch_shapes=[
            pltpu.VMEM((HEADS, width, LANES), jnp.bfloat16),
            pltpu.VMEM((HEADS, key_rows, LANES), jnp.bfloat16),
            pltpu.VMEM((HEADS, key_rows, LANES), jnp.bfloat16),
            pltpu.VMEM((HEADS, width, LANES), jnp.bfloat16),
            pltpu.VMEM((HEADS, width, LANES), jnp.bfloat16),
            pltpu.VMEM((key_rows, width), jnp.bfloat16),
            pltpu.VMEM((key_rows, width), jnp.bfloat16),
        ],
        input_output_aliases={8: 0, 9: 1} if old else {},
        compiler_params=pltpu.CompilerParams(vmem_limit_bytes=VMEM_BYTES),
        cost_estimate=pl.CostEstimate(
            flops=10 * HEADS * width * key_rows * LANES,
            transcendentals=HEADS * width * key_rows,
            bytes_accessed=8 * features * (width + key_rows),
        ),
        name="attend_back",
    )(
        query,
        own,
        far,
        mixed,
        grad,
        level,
        query_ids,
        key_ids,
        *old,
    )


def split_rows(total_ref, here, outer, keep_ref, give_ref):
    inner = total_ref.shape[0] // (2 * outer)
    for group in range(outer):
        start = group * 2 * inner
        span = slice(group * inner, (group + 1) * inner)
        keep_ref[span] = total_ref[pl.ds(pl.multiple_of(start + here * inner, 16), inner)]
        give_ref[span] = total_ref[pl.ds(pl.multiple_of(start + (1 - here) * inner, 16), inner)]


def wide_grad_kernel(outer, here_ref, left_ref, right_ref, keep_ref, give_ref, total):
    total[...] = tn_dot(left_ref[...], right_ref[...]).astype(jnp.bfloat16)
    split_rows(total, here_ref[0], outer, keep_ref, give_ref)


def wide_grad(left, right, here, outer, name):
    tokens, rows = left.shape
    blocks = right.shape[1] // rows
    half = jax.ShapeDtypeStruct((rows // 2, right.shape[1]), jnp.bfloat16)
    spec = pl.BlockSpec((rows // 2, rows), lambda j, here: (0, j))
    return pl.pallas_call(
        lambda *refs: wide_grad_kernel(outer, *refs),
        grid_spec=pltpu.PrefetchScalarGridSpec(
            num_scalar_prefetch=1,
            grid=(blocks,),
            in_specs=[
                pl.BlockSpec((tokens, rows), lambda j, here: (0, 0)),
                pl.BlockSpec((tokens, rows), lambda j, here: (0, j)),
            ],
            out_specs=[spec, spec],
            scratch_shapes=[pltpu.VMEM((rows, rows), jnp.bfloat16)],
        ),
        out_shape=[half, half],
        compiler_params=pltpu.CompilerParams(vmem_limit_bytes=VMEM_BYTES),
        cost_estimate=pl.CostEstimate(
            flops=2 * tokens * rows * right.shape[1],
            transcendentals=0,
            bytes_accessed=2 * (tokens + right.shape[1]) * rows,
        ),
        name=name,
    )(here, left, right)


def tall_grad_kernel(groups, here_ref, left_ref, right_ref, keep_ref, give_ref, total):
    total[...] = tn_dot(left_ref[...], right_ref[...]).astype(jnp.bfloat16)
    here = here_ref[0]
    inner = total.shape[0] // (2 * groups)
    columns = total.shape[1] // 4
    for group in range(groups):
        start = group * 2 * inner
        for core, out_ref in ((here, keep_ref), (1 - here, give_ref)):
            rows = total[pl.ds(pl.multiple_of(start + core * inner, 16), inner)]
            for place in range(4):
                out_ref[group, place] = pack_lanes(rows[:, place * columns : (place + 1) * columns])


def tall_grad(left, right, here, outer, name):
    tokens, model = right.shape
    blocks = left.shape[1] // model
    groups = outer // blocks
    packed = left.shape[1] // (2 * outer) * (model // 4) // LANES
    half = jax.ShapeDtypeStruct((outer, 4, packed, LANES), jnp.bfloat16)
    spec = pl.BlockSpec((groups, 4, packed, LANES), lambda i, here: (i, 0, 0, 0))
    return pl.pallas_call(
        lambda *refs: tall_grad_kernel(groups, *refs),
        grid_spec=pltpu.PrefetchScalarGridSpec(
            num_scalar_prefetch=1,
            grid=(blocks,),
            in_specs=[
                pl.BlockSpec((tokens, model), lambda i, here: (0, i)),
                pl.BlockSpec((tokens, model), lambda i, here: (0, 0)),
            ],
            out_specs=[spec, spec],
            scratch_shapes=[pltpu.VMEM((model, model), jnp.bfloat16)],
        ),
        out_shape=[half, half],
        compiler_params=pltpu.CompilerParams(vmem_limit_bytes=VMEM_BYTES),
        cost_estimate=pl.CostEstimate(
            flops=2 * tokens * model * left.shape[1],
            transcendentals=0,
            bytes_accessed=2 * (tokens + model) * left.shape[1],
        ),
        name=name,
    )(here, left, right)


def mixed_grad_kernel(
    outer, here_ref, first_ref, far_a, far_b, att_ref, query_ref, both_ref, proj_ref,
    keep_ref, give_ref, total, sums,
):
    step = pl.program_id(0)
    width = far_a.shape[0]
    span = far_a.shape[0] + first_ref.shape[0] // 2
    own = first_ref.shape[0] // 2

    @pl.when(step == 0)
    def _():
        total[0] = tn_dot(first_ref[...], query_ref[...]).astype(jnp.bfloat16)

    @pl.when((step == 1) | (step == 2))
    def _():
        sums[...] = tn_dot(first_ref[0:own], both_ref[0:own])
        sums[...] += tn_dot(far_a[...], both_ref[own:span])
        sums[...] += tn_dot(first_ref[own:], both_ref[span : span + own])
        total[step] = (sums[...] + tn_dot(far_b[...], both_ref[span + own :])).astype(jnp.bfloat16)

    @pl.when(step == 3)
    def _():
        total[3] = tn_dot(att_ref[...], proj_ref[...]).astype(jnp.bfloat16)
        here = here_ref[0]
        model = total.shape[2]
        inner = model // (2 * outer)
        cut = model * 3 // 4
        for group in range(outer):
            rows = slice(group * inner, (group + 1) * inner)
            for core, out_ref in ((here, keep_ref), (1 - here, give_ref)):
                start = pl.multiple_of((group * 2 + core) * inner, 16)
                wide = jnp.concatenate([total[k, pl.ds(start, inner)] for k in range(3)], axis=1)
                last = total[3, pl.ds(start, inner)]
                for place in range(4):
                    out_ref[rows, place * model : (place + 1) * model] = jnp.concatenate(
                        [
                            wide[:, place * cut : (place + 1) * cut],
                            last[:, place * (model - cut) : (place + 1) * (model - cut)],
                        ],
                        axis=1,
                    )


def mixed_grad(first, far, attended, query_grad, both_grad, proj_grad, here, outer):
    tokens, model = first.shape
    half = jax.ShapeDtypeStruct((model // 2, 4 * model), jnp.bfloat16)
    fixed = lambda *shape: pl.BlockSpec(
        shape, lambda j, here: (0, 0), pipeline_mode=pl.Buffered(1)
    )
    return pl.pallas_call(
        lambda *refs: mixed_grad_kernel(outer, *refs),
        grid_spec=pltpu.PrefetchScalarGridSpec(
            num_scalar_prefetch=1,
            grid=(4,),
            in_specs=[
                fixed(tokens, model),
                fixed(*far[0].shape),
                fixed(*far[1].shape),
                fixed(tokens, model),
                fixed(tokens, model),
                pl.BlockSpec(
                    (both_grad.shape[0], model),
                    lambda j, here: (0, jnp.minimum(jnp.maximum(j - 1, 0), 1)),
                ),
                fixed(tokens, model),
            ],
            out_specs=[fixed(model // 2, 4 * model), fixed(model // 2, 4 * model)],
            scratch_shapes=[
                pltpu.VMEM((4, model, model), jnp.bfloat16),
                pltpu.VMEM((model, model), jnp.float32),
            ],
        ),
        out_shape=[half, half],
        compiler_params=pltpu.CompilerParams(vmem_limit_bytes=VMEM_BYTES),
        cost_estimate=pl.CostEstimate(
            flops=2 * model * model * (2 * tokens + 2 * both_grad.shape[0]),
            transcendentals=0,
            bytes_accessed=2 * model * (6 * tokens + 2 * both_grad.shape[0] + 4 * model),
        ),
        name="mixed_weight_grad",
    )(here, first, far[0], far[1], attended, query_grad, both_grad, proj_grad)


def column_chunks(width):
    cut = width // 256 // 2 * 256
    return ((0, cut), (cut, width)) if cut else ((0, width),)


def middle_kernel(
    stream_ref, att_ref, cot_ref, used_ref, proj_ref, hidden_ref, down_ref,
    proj_bias_ref, gain_ref, shift_ref, hidden_bias_ref, down_bias_ref,
    out_ref, second_ref, act_ref, pre_ref, middle_grad_ref, proj_grad_ref, att_grad_ref,
    hidden_sum_ref, sums_ref,
    low, normal, scale, branch, total, back,
):
    step = pl.program_id(1)
    steps = pl.num_programs(1)

    @pl.when(step == 0)
    def _():
        middle = stream_ref[...] + nn_dot(att_ref[...], proj_ref[...]) + proj_bias_ref[...]
        centred = middle - jnp.mean(middle, axis=-1, keepdims=True)
        inverse = lax.rsqrt(jnp.mean(centred * centred, axis=-1, keepdims=True) + epsilon)
        unit = centred * inverse
        normal[...] = unit
        scale[...] = inverse
        second = (unit * gain_ref[...] + shift_ref[...]).astype(jnp.bfloat16)
        low[...] = second
        second_ref[...] = second
        branch[...] = (cot_ref[...].astype(jnp.float32) * used_ref[...]).astype(jnp.bfloat16)
        total[...] = middle + down_bias_ref[...]
        back[...] = jnp.zeros_like(back)

    for start, stop in column_chunks(hidden_ref.shape[2]):
        pre_act = nn_dot(low[...], hidden_ref[0, :, start:stop]) + hidden_bias_ref[0, :, start:stop]
        grad_act = nt_dot(branch[...], down_ref[0, start:stop])
        below = 0.5 + 0.5 * lax.erf(pre_act * (0.5**0.5))
        density = jnp.exp(-0.5 * pre_act * pre_act) * ((2.0 * jnp.pi) ** -0.5)
        act = (pre_act * below).astype(jnp.bfloat16)
        grad_pre = (grad_act * (below + pre_act * density)).astype(jnp.bfloat16)
        act_ref[:, start:stop] = act
        pre_ref[:, start:stop] = grad_pre
        hidden_sum_ref[0, 0, :, start:stop] = jnp.sum(
            grad_pre.astype(jnp.float32), axis=0, keepdims=True
        )
        total[...] += nn_dot(act, down_ref[0, start:stop])
        back[...] += nt_dot(grad_pre, hidden_ref[0, :, start:stop])

    @pl.when(step == steps - 1)
    def _():
        out_ref[...] = total[...].astype(jnp.bfloat16)
        grad = back[...]
        unit = normal[...]
        part = grad * gain_ref[...]
        mean_part = jnp.mean(part, axis=-1, keepdims=True)
        mean_both = jnp.mean(part * unit, axis=-1, keepdims=True)
        grad_out = cot_ref[...].astype(jnp.float32) * used_ref[...]
        grad_middle = grad_out + (part - mean_part - unit * mean_both) * scale[...]
        middle_grad_ref[...] = grad_middle
        grad_low = grad_middle.astype(jnp.bfloat16)
        proj_grad_ref[...] = grad_low
        att_grad_ref[...] = nt_dot(grad_low, proj_ref[...]).astype(jnp.bfloat16)
        sums_ref[0, 0:1] = jnp.sum(grad * unit, axis=0, keepdims=True)
        sums_ref[0, 1:2] = jnp.sum(grad, axis=0, keepdims=True)
        sums_ref[0, 2:3] = jnp.sum(grad_low.astype(jnp.float32), axis=0, keepdims=True)
        sums_ref[0, 3:4] = jnp.sum(grad_out, axis=0, keepdims=True)


def token_block(tokens):
    return tokens // 4 if tokens % 64 == 0 else tokens


def middle_block(
    stream, attended, cotangent, used, proj, hidden, down, proj_bias, gain, shift, hidden_bias,
    down_bias,
):
    tokens, model = stream.shape
    steps = hidden.shape[0]
    rows = token_block(tokens)
    blocks = tokens // rows
    by_rows = pl.BlockSpec((rows, model), lambda i, s: (i, 0))
    by_step = pl.BlockSpec((rows, model), lambda i, s: (i, s))
    vector = pl.BlockSpec((1, model), lambda i, s: (0, 0))
    low_rows = jax.ShapeDtypeStruct((tokens, model), jnp.bfloat16)
    low_steps = jax.ShapeDtypeStruct((tokens, steps * model), jnp.bfloat16)
    flops = 2 * tokens * model * model * (4 * steps + 2)
    return pl.pallas_call(
        middle_kernel,
        grid=(blocks, steps),
        in_specs=[
            by_rows,
            by_rows,
            by_rows,
            pl.BlockSpec((rows, 1), lambda i, s: (i, 0)),
            pl.BlockSpec((model, model), lambda i, s: (0, 0), pipeline_mode=pl.Buffered(1)),
            pl.BlockSpec((1, model, model), lambda i, s: (s, 0, 0)),
            pl.BlockSpec((1, model, model), lambda i, s: (s, 0, 0)),
            vector,
            vector,
            vector,
            pl.BlockSpec((1, 1, model), lambda i, s: (s, 0, 0)),
            vector,
        ],
        out_specs=[
            by_rows,
            by_rows,
            by_step,
            by_step,
            by_rows,
            by_rows,
            by_rows,
            pl.BlockSpec((1, 1, 1, model), lambda i, s: (i, s, 0, 0)),
            pl.BlockSpec((1, 4, model), lambda i, s: (i, 0, 0)),
        ],
        out_shape=[
            low_rows,
            low_rows,
            low_steps,
            low_steps,
            jax.ShapeDtypeStruct((tokens, model), jnp.float32),
            low_rows,
            low_rows,
            jax.ShapeDtypeStruct((blocks, steps, 1, model), jnp.float32),
            jax.ShapeDtypeStruct((blocks, 4, model), jnp.float32),
        ],
        scratch_shapes=[
            pltpu.VMEM((rows, model), jnp.bfloat16),
            pltpu.VMEM((rows, model), jnp.float32),
            pltpu.VMEM((rows, 1), jnp.float32),
            pltpu.VMEM((rows, model), jnp.bfloat16),
            pltpu.VMEM((rows, model), jnp.float32),
            pltpu.VMEM((rows, model), jnp.float32),
        ],
        compiler_params=pltpu.CompilerParams(vmem_limit_bytes=VMEM_BYTES),
        cost_estimate=pl.CostEstimate(
            flops=flops,
            transcendentals=2 * tokens * model * steps,
            bytes_accessed=2 * tokens * model * (2 * steps + 12) + 4 * model * model * steps * blocks,
        ),
        name="middle_block",
    )(
        stream,
        attended,
        cotangent,
        used,
        proj,
        hidden,
        down,
        proj_bias[None],
        gain[None],
        shift[None],
        hidden_bias.reshape(steps, 1, model),
        down_bias[None],
    )


def layer_norm(stream, norm_gain, norm_shift):
    centred = stream - jnp.mean(stream, axis=-1, keepdims=True)
    scale = lax.rsqrt(jnp.mean(centred * centred, axis=-1, keepdims=True) + epsilon)
    normal = centred * scale
    return (normal * norm_gain + norm_shift).astype(jnp.bfloat16), normal, scale


def layer_norm_back(grad, normal, scale, norm_gain):
    part = grad * norm_gain
    mean_part = jnp.mean(part, axis=-1, keepdims=True)
    mean_both = jnp.mean(part * normal, axis=-1, keepdims=True)
    gain_grad = jnp.sum(grad * normal, axis=(0, 1))
    shift_grad = jnp.sum(grad, axis=(0, 1))
    return (part - mean_part - normal * mean_both) * scale, gain_grad, shift_grad


def outer_dot(left_side, right_side):
    return lax.dot_general(
        left_side, right_side, (((0,), (0,)), ((), ())), preferred_element_type=jnp.bfloat16
    )


def dot_last(left_side, right_side):
    return lax.dot_general(
        left_side, right_side, (((2,), (0,)), ((), ())), preferred_element_type=jnp.float32
    )


def dot_back(left_side, right_side):
    return lax.dot_general(
        left_side, right_side, (((2,), (1,)), ((), ())), preferred_element_type=jnp.float32
    )


def dot_tokens(left_side, right_side):
    return lax.dot_general(
        left_side, right_side, (((0, 1), (0, 1)), ((), ())), preferred_element_type=jnp.bfloat16
    )


class Grid:
    def __init__(self):
        self.batch_count = lax.axis_size("batch")
        self.seq_count = lax.axis_size("seq")
        self.seq_index = lax.axis_index("seq")
        batch_index = lax.axis_index("batch")
        self.outer_count = self.batch_count // 2
        self.square = self.seq_count == 4 and self.outer_count == 4
        self.at = {
            "z": batch_index // 2,
            "c": batch_index % 2,
            "y": self.seq_index // 2,
            "x": self.seq_index % 2,
        }

    def index(self, z, c, s):
        return (z * 2 + c) * self.seq_count + s

    def send(self, value, axis, turn=0):
        pairs = []
        for z in range(self.outer_count):
            for c in range(2):
                for s in range(self.seq_count):
                    far_z, far_c, far_s = z, c, s
                    if axis == "z":
                        far_z = z ^ turn
                    elif axis == "c":
                        far_c = 1 - c
                    elif axis == "y":
                        far_s = s ^ 2
                    else:
                        far_s = s ^ 1
                    pairs.append((self.index(z, c, s), self.index(far_z, far_c, far_s)))
        return lax.ppermute(value, ("batch", "seq"), pairs)

    def shift(self, value, source, target):
        pairs = [
            (b * self.seq_count + source, b * self.seq_count + target)
            for b in range(self.batch_count)
        ]
        return lax.ppermute(value, ("batch", "seq"), pairs)


def tie(value, *others):
    return lax.optimization_barrier((value, *others))[0]


def square_gather(grid, shard):
    over_x = grid.send(shard, "x")
    found = jnp.stack([shard, over_x, grid.send(shard, "y"), grid.send(over_x, "y")])
    return jnp.stack(
        [
            lax.dynamic_index_in_dim(found, grid.seq_index ^ place, 0, keepdims=False)
            for place in range(4)
        ]
    )


def pack_lanes(shard):
    rows, columns = shard.shape
    whole = columns // LANES
    rest = columns - whole * LANES
    pieces = [shard[:, k * LANES : (k + 1) * LANES] for k in range(whole)]
    if rest:
        fold = LANES // rest
        step = rows // fold
        last = [shard[k * step : (k + 1) * step, whole * LANES :] for k in range(fold)]
        pieces.append(jnp.concatenate(last, axis=1))
    return jnp.concatenate(pieces, axis=0)


def unpack_lanes(packed, rows, columns):
    whole = columns // LANES
    rest = columns - whole * LANES
    pieces = [packed[k * rows : (k + 1) * rows] for k in range(whole)]
    if rest:
        fold = LANES // rest
        last = packed[whole * rows : whole * rows + rows // fold]
        pieces.append(
            jnp.concatenate([last[:, k * rest : (k + 1) * rest] for k in range(fold)], axis=0)
        )
    return jnp.concatenate(pieces, axis=1)


def rows_kernel(rows, columns, turn_ref, to_ref, *refs):
    blocks, out_ref, found = refs[:8], refs[8], refs[9]
    for block in range(8):
        found[to_ref[block]] = blocks[block][...]
    for core in range(2):
        wide = [unpack_lanes(found[core * 4 + place], rows, columns) for place in range(4)]
        out_ref[core * rows : (core + 1) * rows] = jnp.concatenate(wide, axis=1)


def mixed_kernel(columns, turn_ref, to_ref, *refs):
    blocks, query_ref, both_ref, proj_ref, found = refs[:8], refs[8], refs[9], refs[10], refs[11]
    rows, model = found.shape[1:]
    for block in range(8):
        found[to_ref[block]] = blocks[block][...]
    for core in range(2):
        span = slice(core * rows, (core + 1) * rows)
        parts = [found[core * 4 + place] for place in range(4)]
        wide = jnp.concatenate([part[:, :columns] for part in parts], axis=1)
        query_ref[span] = wide[:, :model]
        both_ref[span] = wide[:, model:]
        proj_ref[span] = jnp.concatenate([part[:, columns:] for part in parts], axis=1)


def swap_bits(value):
    return ((value & 1) << 1) | (value >> 1)


def assemble(grid, blocks, order, piece, kernel, widths, rows, name):
    outer = grid.outer_count
    turns = grid.at["z"] ^ jnp.arange(4, dtype=jnp.int32)
    if order[1] == 2:
        turns = swap_bits(turns)
    block = jnp.arange(8, dtype=jnp.int32)
    places = (grid.at["c"] ^ (block >> 2)) * 4 + (grid.seq_index ^ (block & 3))
    shapes = [jax.ShapeDtypeStruct((outer * 2 * rows, w), jnp.bfloat16) for w in widths]
    return pl.pallas_call(
        kernel,
        grid_spec=pltpu.PrefetchScalarGridSpec(
            num_scalar_prefetch=2,
            grid=(outer,),
            in_specs=[pl.BlockSpec(piece, lambda z, turn, to: (turn[z], 0))] * 8,
            out_specs=[pl.BlockSpec((2 * rows, w), lambda z, turn, to: (z, 0)) for w in widths],
            scratch_shapes=[pltpu.VMEM((8,) + piece, jnp.bfloat16)],
        ),
        out_shape=shapes,
        compiler_params=pltpu.CompilerParams(vmem_limit_bytes=VMEM_BYTES),
        cost_estimate=pl.CostEstimate(
            flops=0,
            transcendentals=0,
            bytes_accessed=8 * outer * rows * sum(widths),
        ),
        name=name,
    )(turns, places, *blocks)


def place_kernel(block_count, outer_count, to_ref, *refs):
    blocks, out_ref, sems = refs[:block_count], refs[block_count], refs[block_count + 1]
    rows = out_ref.shape[1]
    copies = []
    for block in range(block_count):
        for turn in range(outer_count):
            slot = block * outer_count + turn
            copies.append(
                pltpu.make_async_copy(
                    blocks[block].at[pl.ds(turn * rows, rows)], out_ref.at[to_ref[slot]], sems.at[slot]
                )
            )
    for copy in copies:
        copy.start()
    for copy in copies:
        copy.wait()


def place_blocks(grid, blocks, order):
    outer = grid.outer_count
    rows, columns = blocks[0].shape[0] // outer, blocks[0].shape[1]
    spot = jnp.arange(8 * outer, dtype=jnp.int32)
    core, place = grid.at["c"] ^ (spot >> 4), grid.seq_index ^ (spot >> 2 & 3)
    turn = spot & 3
    if order[1] == 2:
        turn = swap_bits(turn)
    slots = (place * outer + (grid.at["z"] ^ turn)) * 2 + core
    count = 8 * outer
    return pl.pallas_call(
        lambda *refs: place_kernel(8, outer, *refs),
        grid_spec=pltpu.PrefetchScalarGridSpec(
            num_scalar_prefetch=1,
            grid=(1,),
            in_specs=[pl.BlockSpec(memory_space=pl.ANY)] * 8,
            out_specs=pl.BlockSpec((count, rows, columns), lambda i, to: (0, 0, 0)),
            scratch_shapes=[pltpu.SemaphoreType.DMA((count,))],
        ),
        compiler_params=pltpu.CompilerParams(vmem_limit_bytes=VMEM_BYTES),
        out_shape=jax.ShapeDtypeStruct((count, rows, columns), blocks[0].dtype),
        cost_estimate=pl.CostEstimate(
            flops=0, transcendentals=0, bytes_accessed=4 * count * rows * columns
        ),
        name="place_blocks",
    )(slots, *blocks)


class Gather:
    def __init__(self, grid, piece):
        self.grid, self.piece, self.crossed = grid, piece, []

    def direct(self, *extra):
        self.order = [0, 1, 2, 3]
        parts = [self.piece] + [self.grid.send(self.piece, "z", turn) for turn in (1, 2, 3)]
        self.column = jnp.concatenate(parts + list(extra), axis=0)

    def first(self):
        self.order = [0, 2, 1, 3]
        self.far = self.grid.send(self.piece, "z", 2)

    def second(self, *after):
        piece = tie(self.piece, *after) if after else self.piece
        self.pair = jnp.concatenate([piece, self.far], axis=0)
        self.far = self.grid.send(self.pair, "z", 1)

    def last(self, *after):
        pair = tie(self.pair, *after) if after else self.pair
        self.column = jnp.concatenate([pair, self.far], axis=0)

    def spread(self):
        self.over_x = self.grid.send(self.column, "x")
        self.over_y = self.grid.send(self.column, "y")

    def forward(self, axis, *after):
        value = self.over_x if axis == "y" else self.over_y
        if after:
            value = tie(value, *after)
            if axis == "y":
                self.over_x = value
            else:
                self.over_y = value
        self.blocks = [self.column, self.over_x, self.over_y, self.grid.send(value, axis)]

    def cross(self, at, *after):
        block = (self.column, self.over_x, self.over_y)[at]
        block = tie(block, *after) if after else block
        self.crossed.append(self.grid.send(block, "c"))

    def core(self, *after):
        block = tie(self.blocks[3], *self.crossed[1:], *after)
        return self.blocks + self.crossed + [self.grid.send(block, "c")]


def split_vectors(joint, widths):
    result, start = [], 0
    for width in widths:
        result.append(joint[:, start : start + width].reshape(-1).astype(jnp.float32))
        start += width
    return result


def gather_plain(matrices, vectors):
    joint = lax.all_gather(jnp.concatenate(vectors), "seq", axis=0)
    wide = [
        lax.all_gather(
            lax.all_gather(shard, "batch", axis=0, tiled=True), "seq", axis=1, tiled=True
        )
        for shard in matrices
    ]
    return split_vectors(joint, [vector.shape[0] for vector in vectors]), wide


def hidden_columns(hidden_full, model):
    return jnp.stack(jnp.split(hidden_full, hidden_full.shape[1] // model, axis=1))


def gather_skip(grid, skip_weight, vectors):
    joint = jnp.concatenate(vectors)
    short = -joint.shape[0] % (8 * LANES)
    extra = jnp.pad(joint, (0, short)).reshape(-1, LANES)
    rows, columns = skip_weight.shape
    piece = pack_lanes(skip_weight)
    way = Gather(grid, piece)
    way.direct(extra)
    way.spread()
    way.forward("y")
    for at in range(3):
        way.cross(at)
    found = jnp.stack([block[-extra.shape[0] :].reshape(-1) for block in way.blocks])
    joint = jnp.stack(
        [
            lax.dynamic_index_in_dim(found, grid.seq_index ^ place, 0, keepdims=False)
            for place in range(4)
        ]
    )
    (skip_full,) = assemble(
        grid,
        way.core(),
        way.order,
        piece.shape,
        lambda *refs: rows_kernel(rows, columns, *refs),
        [4 * columns],
        rows,
        "join_skip",
    )
    return way, split_vectors(joint, [vector.shape[0] for vector in vectors]), skip_full


def join_mixed(grid, blocks, order, rows, columns, model):
    return assemble(
        grid,
        blocks,
        order,
        (rows, model),
        lambda *refs: mixed_kernel(columns, *refs),
        [model, 2 * model, model],
        rows,
        "join_mixed",
    )


def join_down(grid, blocks, order, rows, columns):
    packed = rows * columns // LANES
    (full,) = assemble(
        grid,
        blocks,
        order,
        (packed, LANES),
        lambda *refs: rows_kernel(rows, columns, *refs),
        [4 * columns],
        rows,
        "join_down",
    )
    return full.reshape(-1, 4 * columns, 4 * columns)


def add_low(mine, other):
    return (mine.astype(jnp.float32) + other.astype(jnp.float32)).astype(jnp.bfloat16)


class Scatter:
    def __init__(self, grid, keep, give, view):
        self.grid, self.mine, self.sent, self.view = grid, keep, give, view
        self.got = grid.send(give, "c")

    def push(self, axis, choose, turn=0):
        here = self.grid.at[axis]
        if turn:
            here = here // turn % 2
        self.mine, self.sent = choose(self.value, here), choose(self.value, 1 - here)
        self.got = self.grid.send(self.sent, axis, turn)

    def pull(self, *after):
        mine = tie(self.mine, *after) if after else self.mine
        self.value = add_low(mine, self.got)
        if self.view is not None:
            self.value, self.view = self.value.reshape(self.view), None
        return self.value


def fork(way, dim, align):
    whole = way.value.shape[dim]
    cut = -(-whole // (2 * align)) * align
    ways = []
    for start, stop in ((0, cut), (cut, whole)):
        branch = object.__new__(Scatter)
        branch.grid, branch.view = way.grid, None
        branch.value = lax.slice_in_dim(way.value, start, stop, axis=dim)
        ways.append(branch)
    return ways


def choose_dim(dim):
    return lambda value, at: lax.dynamic_index_in_dim(value, at, dim, keepdims=False)


def choose_half(value, at):
    half = value.shape[0] // 2
    return lax.dynamic_slice_in_dim(value, at * half, half, 0)


def choose_odd(value, at):
    pairs = value.reshape((2, 2) + value.shape[1:])
    return lax.dynamic_index_in_dim(pairs, at, 1, keepdims=False)


def choose_lanes(value, at):
    half = value.shape[-1] // 2
    return lax.dynamic_slice_in_dim(value, at * half, half, value.ndim - 1)


def choose_odd_lanes(value, at):
    part = value.shape[-1] // 4
    pieces = [
        lax.dynamic_slice_in_dim(value, (2 * k + at) * part, part, value.ndim - 1) for k in range(2)
    ]
    return jnp.concatenate(pieces, axis=-1)


def seq_scatter(value):
    value = lax.psum_scatter(value, "seq", scatter_dimension=1, tiled=True)
    return lax.psum_scatter(value, "batch", scatter_dimension=0, tiled=True).astype(jnp.float32)


def scatter_vectors(grid, vectors):
    joint = jnp.concatenate(vectors)
    if grid.square:
        joint = lax.all_gather(joint.reshape(-1, LANES), ("batch", "seq"))
    else:
        joint = lax.psum(joint, ("batch", "seq"))[None]
    return lambda *after: own_columns(grid, tie(joint, *after), vectors)


def own_columns(grid, joint, vectors):
    joint = jnp.sum(joint, axis=0).reshape(-1)
    result, start = [], 0
    for vector in vectors:
        width = vector.shape[0] // grid.seq_count
        result.append(lax.dynamic_slice_in_dim(joint, start + grid.seq_index * width, width))
        start += vector.shape[0]
    return result


class Items:
    def __init__(self, grid, segments, occupied, own_rows, all_rows):
        self.grid = grid
        self.segments, self.occupied = segments, occupied
        self.own_rows, self.all_rows = own_rows, all_rows
        self.halo_rows = all_rows - own_rows
        self.border = own_rows * (grid.seq_count // 2)
        tail = slice(self.border - self.halo_rows, self.border)
        self.moved = (segments[:, tail] == segments[:, self.border : self.border + 1]) & (
            occupied[:, tail] > 0
        )

    def of(self, seq_index):
        half = self.grid.seq_count // 2
        start = seq_index * self.own_rows
        rows = self.segments.shape[0]
        segment = lax.dynamic_slice(self.segments, (0, start), (rows, self.own_rows))
        used = lax.dynamic_slice(self.occupied, (0, start), (rows, self.own_rows)) > 0
        gone = jnp.pad(self.moved, ((0, 0), (self.own_rows - self.halo_rows, 0)))
        used = used & ~(gone & (seq_index == half - 1))
        halo_used = self.moved & (seq_index == half)
        halo_segment = self.segments[:, self.border - self.halo_rows : self.border]
        segment = jnp.concatenate([segment, halo_segment], axis=1)
        used = jnp.concatenate([used, halo_used], axis=1)
        alone = 1024 + seq_index * self.all_rows + jnp.arange(self.all_rows, dtype=jnp.int32)
        return jnp.where(used, segment, alone[None]), used


def far_gather(grid, value):
    rows, width, features = value.shape
    half = grid.seq_count // 2
    if half == 2:
        return [grid.send(value[row : row + 1], "x") for row in range(rows)]
    whole = lax.all_gather(value, "seq", axis=0)
    start = grid.seq_index // half * half
    whole = lax.dynamic_slice_in_dim(whole, start, half, 0)
    whole = whole.transpose(1, 0, 2, 3).reshape(rows, half * width, features)
    return [whole[row : row + 1] for row in range(rows)]


def far_ids(grid, items):
    half = grid.seq_count // 2
    if half == 2:
        return items.of(grid.seq_index ^ 1)[0]
    start = grid.seq_index // half * half
    ids = [
        jnp.where(start + part == grid.seq_index, -1, items.of(start + part)[0])
        for part in range(half)
    ]
    return jnp.concatenate(ids, axis=1)


def far_send(grid, value):
    half = grid.seq_count // 2
    if half == 2:
        return grid.send(value, "x")
    split = value.reshape(half, -1, value.shape[2])
    whole = jnp.zeros((grid.seq_count,) + split.shape[1:], jnp.bfloat16)
    start = grid.seq_index // half * half
    whole = lax.dynamic_update_slice_in_dim(whole, split, start, 0)
    return lax.psum_scatter(whole, "seq", scatter_dimension=0)[None]


def body(
    inputs,
    skip_inputs,
    out_cotangent,
    segments,
    occupied,
    skip_weight,
    skip_bias,
    first_gain,
    first_shift,
    qkv_weight,
    proj_weight,
    proj_bias,
    second_gain,
    second_shift,
    hidden_weight,
    hidden_bias,
    down_weight,
    down_bias,
):
    grid = Grid()
    own_rows, model = inputs.shape[1], inputs.shape[2]
    all_rows = -(-(own_rows + 16) // 32) * 32
    halo_rows = all_rows - own_rows
    half = grid.seq_count // 2
    vectors = [
        skip_bias,
        first_gain,
        first_shift,
        proj_bias,
        second_gain,
        second_shift,
        hidden_bias,
        down_bias,
    ]
    if grid.square:
        skip_way, vectors, skip_full = gather_skip(grid, skip_weight, vectors)
        mixed_piece = jnp.concatenate([qkv_weight, proj_weight], axis=1)
        mixed_way = Gather(grid, tie(mixed_piece, skip_way.column))
        mixed_way.first()
        mixed_way.second()
        mixed_way.last()
        mixed_way.spread()
        mixed_way.forward("y")
        for at in range(3):
            mixed_way.cross(at)
    else:
        vectors, wide = gather_plain(
            [skip_weight, qkv_weight, proj_weight, hidden_weight, down_weight], vectors
        )
        skip_full, qkv_full, proj_full, hidden_full, down_full = wide
        query_full, both_full = qkv_full[:, :model], qkv_full[:, model:]
        hidden_blocks = hidden_columns(hidden_full, model)
        down_blocks = down_full.reshape(-1, model, model)
    (
        skip_bias_full,
        gain_one,
        shift_one,
        proj_bias_full,
        gain_two,
        shift_two,
        hidden_bias_full,
        down_bias_full,
    ) = vectors
    joined_inputs = inputs
    if grid.square:
        joined_inputs = tie(inputs, skip_way.over_x, skip_way.over_y)
        segments = tie(segments, skip_way.over_x, skip_way.over_y)
    items = Items(grid, segments, occupied, own_rows, all_rows)
    query_ids, used = items.of(grid.seq_index)
    key_ids = jnp.concatenate([query_ids, far_ids(grid, items)], axis=1)
    tails = jnp.stack([v[:, own_rows - halo_rows :] for v in (inputs, skip_inputs, out_cotangent)])
    halo = grid.shift(tails, half - 1, half)
    first_tokens = jnp.concatenate([joined_inputs, halo[0]], axis=1)
    second_tokens = jnp.concatenate([skip_inputs, halo[1]], axis=1)
    query_ids, key_ids = query_ids[:, None, :], key_ids[:, :, None]
    used_rows = used.astype(jnp.float32).reshape(-1, 1)
    joined = jnp.concatenate([first_tokens, second_tokens], axis=2)
    joined, query_ids, key_ids, used_rows = lax.optimization_barrier(
        (joined, query_ids, key_ids, used_rows)
    )
    cotangent = jnp.concatenate([out_cotangent, halo[2]], axis=1)

    stream = dot_last(joined, skip_full) + skip_bias_full
    if grid.square:
        stream = tie(stream, mixed_way.crossed[0])
    first_low, first_normal, first_scale = layer_norm(stream, gain_one, shift_one)
    rows = inputs.shape[0]
    first_far = far_gather(grid, first_low)
    if grid.square:
        hidden_way = Gather(grid, tie(hidden_weight, stream))
        hidden_way.first()
        mixed_blocks = mixed_way.core(first_far[0], hidden_way.far)
        hidden_way.second(mixed_way.blocks[3])
        down_way = Gather(grid, tie(pack_lanes(down_weight), hidden_way.pair))
        down_way.first()
        query_full, both_full, proj_full = join_mixed(
            grid, mixed_blocks, mixed_way.order, *qkv_weight.shape, model
        )
        hidden_way.last(query_full)
        hidden_way.spread()
        down_way.second(query_full)
        both_full = tie(both_full, hidden_way.column, down_way.pair)
    own = dot_last(first_low, both_full).astype(jnp.bfloat16)
    if grid.square:
        query_full = tie(query_full, own, first_far[1])
    query = dot_last(first_low, query_full).astype(jnp.bfloat16)
    if grid.square:
        down_way.last(query)
        down_way.spread()
        hidden_way.cross(0)
        down_way.cross(0)
        first_far[0] = tie(first_far[0], query, down_way.column, *hidden_way.crossed)
    far, done = [], ()
    for row in range(rows):
        far.append(dot_last(first_far[row], both_full).astype(jnp.bfloat16))
        done = attend(query, own, far[row], query_ids, key_ids, row, *done)
        if row == 0 and grid.square:
            hidden_way.forward("y", done[0])
            down_way.forward("x", done[0])
            first_far[1] = tie(
                first_far[1],
                hidden_way.over_x,
                hidden_way.over_y,
                down_way.over_x,
                down_way.over_y,
                *down_way.crossed,
            )
            hidden_way.cross(1)
            hidden_way.cross(2)
    attended, level = done
    if grid.square:
        down_way.cross(1, attended, down_way.blocks[3])
        down_way.cross(2, attended, down_way.blocks[3])
        hidden_blocks = place_blocks(grid, hidden_way.core(attended), hidden_way.order)
        hidden_blocks = hidden_blocks.reshape(-1, model, model)
        down_blocks = join_down(grid, down_way.core(attended), down_way.order, *down_weight.shape)
    flat = (-1, model)
    (
        output,
        second_low,
        act_low,
        grad_pre,
        grad_middle,
        grad_proj,
        grad_attended,
        hidden_sums,
        middle_sums,
    ) = middle_block(
        stream.reshape(flat),
        attended.reshape(flat),
        cotangent.reshape(flat),
        used_rows,
        proj_full,
        hidden_blocks,
        down_blocks,
        proj_bias_full,
        gain_two,
        shift_two,
        hidden_bias_full,
        down_bias_full,
    )
    hidden_bias_grad = jnp.sum(hidden_sums, axis=0).reshape(-1)
    middle_sums = jnp.sum(middle_sums, axis=0)
    gain_two_grad, shift_two_grad = middle_sums[0], middle_sums[1]
    proj_bias_grad, down_bias_grad = middle_sums[2], middle_sums[3]
    grad_branch = jnp.where(used[..., None], cotangent, 0).reshape(flat)
    here, outer = grid.at["c"].astype(jnp.int32).reshape(1), grid.outer_count
    if grid.square:
        keep, give = tall_grad(act_low, grad_branch, here, outer, "down_weight_grad")
        down_way = Scatter(grid, keep, give, (outer, 2, 2) + keep.shape[2:])
        second_low = tie(second_low, give)
        keep, give = wide_grad(second_low, grad_pre, here, outer, "hidden_weight_grad")
        hidden_way = Scatter(grid, keep, give, (outer, -1, keep.shape[1]))
        down_way.pull(give)
        down_way.push("x", choose_dim(2))
        hidden_way.pull(down_way.sent)
        hidden_way.push("y", choose_lanes)
        grad_attended = tie(grad_attended, hidden_way.sent)
    else:
        down_grad = outer_dot(act_low, grad_branch)
        hidden_grad = outer_dot(second_low, grad_pre)
    output = output.reshape(stream.shape)
    grad_middle = grad_middle.reshape(stream.shape)
    grad_attended = grad_attended.reshape(stream.shape)

    grad_far, done = [], ()
    for row in range(rows):
        done = attend_back(
            query,
            own,
            far[row],
            attended,
            grad_attended,
            level,
            query_ids,
            key_ids,
            row,
            *done,
        )
        both_grad = done[1]
        if grid.square:
            down_way.pull(both_grad)
            hidden_way.pull(down_way.value)
            if row == 0:
                down_way.push("y", choose_dim(1))
                hidden_way.push("x", choose_lanes)
                both_grad = tie(both_grad, down_way.sent, hidden_way.sent)
            else:
                both_grad = tie(both_grad, down_way.value, hidden_way.value, *grad_far)
        share = dot_back(both_grad[row : row + 1, all_rows:], both_full).astype(jnp.bfloat16)
        grad_far.append(far_send(grid, share))
        done = (done[0], tie(both_grad, share))
    query_grad, both_grad = done
    both_flat = both_grad.reshape(-1, 2 * model)
    query_flat = query_grad.reshape(flat)
    if grid.square:
        keep, give = mixed_grad(
            first_low.reshape(flat),
            [value[0] for value in first_far],
            attended.reshape(flat),
            query_flat,
            both_flat,
            grad_proj,
            here,
            outer,
        )
        give = tie(give, *grad_far)
        mixed_way = Scatter(grid, keep, give, (outer, -1, keep.shape[1]))
        down_way.value = tie(down_way.value, give)
        hidden_way.value = tie(hidden_way.value, give)
        down_way.push("z", choose_half, 2)
        hidden_way.push("z", choose_odd, 1)
        query_grad = tie(query_grad, give, *grad_far)
        both_grad = tie(both_grad, give, *grad_far)
    else:
        first_all = [jnp.concatenate([first_low[row], first_far[row][0]]) for row in range(rows)]
        both_weight_grad = outer_dot(jnp.concatenate(first_all), both_flat)
        query_weight_grad = outer_dot(first_low.reshape(flat), query_flat)
        proj_grad = outer_dot(attended.reshape(flat), grad_proj)
    grad_first = dot_back(query_grad, query_full) + dot_back(both_grad[:, :all_rows], both_full)
    if grid.square:
        mixed_way.pull(grad_first)
        down_way.pull(mixed_way.value)
        down_way.push("z", choose_half, 1)
        hidden_way.pull(mixed_way.value)
        hidden_way.push("z", choose_half, 2)
        way_a, way_b = fork(mixed_way, 1, 8)
        way_a.push("y", choose_lanes)
        way_b.push("x", choose_odd_lanes)
        grad_first = tie(grad_first, way_a.sent, way_b.sent)
    grad_first = grad_first + jnp.concatenate(grad_far).astype(jnp.float32)
    grad_norm, gain_one_grad, shift_one_grad = layer_norm_back(
        grad_first, first_normal, first_scale, gain_one
    )
    grad_stream = (grad_middle + grad_norm).astype(jnp.bfloat16)
    skip_bias_grad = jnp.sum(grad_stream.astype(jnp.float32), axis=(0, 1))
    joined_flat, stream_flat = joined.reshape(-1, 2 * model), grad_stream.reshape(flat)
    if grid.square:
        keep, give = tall_grad(joined_flat, stream_flat, here, outer, "skip_weight_grad")
        skip_way = Scatter(grid, keep, give, (outer, 2, 2) + keep.shape[2:])
        grad_stream = tie(grad_stream, give)
    else:
        skip_weight_grad = outer_dot(joined_flat, stream_flat)
    vectors = scatter_vectors(
        grid,
        [
            skip_bias_grad,
            gain_one_grad,
            shift_one_grad,
            proj_bias_grad,
            gain_two_grad,
            shift_two_grad,
            hidden_bias_grad,
            down_bias_grad,
        ],
    )
    input_grad = dot_back(grad_stream, skip_full[:model])
    if grid.square:
        way_a.pull(input_grad)
        way_b.pull(input_grad)
        way_a.push("x", choose_lanes)
        way_b.push("y", choose_lanes)
        skip_way.pull(way_a.sent, way_b.sent)
        skip_a, skip_b = fork(skip_way, 3, 8)
        skip_a.push("x", choose_dim(2))
        skip_b.push("y", choose_dim(1))
        grad_stream = tie(grad_stream, skip_a.sent, skip_b.sent)
    skip_grad = dot_back(grad_stream, skip_full[model:])
    if grid.square:
        way_a.pull(skip_grad)
        way_b.pull(skip_grad)
        mixed_way.value = jnp.concatenate([way_a.value, way_b.value], axis=1)
        mixed_way.push("z", choose_half, 2)
        skip_a.pull(mixed_way.sent)
        skip_b.pull(mixed_way.sent)
        skip_a.push("y", choose_dim(1))
        skip_b.push("x", choose_dim(1))
        skip_a.pull()
        skip_b.pull()
        skip_way.value = jnp.concatenate([skip_a.value, skip_b.value], axis=1)
        skip_way.push("z", choose_odd, 1)
        mixed_way.pull(skip_way.sent)
        mixed_way.push("z", choose_half, 1)
        skip_way.pull(mixed_way.sent)
        skip_way.push("z", choose_half, 2)
        vectors = vectors(skip_way.sent)

        def tall_shard(way, shape):
            return unpack_lanes(wide_shard(way), *shape)

        def wide_shard(way):
            mine = tie(way.mine, skip_way.sent, mixed_way.sent)
            return (mine.astype(jnp.float32) + way.got.astype(jnp.float32))[0]

        down_shard = tall_shard(down_way, down_weight.shape)
        hidden_shard = wide_shard(hidden_way)
        skip_shard = tall_shard(skip_way, skip_weight.shape)
        mixed_shard = wide_shard(mixed_way)
        qkv_shard = mixed_shard[:, : qkv_weight.shape[1]]
        proj_shard = mixed_shard[:, qkv_weight.shape[1] :]
    else:
        down_shard = seq_scatter(down_grad)
        hidden_shard = seq_scatter(hidden_grad)
        skip_shard = seq_scatter(skip_weight_grad)
        proj_shard = seq_scatter(proj_grad)
        qkv_shard = seq_scatter(jnp.concatenate([query_weight_grad, both_weight_grad], axis=1))
        vectors = vectors()

    moved = items.moved[..., None] & (grid.seq_index == half - 1)
    results = [tie(output, skip_grad), input_grad, skip_grad]
    tails = jnp.stack([value[:, own_rows:].astype(jnp.float32) for value in results])
    tails = grid.shift(tails, half, half - 1)

    def settle(place):
        own = results[place][:, :own_rows]
        tail = own[:, own_rows - halo_rows :]
        tail = jnp.where(moved, tails[place].astype(own.dtype), tail)
        return lax.dynamic_update_slice_in_dim(own, tail, own_rows - halo_rows, 1)

    return (
        settle(0),
        settle(1),
        settle(2),
        skip_shard,
        vectors[0],
        vectors[1],
        vectors[2],
        qkv_shard,
        proj_shard,
        vectors[3],
        vectors[4],
        vectors[5],
        hidden_shard,
        vectors[6],
        down_shard,
        vectors[7],
    )


def solution(mesh):
    return jax.shard_map(
        body,
        mesh=mesh,
        in_specs=(
            P("batch", "seq", None),
            P("batch", "seq", None),
            P("batch", "seq", None),
            P("batch", None),
            P("batch", None),
            P("batch", "seq"),
            P("seq"),
            P("seq"),
            P("seq"),
            P("batch", "seq"),
            P("batch", "seq"),
            P("seq"),
            P("seq"),
            P("seq"),
            P("batch", "seq"),
            P("seq"),
            P("batch", "seq"),
            P("seq"),
        ),
        out_specs=(
            P("batch", "seq", None),
            P("batch", "seq", None),
            P("batch", "seq", None),
            P("batch", "seq"),
            P("seq"),
            P("seq"),
            P("seq"),
            P("batch", "seq"),
            P("batch", "seq"),
            P("seq"),
            P("seq"),
            P("seq"),
            P("batch", "seq"),
            P("seq"),
            P("batch", "seq"),
            P("seq"),
        ),
        check_vma=False,
    )
```

```python
import jax
import jax.numpy as jnp
from jax import lax
from jax.experimental import pallas as pl
from jax.experimental.pallas import tpu as pltpu
from jax.sharding import PartitionSpec as P

HEADS = 16
HEAD_DIM = 72
LANES = 128
epsilon = 1e-05
masked_score = -1e30
VMEM_BYTES = 60 * 1024 * 1024
FORWARD_HEADS, BACKWARD_HEADS = 1, 2
def nt_dot(left_side, right_side):
    return lax.dot_general(
        left_side, right_side, (((1,), (1,)), ((), ())), preferred_element_type=jnp.float32
    )


def tn_dot(left_side, right_side):
    return lax.dot_general(
        left_side, right_side, (((0,), (0,)), ((), ())), preferred_element_type=jnp.float32
    )


def nn_dot(left_side, right_side):
    return lax.dot_general(
        left_side, right_side, (((1,), (0,)), ((), ())), preferred_element_type=jnp.float32
    )


def split_heads(wide, head_ref, start=0):
    rows = wide.shape[0]
    pad = jnp.zeros((rows, LANES - HEAD_DIM), wide.dtype)
    for head in range(HEADS):
        piece = wide[:, head * HEAD_DIM : (head + 1) * HEAD_DIM]
        head_ref[head, start : start + rows] = jnp.concatenate([piece, pad], axis=1)


def split_keys(own_ref, far_ref, kh, vh):
    features = own_ref.shape[2] // 2
    start = 0
    for ref in (own_ref, far_ref):
        split_heads(ref[0, :, :features], kh, start)
        split_heads(ref[0, :, features:], vh, start)
        start += ref.shape[1]


def join_heads(head_ref):
    return jnp.concatenate([head_ref[head][:, :HEAD_DIM] for head in range(HEADS)], axis=1)


def chunk_of(rows, most=4):
    for count in (most, 2, 1):
        if rows % (count * 16) == 0:
            return rows // count
    return rows


def attend_kernel(
    q_ref, own_ref, far_ref, qid_ref, kid_ref, *refs
):
    out_ref, lse_ref, qh, kh, vh, score, prob = refs[-7:]
    split_heads(q_ref[0], qh)
    split_keys(own_ref, far_ref, kh, vh)
    key_rows = kh.shape[1]
    step = chunk_of(key_rows)
    scale = HEAD_DIM ** (-0.5)
    query_ids = qid_ref[0]

    def one_head(head, score, prob):
        query = qh[head]
        top = jnp.full((1, query.shape[0]), masked_score, jnp.float32)
        for start in range(0, key_rows, step):
            part = nt_dot(kh[head, start : start + step], query) * scale
            part = jnp.where(kid_ref[0, start : start + step] == query_ids, part, masked_score)
            score[start : start + step] = part
            top = jnp.maximum(top, jnp.max(part, axis=0, keepdims=True))
        total = jnp.zeros_like(top)
        for start in range(0, key_rows, step):
            part = jnp.exp(score[start : start + step] - top)
            total = total + jnp.sum(part, axis=0, keepdims=True)
            prob[start : start + step] = part.astype(jnp.bfloat16)
        mixed = tn_dot(vh[head], prob[...]) / total
        qh[head] = mixed.T.astype(jnp.bfloat16)
        lse_ref[0, pl.ds(head, 1)] = top + jnp.log(total)

    def some_heads(index, carry):
        for lane in range(FORWARD_HEADS):
            one_head(index * FORWARD_HEADS + lane, score.at[lane], prob.at[lane])
        return carry

    lax.fori_loop(0, HEADS // FORWARD_HEADS, some_heads, 0)
    out_ref[0] = join_heads(qh)


def attend(query, own, far, query_ids, key_ids, row, *old):
    rows, width, features = query.shape
    far_rows = far.shape[1]
    key_rows = width + far_rows
    here = lambda i: (row, 0, 0)
    only = lambda i: (0, 0, 0)
    wide = pl.BlockSpec((1, width, features), here)
    levels = pl.BlockSpec((1, HEADS, width), here)
    return pl.pallas_call(
        attend_kernel,
        grid=(1,),
        in_specs=[
            wide,
            pl.BlockSpec((1, width, 2 * features), here),
            pl.BlockSpec((1, far_rows, 2 * features), only),
            pl.BlockSpec((1, 1, width), here),
            pl.BlockSpec((1, key_rows, 1), here),
        ]
        + [pl.BlockSpec(memory_space=pl.ANY)] * len(old),
        out_specs=[wide, levels],
        out_shape=[
            jax.ShapeDtypeStruct((rows, width, features), jnp.bfloat16),
            jax.ShapeDtypeStruct((rows, HEADS, width), jnp.float32),
        ],
        scratch_shapes=[
            pltpu.VMEM((HEADS, width, LANES), jnp.bfloat16),
            pltpu.VMEM((HEADS, key_rows, LANES), jnp.bfloat16),
            pltpu.VMEM((HEADS, key_rows, LANES), jnp.bfloat16),
            pltpu.VMEM((FORWARD_HEADS, key_rows, width), jnp.float32),
            pltpu.VMEM((FORWARD_HEADS, key_rows, width), jnp.bfloat16),
        ],
        input_output_aliases={5: 0, 6: 1} if old else {},
        compiler_params=pltpu.CompilerParams(vmem_limit_bytes=VMEM_BYTES),
        cost_estimate=pl.CostEstimate(
            flops=4 * HEADS * width * key_rows * LANES,
            transcendentals=HEADS * width * key_rows,
            bytes_accessed=4 * features * (width + key_rows),
        ),
        name="attend",
    )(query, own, far, query_ids, key_ids, *old)


def attend_back_kernel(
    q_ref, own_ref, far_ref, o_ref, g_ref, lse_ref, qid_ref, kid_ref, *refs
):
    dq_ref, dkv_ref, qh, kh, vh, oh, gh, prob, slope = refs[-9:]
    split_heads(q_ref[0], qh)
    features = q_ref.shape[2]
    split_keys(own_ref, far_ref, kh, vh)
    split_heads(o_ref[0], oh)
    split_heads(g_ref[0], gh)
    key_rows = kh.shape[1]
    step = chunk_of(key_rows, 2)
    scale = HEAD_DIM ** (-0.5)
    query_ids = qid_ref[0]

    def one_head(head, prob, slope):
        query = qh[head]
        grad = gh[head]
        level = lse_ref[0, pl.ds(head, 1)]
        overlap = oh[head].astype(jnp.float32) * grad.astype(jnp.float32)
        row_dot = jnp.sum(overlap.T, axis=0, keepdims=True)
        for start in range(0, key_rows, step):
            part = nt_dot(kh[head, start : start + step], query) * scale
            part = jnp.where(kid_ref[0, start : start + step] == query_ids, part, masked_score)
            soft = jnp.exp(part - level)
            prob[start : start + step] = soft.astype(jnp.bfloat16)
            turn = nt_dot(vh[head, start : start + step], grad)
            slope[start : start + step] = (soft * (turn - row_dot)).astype(jnp.bfloat16)
        value_grad = nn_dot(prob[...], grad)
        query_grad = tn_dot(kh[head], slope[...]) * scale
        key_grad = nn_dot(slope[...], query) * scale
        vh[head] = value_grad.astype(jnp.bfloat16)
        kh[head] = key_grad.astype(jnp.bfloat16)
        qh[head] = query_grad.T.astype(jnp.bfloat16)

    def some_heads(index, carry):
        for lane in range(BACKWARD_HEADS):
            one_head(index * BACKWARD_HEADS + lane, prob.at[lane], slope.at[lane])
        return carry

    lax.fori_loop(0, HEADS // BACKWARD_HEADS, some_heads, 0)
    dq_ref[0] = join_heads(qh)
    dkv_ref[0, :, :features] = join_heads(kh)
    dkv_ref[0, :, features:] = join_heads(vh)


def attend_back(
    query, own, far, mixed, grad, level, query_ids, key_ids, row, *old
):
    rows, width, features = query.shape
    far_rows = far.shape[1]
    key_rows = width + far_rows
    here = lambda i: (row, 0, 0)
    only = lambda i: (0, 0, 0)
    wide = pl.BlockSpec((1, width, features), here, pipeline_mode=pl.Buffered(1))
    return pl.pallas_call(
        attend_back_kernel,
        grid=(1,),
        in_specs=[
            wide,
            pl.BlockSpec((1, width, 2 * features), here, pipeline_mode=pl.Buffered(1)),
            pl.BlockSpec((1, far_rows, 2 * features), only, pipeline_mode=pl.Buffered(1)),
            wide,
            wide,
            pl.BlockSpec((1, HEADS, width), here),
            pl.BlockSpec((1, 1, width), here),
            pl.BlockSpec((1, key_rows, 1), here),
        ]
        + [pl.BlockSpec(memory_space=pl.ANY)] * len(old),
        out_specs=[
            pl.BlockSpec((1, width, features), here),
            pl.BlockSpec((1, key_rows, 2 * features), here),
        ],
        out_shape=[
            jax.ShapeDtypeStruct((rows, width, features), jnp.bfloat16),
            jax.ShapeDtypeStruct((rows, key_rows, 2 * features), jnp.bfloat16),
        ],
        scratch_shapes=[
            pltpu.VMEM((HEADS, width, LANES), jnp.bfloat16),
            pltpu.VMEM((HEADS, key_rows, LANES), jnp.bfloat16),
            pltpu.VMEM((HEADS, key_rows, LANES), jnp.bfloat16),
            pltpu.VMEM((HEADS, width, LANES), jnp.bfloat16),
            pltpu.VMEM((HEADS, width, LANES), jnp.bfloat16),
            pltpu.VMEM((BACKWARD_HEADS, key_rows, width), jnp.bfloat16),
            pltpu.VMEM((BACKWARD_HEADS, key_rows, width), jnp.bfloat16),
        ],
        input_output_aliases={8: 0, 9: 1} if old else {},
        compiler_params=pltpu.CompilerParams(vmem_limit_bytes=VMEM_BYTES),
        cost_estimate=pl.CostEstimate(
            flops=10 * HEADS * width * key_rows * LANES,
            transcendentals=HEADS * width * key_rows,
            bytes_accessed=8 * features * (width + key_rows),
        ),
        name="attend_back",
    )(
        query,
        own,
        far,
        mixed,
        grad,
        level,
        query_ids,
        key_ids,
        *old,
    )


def split_rows(total_ref, here, outer, keep_ref, give_ref):
    inner = total_ref.shape[0] // (2 * outer)
    for group in range(outer):
        start = group * 2 * inner
        span = slice(group * inner, (group + 1) * inner)
        keep_ref[span] = total_ref[pl.ds(pl.multiple_of(start + here * inner, 16), inner)]
        give_ref[span] = total_ref[pl.ds(pl.multiple_of(start + (1 - here) * inner, 16), inner)]


def wide_grad_kernel(outer, here_ref, left_ref, right_ref, keep_ref, give_ref, total):
    total[...] = tn_dot(left_ref[...], right_ref[...]).astype(jnp.bfloat16)
    split_rows(total, here_ref[0], outer, keep_ref, give_ref)


def wide_grad(left, right, here, outer, name):
    tokens, rows = left.shape
    blocks = right.shape[1] // rows
    half = jax.ShapeDtypeStruct((rows // 2, right.shape[1]), jnp.bfloat16)
    spec = pl.BlockSpec((rows // 2, rows), lambda j, here: (0, j))
    return pl.pallas_call(
        lambda *refs: wide_grad_kernel(outer, *refs),
        grid_spec=pltpu.PrefetchScalarGridSpec(
            num_scalar_prefetch=1,
            grid=(blocks,),
            in_specs=[
                pl.BlockSpec((tokens, rows), lambda j, here: (0, 0)),
                pl.BlockSpec((tokens, rows), lambda j, here: (0, j)),
            ],
            out_specs=[spec, spec],
            scratch_shapes=[pltpu.VMEM((rows, rows), jnp.bfloat16)],
        ),
        out_shape=[half, half],
        compiler_params=pltpu.CompilerParams(vmem_limit_bytes=VMEM_BYTES),
        cost_estimate=pl.CostEstimate(
            flops=2 * tokens * rows * right.shape[1],
            transcendentals=0,
            bytes_accessed=2 * (tokens + right.shape[1]) * rows,
        ),
        name=name,
    )(here, left, right)


def tall_grad_kernel(groups, here_ref, left_ref, right_ref, keep_ref, give_ref, total):
    total[...] = tn_dot(left_ref[...], right_ref[...]).astype(jnp.bfloat16)
    here = here_ref[0]
    inner = total.shape[0] // (2 * groups)
    columns = total.shape[1] // 4
    for group in range(groups):
        start = group * 2 * inner
        for core, out_ref in ((here, keep_ref), (1 - here, give_ref)):
            rows = total[pl.ds(pl.multiple_of(start + core * inner, 16), inner)]
            for place in range(4):
                out_ref[group, place] = pack_lanes(rows[:, place * columns : (place + 1) * columns])


def tall_grad(left, right, here, outer, name):
    tokens, model = right.shape
    blocks = left.shape[1] // model
    groups = outer // blocks
    packed = left.shape[1] // (2 * outer) * (model // 4) // LANES
    half = jax.ShapeDtypeStruct((outer, 4, packed, LANES), jnp.bfloat16)
    spec = pl.BlockSpec((groups, 4, packed, LANES), lambda i, here: (i, 0, 0, 0))
    return pl.pallas_call(
        lambda *refs: tall_grad_kernel(groups, *refs),
        grid_spec=pltpu.PrefetchScalarGridSpec(
            num_scalar_prefetch=1,
            grid=(blocks,),
            in_specs=[
                pl.BlockSpec((tokens, model), lambda i, here: (0, i)),
                pl.BlockSpec((tokens, model), lambda i, here: (0, 0)),
            ],
            out_specs=[spec, spec],
            scratch_shapes=[pltpu.VMEM((model, model), jnp.bfloat16)],
        ),
        out_shape=[half, half],
        compiler_params=pltpu.CompilerParams(vmem_limit_bytes=VMEM_BYTES),
        cost_estimate=pl.CostEstimate(
            flops=2 * tokens * model * left.shape[1],
            transcendentals=0,
            bytes_accessed=2 * (tokens + model) * left.shape[1],
        ),
        name=name,
    )(here, left, right)


def mixed_grad_kernel(
    outer, here_ref, first_ref, far_a, far_b, att_ref, query_ref, both_ref, proj_ref,
    keep_ref, give_ref, total, sums,
):
    step = pl.program_id(0)
    width = far_a.shape[0]
    span = far_a.shape[0] + first_ref.shape[0] // 2
    own = first_ref.shape[0] // 2

    @pl.when(step == 0)
    def _():
        total[0] = tn_dot(first_ref[...], query_ref[...]).astype(jnp.bfloat16)

    @pl.when((step == 1) | (step == 2))
    def _():
        sums[...] = tn_dot(first_ref[0:own], both_ref[0:own])
        sums[...] += tn_dot(far_a[...], both_ref[own:span])
        sums[...] += tn_dot(first_ref[own:], both_ref[span : span + own])
        total[step] = (sums[...] + tn_dot(far_b[...], both_ref[span + own :])).astype(jnp.bfloat16)

    @pl.when(step == 3)
    def _():
        total[3] = tn_dot(att_ref[...], proj_ref[...]).astype(jnp.bfloat16)
        here = here_ref[0]
        model = total.shape[2]
        inner = model // (2 * outer)
        cut = model * 3 // 4
        for group in range(outer):
            rows = slice(group * inner, (group + 1) * inner)
            for core, out_ref in ((here, keep_ref), (1 - here, give_ref)):
                start = pl.multiple_of((group * 2 + core) * inner, 16)
                wide = jnp.concatenate([total[k, pl.ds(start, inner)] for k in range(3)], axis=1)
                last = total[3, pl.ds(start, inner)]
                for place in range(4):
                    out_ref[rows, place * model : (place + 1) * model] = jnp.concatenate(
                        [
                            wide[:, place * cut : (place + 1) * cut],
                            last[:, place * (model - cut) : (place + 1) * (model - cut)],
                        ],
                        axis=1,
                    )


def mixed_grad(first, far, attended, query_grad, both_grad, proj_grad, here, outer):
    tokens, model = first.shape
    half = jax.ShapeDtypeStruct((model // 2, 4 * model), jnp.bfloat16)
    fixed = lambda *shape: pl.BlockSpec(
        shape, lambda j, here: (0, 0), pipeline_mode=pl.Buffered(1)
    )
    return pl.pallas_call(
        lambda *refs: mixed_grad_kernel(outer, *refs),
        grid_spec=pltpu.PrefetchScalarGridSpec(
            num_scalar_prefetch=1,
            grid=(4,),
            in_specs=[
                fixed(tokens, model),
                fixed(*far[0].shape),
                fixed(*far[1].shape),
                fixed(tokens, model),
                fixed(tokens, model),
                pl.BlockSpec(
                    (both_grad.shape[0], model),
                    lambda j, here: (0, jnp.minimum(jnp.maximum(j - 1, 0), 1)),
                ),
                fixed(tokens, model),
            ],
            out_specs=[fixed(model // 2, 4 * model), fixed(model // 2, 4 * model)],
            scratch_shapes=[
                pltpu.VMEM((4, model, model), jnp.bfloat16),
                pltpu.VMEM((model, model), jnp.float32),
            ],
        ),
        out_shape=[half, half],
        compiler_params=pltpu.CompilerParams(vmem_limit_bytes=VMEM_BYTES),
        cost_estimate=pl.CostEstimate(
            flops=2 * model * model * (2 * tokens + 2 * both_grad.shape[0]),
            transcendentals=0,
            bytes_accessed=2 * model * (6 * tokens + 2 * both_grad.shape[0] + 4 * model),
        ),
        name="mixed_weight_grad",
    )(here, first, far[0], far[1], attended, query_grad, both_grad, proj_grad)


def column_chunks(width):
    cut = width // 256 // 2 * 256
    return ((0, cut), (cut, width)) if cut else ((0, width),)


def middle_kernel(
    stream_ref, att_ref, cot_ref, used_ref, proj_ref, hidden_ref, down_ref,
    proj_bias_ref, gain_ref, shift_ref, hidden_bias_ref, down_bias_ref,
    out_ref, second_ref, act_ref, pre_ref, middle_grad_ref, proj_grad_ref, att_grad_ref,
    hidden_sum_ref, sums_ref,
    low, normal, scale, branch, total, back,
):
    step = pl.program_id(1)
    steps = pl.num_programs(1)

    @pl.when(step == 0)
    def _():
        middle = stream_ref[...] + nn_dot(att_ref[...], proj_ref[...]) + proj_bias_ref[...]
        centred = middle - jnp.mean(middle, axis=-1, keepdims=True)
        inverse = lax.rsqrt(jnp.mean(centred * centred, axis=-1, keepdims=True) + epsilon)
        unit = centred * inverse
        normal[...] = unit
        scale[...] = inverse
        second = (unit * gain_ref[...] + shift_ref[...]).astype(jnp.bfloat16)
        low[...] = second
        second_ref[...] = second
        branch[...] = (cot_ref[...].astype(jnp.float32) * used_ref[...]).astype(jnp.bfloat16)
        total[...] = middle + down_bias_ref[...]
        back[...] = jnp.zeros_like(back)

    for start, stop in column_chunks(hidden_ref.shape[2]):
        pre_act = nn_dot(low[...], hidden_ref[0, :, start:stop]) + hidden_bias_ref[0, :, start:stop]
        grad_act = nt_dot(branch[...], down_ref[0, start:stop])
        below = 0.5 + 0.5 * lax.erf(pre_act * (0.5**0.5))
        density = jnp.exp(-0.5 * pre_act * pre_act) * ((2.0 * jnp.pi) ** -0.5)
        act = (pre_act * below).astype(jnp.bfloat16)
        grad_pre = (grad_act * (below + pre_act * density)).astype(jnp.bfloat16)
        act_ref[:, start:stop] = act
        pre_ref[:, start:stop] = grad_pre
        hidden_sum_ref[0, 0, :, start:stop] = jnp.sum(
            grad_pre.astype(jnp.float32), axis=0, keepdims=True
        )
        total[...] += nn_dot(act, down_ref[0, start:stop])
        back[...] += nt_dot(grad_pre, hidden_ref[0, :, start:stop])

    @pl.when(step == steps - 1)
    def _():
        out_ref[...] = total[...].astype(jnp.bfloat16)
        grad = back[...]
        unit = normal[...]
        part = grad * gain_ref[...]
        mean_part = jnp.mean(part, axis=-1, keepdims=True)
        mean_both = jnp.mean(part * unit, axis=-1, keepdims=True)
        grad_out = cot_ref[...].astype(jnp.float32) * used_ref[...]
        grad_middle = grad_out + (part - mean_part - unit * mean_both) * scale[...]
        middle_grad_ref[...] = grad_middle
        grad_low = grad_middle.astype(jnp.bfloat16)
        proj_grad_ref[...] = grad_low
        att_grad_ref[...] = nt_dot(grad_low, proj_ref[...]).astype(jnp.bfloat16)
        sums_ref[0, 0:1] = jnp.sum(grad * unit, axis=0, keepdims=True)
        sums_ref[0, 1:2] = jnp.sum(grad, axis=0, keepdims=True)
        sums_ref[0, 2:3] = jnp.sum(grad_low.astype(jnp.float32), axis=0, keepdims=True)
        sums_ref[0, 3:4] = jnp.sum(grad_out, axis=0, keepdims=True)


def token_block(tokens):
    return tokens // 4 if tokens % 64 == 0 else tokens


def middle_block(
    stream, attended, cotangent, used, proj, hidden, down, proj_bias, gain, shift, hidden_bias,
    down_bias,
):
    tokens, model = stream.shape
    steps = hidden.shape[0]
    rows = token_block(tokens)
    blocks = tokens // rows
    by_rows = pl.BlockSpec((rows, model), lambda i, s: (i, 0))
    by_step = pl.BlockSpec((rows, model), lambda i, s: (i, s))
    vector = pl.BlockSpec((1, model), lambda i, s: (0, 0))
    low_rows = jax.ShapeDtypeStruct((tokens, model), jnp.bfloat16)
    low_steps = jax.ShapeDtypeStruct((tokens, steps * model), jnp.bfloat16)
    flops = 2 * tokens * model * model * (4 * steps + 2)
    return pl.pallas_call(
        middle_kernel,
        grid=(blocks, steps),
        in_specs=[
            by_rows,
            by_rows,
            by_rows,
            pl.BlockSpec((rows, 1), lambda i, s: (i, 0)),
            pl.BlockSpec((model, model), lambda i, s: (0, 0), pipeline_mode=pl.Buffered(1)),
            pl.BlockSpec((1, model, model), lambda i, s: (s, 0, 0)),
            pl.BlockSpec((1, model, model), lambda i, s: (s, 0, 0)),
            vector,
            vector,
            vector,
            pl.BlockSpec((1, 1, model), lambda i, s: (s, 0, 0)),
            vector,
        ],
        out_specs=[
            by_rows,
            by_rows,
            by_step,
            by_step,
            by_rows,
            by_rows,
            by_rows,
            pl.BlockSpec((1, 1, 1, model), lambda i, s: (i, s, 0, 0)),
            pl.BlockSpec((1, 4, model), lambda i, s: (i, 0, 0)),
        ],
        out_shape=[
            low_rows,
            low_rows,
            low_steps,
            low_steps,
            jax.ShapeDtypeStruct((tokens, model), jnp.float32),
            low_rows,
            low_rows,
            jax.ShapeDtypeStruct((blocks, steps, 1, model), jnp.float32),
            jax.ShapeDtypeStruct((blocks, 4, model), jnp.float32),
        ],
        scratch_shapes=[
            pltpu.VMEM((rows, model), jnp.bfloat16),
            pltpu.VMEM((rows, model), jnp.float32),
            pltpu.VMEM((rows, 1), jnp.float32),
            pltpu.VMEM((rows, model), jnp.bfloat16),
            pltpu.VMEM((rows, model), jnp.float32),
            pltpu.VMEM((rows, model), jnp.float32),
        ],
        compiler_params=pltpu.CompilerParams(vmem_limit_bytes=VMEM_BYTES),
        cost_estimate=pl.CostEstimate(
            flops=flops,
            transcendentals=2 * tokens * model * steps,
            bytes_accessed=2 * tokens * model * (2 * steps + 12) + 4 * model * model * steps * blocks,
        ),
        name="middle_block",
    )(
        stream,
        attended,
        cotangent,
        used,
        proj,
        hidden,
        down,
        proj_bias[None],
        gain[None],
        shift[None],
        hidden_bias.reshape(steps, 1, model),
        down_bias[None],
    )


def layer_norm(stream, norm_gain, norm_shift):
    centred = stream - jnp.mean(stream, axis=-1, keepdims=True)
    scale = lax.rsqrt(jnp.mean(centred * centred, axis=-1, keepdims=True) + epsilon)
    normal = centred * scale
    return (normal * norm_gain + norm_shift).astype(jnp.bfloat16), normal, scale


def layer_norm_back(grad, normal, scale, norm_gain):
    part = grad * norm_gain
    mean_part = jnp.mean(part, axis=-1, keepdims=True)
    mean_both = jnp.mean(part * normal, axis=-1, keepdims=True)
    gain_grad = jnp.sum(grad * normal, axis=(0, 1))
    shift_grad = jnp.sum(grad, axis=(0, 1))
    return (part - mean_part - normal * mean_both) * scale, gain_grad, shift_grad


def outer_dot(left_side, right_side):
    return lax.dot_general(
        left_side, right_side, (((0,), (0,)), ((), ())), preferred_element_type=jnp.bfloat16
    )


def dot_last(left_side, right_side):
    return lax.dot_general(
        left_side, right_side, (((2,), (0,)), ((), ())), preferred_element_type=jnp.float32
    )


def dot_back(left_side, right_side):
    return lax.dot_general(
        left_side, right_side, (((2,), (1,)), ((), ())), preferred_element_type=jnp.float32
    )


def dot_tokens(left_side, right_side):
    return lax.dot_general(
        left_side, right_side, (((0, 1), (0, 1)), ((), ())), preferred_element_type=jnp.bfloat16
    )


class Grid:
    def __init__(self):
        self.batch_count = lax.axis_size("batch")
        self.seq_count = lax.axis_size("seq")
        self.seq_index = lax.axis_index("seq")
        batch_index = lax.axis_index("batch")
        self.outer_count = self.batch_count // 2
        self.square = self.seq_count == 4 and self.outer_count == 4
        self.at = {
            "z": batch_index // 2,
            "c": batch_index % 2,
            "y": self.seq_index // 2,
            "x": self.seq_index % 2,
        }

    def index(self, z, c, s):
        return (z * 2 + c) * self.seq_count + s

    def send(self, value, axis, turn=0):
        pairs = []
        for z in range(self.outer_count):
            for c in range(2):
                for s in range(self.seq_count):
                    far_z, far_c, far_s = z, c, s
                    if axis == "z":
                        far_z = z ^ turn
                    elif axis == "c":
                        far_c = 1 - c
                    elif axis == "y":
                        far_s = s ^ 2
                    else:
                        far_s = s ^ 1
                    pairs.append((self.index(z, c, s), self.index(far_z, far_c, far_s)))
        return lax.ppermute(value, ("batch", "seq"), pairs)

    def shift(self, value, source, target):
        pairs = [
            (b * self.seq_count + source, b * self.seq_count + target)
            for b in range(self.batch_count)
        ]
        return lax.ppermute(value, ("batch", "seq"), pairs)


def tie(value, *others):
    return lax.optimization_barrier((value, *others))[0]


def square_gather(grid, shard):
    over_x = grid.send(shard, "x")
    found = jnp.stack([shard, over_x, grid.send(shard, "y"), grid.send(over_x, "y")])
    return jnp.stack(
        [
            lax.dynamic_index_in_dim(found, grid.seq_index ^ place, 0, keepdims=False)
            for place in range(4)
        ]
    )


def pack_lanes(shard):
    rows, columns = shard.shape
    whole = columns // LANES
    rest = columns - whole * LANES
    pieces = [shard[:, k * LANES : (k + 1) * LANES] for k in range(whole)]
    if rest:
        fold = LANES // rest
        step = rows // fold
        last = [shard[k * step : (k + 1) * step, whole * LANES :] for k in range(fold)]
        pieces.append(jnp.concatenate(last, axis=1))
    return jnp.concatenate(pieces, axis=0)


def unpack_lanes(packed, rows, columns):
    whole = columns // LANES
    rest = columns - whole * LANES
    pieces = [packed[k * rows : (k + 1) * rows] for k in range(whole)]
    if rest:
        fold = LANES // rest
        last = packed[whole * rows : whole * rows + rows // fold]
        pieces.append(
            jnp.concatenate([last[:, k * rest : (k + 1) * rest] for k in range(fold)], axis=0)
        )
    return jnp.concatenate(pieces, axis=1)


def rows_kernel(rows, columns, turn_ref, to_ref, *refs):
    blocks, out_ref, found = refs[:8], refs[8], refs[9]
    for block in range(8):
        found[to_ref[block]] = blocks[block][...]
    for core in range(2):
        wide = [unpack_lanes(found[core * 4 + place], rows, columns) for place in range(4)]
        out_ref[core * rows : (core + 1) * rows] = jnp.concatenate(wide, axis=1)


def mixed_kernel(columns, turn_ref, to_ref, *refs):
    blocks, query_ref, both_ref, proj_ref, found = refs[:8], refs[8], refs[9], refs[10], refs[11]
    rows, model = found.shape[1:]
    for block in range(8):
        found[to_ref[block]] = blocks[block][...]
    for core in range(2):
        span = slice(core * rows, (core + 1) * rows)
        parts = [found[core * 4 + place] for place in range(4)]
        wide = jnp.concatenate([part[:, :columns] for part in parts], axis=1)
        query_ref[span] = wide[:, :model]
        both_ref[span] = wide[:, model:]
        proj_ref[span] = jnp.concatenate([part[:, columns:] for part in parts], axis=1)


def swap_bits(value):
    return ((value & 1) << 1) | (value >> 1)


def assemble(grid, blocks, order, piece, kernel, widths, rows, name):
    outer = grid.outer_count
    turns = grid.at["z"] ^ jnp.arange(4, dtype=jnp.int32)
    if order[1] == 2:
        turns = swap_bits(turns)
    block = jnp.arange(8, dtype=jnp.int32)
    places = (grid.at["c"] ^ (block >> 2)) * 4 + (grid.seq_index ^ (block & 3))
    shapes = [jax.ShapeDtypeStruct((outer * 2 * rows, w), jnp.bfloat16) for w in widths]
    return pl.pallas_call(
        kernel,
        grid_spec=pltpu.PrefetchScalarGridSpec(
            num_scalar_prefetch=2,
            grid=(outer,),
            in_specs=[pl.BlockSpec(piece, lambda z, turn, to: (turn[z], 0))] * 8,
            out_specs=[pl.BlockSpec((2 * rows, w), lambda z, turn, to: (z, 0)) for w in widths],
            scratch_shapes=[pltpu.VMEM((8,) + piece, jnp.bfloat16)],
        ),
        out_shape=shapes,
        compiler_params=pltpu.CompilerParams(vmem_limit_bytes=VMEM_BYTES),
        cost_estimate=pl.CostEstimate(
            flops=0,
            transcendentals=0,
            bytes_accessed=8 * outer * rows * sum(widths),
        ),
        name=name,
    )(turns, places, *blocks)


def place_kernel(block_count, outer_count, to_ref, *refs):
    blocks, out_ref, sems = refs[:block_count], refs[block_count], refs[block_count + 1]
    rows = out_ref.shape[1]
    copies = []
    for block in range(block_count):
        for turn in range(outer_count):
            slot = block * outer_count + turn
            copies.append(
                pltpu.make_async_copy(
                    blocks[block].at[pl.ds(turn * rows, rows)], out_ref.at[to_ref[slot]], sems.at[slot]
                )
            )
    for copy in copies:
        copy.start()
    for copy in copies:
        copy.wait()


def place_blocks(grid, blocks, order):
    outer = grid.outer_count
    rows, columns = blocks[0].shape[0] // outer, blocks[0].shape[1]
    spot = jnp.arange(8 * outer, dtype=jnp.int32)
    core, place = grid.at["c"] ^ (spot >> 4), grid.seq_index ^ (spot >> 2 & 3)
    turn = spot & 3
    if order[1] == 2:
        turn = swap_bits(turn)
    slots = (place * outer + (grid.at["z"] ^ turn)) * 2 + core
    count = 8 * outer
    return pl.pallas_call(
        lambda *refs: place_kernel(8, outer, *refs),
        grid_spec=pltpu.PrefetchScalarGridSpec(
            num_scalar_prefetch=1,
            grid=(1,),
            in_specs=[pl.BlockSpec(memory_space=pl.ANY)] * 8,
            out_specs=pl.BlockSpec((count, rows, columns), lambda i, to: (0, 0, 0)),
            scratch_shapes=[pltpu.SemaphoreType.DMA((count,))],
        ),
        compiler_params=pltpu.CompilerParams(vmem_limit_bytes=VMEM_BYTES),
        out_shape=jax.ShapeDtypeStruct((count, rows, columns), blocks[0].dtype),
        cost_estimate=pl.CostEstimate(
            flops=0, transcendentals=0, bytes_accessed=4 * count * rows * columns
        ),
        name="place_blocks",
    )(slots, *blocks)


class Gather:
    def __init__(self, grid, piece):
        self.grid, self.piece, self.crossed = grid, piece, []

    def direct(self, *extra):
        self.order = [0, 1, 2, 3]
        parts = [self.piece] + [self.grid.send(self.piece, "z", turn) for turn in (1, 2, 3)]
        self.column = jnp.concatenate(parts + list(extra), axis=0)

    def first(self):
        self.order = [0, 2, 1, 3]
        self.far = self.grid.send(self.piece, "z", 2)

    def second(self, *after):
        piece = tie(self.piece, *after) if after else self.piece
        self.pair = jnp.concatenate([piece, self.far], axis=0)
        self.far = self.grid.send(self.pair, "z", 1)

    def last(self, *after):
        pair = tie(self.pair, *after) if after else self.pair
        self.column = jnp.concatenate([pair, self.far], axis=0)

    def spread(self):
        self.over_x = self.grid.send(self.column, "x")
        self.over_y = self.grid.send(self.column, "y")

    def forward(self, axis, *after):
        value = self.over_x if axis == "y" else self.over_y
        if after:
            value = tie(value, *after)
            if axis == "y":
                self.over_x = value
            else:
                self.over_y = value
        self.blocks = [self.column, self.over_x, self.over_y, self.grid.send(value, axis)]

    def cross(self, at, *after):
        block = (self.column, self.over_x, self.over_y)[at]
        block = tie(block, *after) if after else block
        self.crossed.append(self.grid.send(block, "c"))

    def core(self, *after):
        block = tie(self.blocks[3], *self.crossed[1:], *after)
        return self.blocks + self.crossed + [self.grid.send(block, "c")]


def split_vectors(joint, widths):
    result, start = [], 0
    for width in widths:
        result.append(joint[:, start : start + width].reshape(-1).astype(jnp.float32))
        start += width
    return result


def gather_plain(matrices, vectors):
    joint = lax.all_gather(jnp.concatenate(vectors), "seq", axis=0)
    wide = [
        lax.all_gather(
            lax.all_gather(shard, "batch", axis=0, tiled=True), "seq", axis=1, tiled=True
        )
        for shard in matrices
    ]
    return split_vectors(joint, [vector.shape[0] for vector in vectors]), wide


def hidden_columns(hidden_full, model):
    return jnp.stack(jnp.split(hidden_full, hidden_full.shape[1] // model, axis=1))


def gather_skip(grid, skip_weight, vectors):
    joint = jnp.concatenate(vectors)
    short = -joint.shape[0] % (8 * LANES)
    extra = jnp.pad(joint, (0, short)).reshape(-1, LANES)
    rows, columns = skip_weight.shape
    piece = pack_lanes(skip_weight)
    way = Gather(grid, piece)
    way.direct(extra)
    way.spread()
    way.forward("y")
    for at in range(3):
        way.cross(at)
    found = jnp.stack([block[-extra.shape[0] :].reshape(-1) for block in way.blocks])
    joint = jnp.stack(
        [
            lax.dynamic_index_in_dim(found, grid.seq_index ^ place, 0, keepdims=False)
            for place in range(4)
        ]
    )
    (skip_full,) = assemble(
        grid,
        way.core(),
        way.order,
        piece.shape,
        lambda *refs: rows_kernel(rows, columns, *refs),
        [4 * columns],
        rows,
        "join_skip",
    )
    return way, split_vectors(joint, [vector.shape[0] for vector in vectors]), skip_full


def join_mixed(grid, blocks, order, rows, columns, model):
    return assemble(
        grid,
        blocks,
        order,
        (rows, model),
        lambda *refs: mixed_kernel(columns, *refs),
        [model, 2 * model, model],
        rows,
        "join_mixed",
    )


def join_down(grid, blocks, order, rows, columns):
    packed = rows * columns // LANES
    (full,) = assemble(
        grid,
        blocks,
        order,
        (packed, LANES),
        lambda *refs: rows_kernel(rows, columns, *refs),
        [4 * columns],
        rows,
        "join_down",
    )
    return full.reshape(-1, 4 * columns, 4 * columns)


def add_low(mine, other):
    return (mine.astype(jnp.float32) + other.astype(jnp.float32)).astype(jnp.bfloat16)


class Scatter:
    def __init__(self, grid, keep, give, view):
        self.grid, self.mine, self.sent, self.view = grid, keep, give, view
        self.got = grid.send(give, "c")

    def push(self, axis, choose, turn=0):
        here = self.grid.at[axis]
        if turn:
            here = here // turn % 2
        self.mine, self.sent = choose(self.value, here), choose(self.value, 1 - here)
        self.got = self.grid.send(self.sent, axis, turn)

    def pull(self, *after):
        mine = tie(self.mine, *after) if after else self.mine
        self.value = add_low(mine, self.got)
        if self.view is not None:
            self.value, self.view = self.value.reshape(self.view), None
        return self.value


def fork(way, dim, align):
    whole = way.value.shape[dim]
    cut = -(-whole // (2 * align)) * align
    ways = []
    for start, stop in ((0, cut), (cut, whole)):
        branch = object.__new__(Scatter)
        branch.grid, branch.view = way.grid, None
        branch.value = lax.slice_in_dim(way.value, start, stop, axis=dim)
        ways.append(branch)
    return ways


def choose_dim(dim):
    return lambda value, at: lax.dynamic_index_in_dim(value, at, dim, keepdims=False)


def choose_half(value, at):
    half = value.shape[0] // 2
    return lax.dynamic_slice_in_dim(value, at * half, half, 0)


def choose_odd(value, at):
    pairs = value.reshape((2, 2) + value.shape[1:])
    return lax.dynamic_index_in_dim(pairs, at, 1, keepdims=False)


def choose_lanes(value, at):
    half = value.shape[-1] // 2
    return lax.dynamic_slice_in_dim(value, at * half, half, value.ndim - 1)


def choose_odd_lanes(value, at):
    part = value.shape[-1] // 4
    pieces = [
        lax.dynamic_slice_in_dim(value, (2 * k + at) * part, part, value.ndim - 1) for k in range(2)
    ]
    return jnp.concatenate(pieces, axis=-1)


def seq_scatter(value):
    value = lax.psum_scatter(value, "seq", scatter_dimension=1, tiled=True)
    return lax.psum_scatter(value, "batch", scatter_dimension=0, tiled=True).astype(jnp.float32)


def scatter_vectors(grid, vectors):
    joint = jnp.concatenate(vectors)
    if grid.square:
        joint = lax.all_gather(joint.reshape(-1, LANES), ("batch", "seq"))
    else:
        joint = lax.psum(joint, ("batch", "seq"))[None]
    return lambda *after: own_columns(grid, tie(joint, *after), vectors)


def own_columns(grid, joint, vectors):
    joint = jnp.sum(joint, axis=0).reshape(-1)
    result, start = [], 0
    for vector in vectors:
        width = vector.shape[0] // grid.seq_count
        result.append(lax.dynamic_slice_in_dim(joint, start + grid.seq_index * width, width))
        start += vector.shape[0]
    return result


class Items:
    def __init__(self, grid, segments, occupied, own_rows, all_rows):
        self.grid = grid
        self.segments, self.occupied = segments, occupied
        self.own_rows, self.all_rows = own_rows, all_rows
        self.halo_rows = all_rows - own_rows
        self.border = own_rows * (grid.seq_count // 2)
        tail = slice(self.border - self.halo_rows, self.border)
        self.moved = (segments[:, tail] == segments[:, self.border : self.border + 1]) & (
            occupied[:, tail] > 0
        )

    def of(self, seq_index):
        half = self.grid.seq_count // 2
        start = seq_index * self.own_rows
        rows = self.segments.shape[0]
        segment = lax.dynamic_slice(self.segments, (0, start), (rows, self.own_rows))
        used = lax.dynamic_slice(self.occupied, (0, start), (rows, self.own_rows)) > 0
        gone = jnp.pad(self.moved, ((0, 0), (self.own_rows - self.halo_rows, 0)))
        used = used & ~(gone & (seq_index == half - 1))
        halo_used = self.moved & (seq_index == half)
        halo_segment = self.segments[:, self.border - self.halo_rows : self.border]
        segment = jnp.concatenate([segment, halo_segment], axis=1)
        used = jnp.concatenate([used, halo_used], axis=1)
        alone = 1024 + seq_index * self.all_rows + jnp.arange(self.all_rows, dtype=jnp.int32)
        return jnp.where(used, segment, alone[None]), used


def far_gather(grid, value):
    rows, width, features = value.shape
    half = grid.seq_count // 2
    if half == 2:
        return [grid.send(value[row : row + 1], "x") for row in range(rows)]
    whole = lax.all_gather(value, "seq", axis=0)
    start = grid.seq_index // half * half
    whole = lax.dynamic_slice_in_dim(whole, start, half, 0)
    whole = whole.transpose(1, 0, 2, 3).reshape(rows, half * width, features)
    return [whole[row : row + 1] for row in range(rows)]


def far_ids(grid, items):
    half = grid.seq_count // 2
    if half == 2:
        return items.of(grid.seq_index ^ 1)[0]
    start = grid.seq_index // half * half
    ids = [
        jnp.where(start + part == grid.seq_index, -1, items.of(start + part)[0])
        for part in range(half)
    ]
    return jnp.concatenate(ids, axis=1)


def far_send(grid, value):
    half = grid.seq_count // 2
    if half == 2:
        return grid.send(value, "x")
    split = value.reshape(half, -1, value.shape[2])
    whole = jnp.zeros((grid.seq_count,) + split.shape[1:], jnp.bfloat16)
    start = grid.seq_index // half * half
    whole = lax.dynamic_update_slice_in_dim(whole, split, start, 0)
    return lax.psum_scatter(whole, "seq", scatter_dimension=0)[None]


def body(
    inputs,
    skip_inputs,
    out_cotangent,
    segments,
    occupied,
    skip_weight,
    skip_bias,
    first_gain,
    first_shift,
    qkv_weight,
    proj_weight,
    proj_bias,
    second_gain,
    second_shift,
    hidden_weight,
    hidden_bias,
    down_weight,
    down_bias,
):
    grid = Grid()
    own_rows, model = inputs.shape[1], inputs.shape[2]
    all_rows = -(-(own_rows + 16) // 32) * 32
    halo_rows = all_rows - own_rows
    half = grid.seq_count // 2
    vectors = [
        skip_bias,
        first_gain,
        first_shift,
        proj_bias,
        second_gain,
        second_shift,
        hidden_bias,
        down_bias,
    ]
    if grid.square:
        skip_way, vectors, skip_full = gather_skip(grid, skip_weight, vectors)
        mixed_piece = jnp.concatenate([qkv_weight, proj_weight], axis=1)
        mixed_way = Gather(grid, tie(mixed_piece, skip_way.column))
        mixed_way.first()
        mixed_way.second(skip_way.over_x, skip_way.over_y)
        mixed_way.last()
        mixed_way.spread()
        mixed_way.forward("y")
        for at in range(3):
            mixed_way.cross(at)
    else:
        vectors, wide = gather_plain(
            [skip_weight, qkv_weight, proj_weight, hidden_weight, down_weight], vectors
        )
        skip_full, qkv_full, proj_full, hidden_full, down_full = wide
        query_full, both_full = qkv_full[:, :model], qkv_full[:, model:]
        hidden_blocks = hidden_columns(hidden_full, model)
        down_blocks = down_full.reshape(-1, model, model)
    (
        skip_bias_full,
        gain_one,
        shift_one,
        proj_bias_full,
        gain_two,
        shift_two,
        hidden_bias_full,
        down_bias_full,
    ) = vectors
    joined_inputs = inputs
    if grid.square:
        joined_inputs = tie(inputs, skip_way.column)
        segments = tie(segments, skip_way.column)
    items = Items(grid, segments, occupied, own_rows, all_rows)
    query_ids, used = items.of(grid.seq_index)
    key_ids = jnp.concatenate([query_ids, far_ids(grid, items)], axis=1)
    tails = jnp.stack([v[:, own_rows - halo_rows :] for v in (inputs, skip_inputs, out_cotangent)])
    halo = grid.shift(tails, half - 1, half)
    first_tokens = jnp.concatenate([joined_inputs, halo[0]], axis=1)
    second_tokens = jnp.concatenate([skip_inputs, halo[1]], axis=1)
    query_ids, key_ids = query_ids[:, None, :], key_ids[:, :, None]
    used_rows = used.astype(jnp.float32).reshape(-1, 1)
    joined = jnp.concatenate([first_tokens, second_tokens], axis=2)
    joined, query_ids, key_ids, used_rows = lax.optimization_barrier(
        (joined, query_ids, key_ids, used_rows)
    )
    cotangent = jnp.concatenate([out_cotangent, halo[2]], axis=1)

    stream = dot_last(joined, skip_full) + skip_bias_full
    if grid.square:
        stream = tie(stream, mixed_way.crossed[0])
    first_low, first_normal, first_scale = layer_norm(stream, gain_one, shift_one)
    rows = inputs.shape[0]
    first_far = far_gather(grid, first_low)
    if grid.square:
        hidden_way = Gather(grid, tie(hidden_weight, stream))
        hidden_way.first()
        mixed_blocks = mixed_way.core(first_far[0], hidden_way.far)
        hidden_way.second(mixed_way.blocks[3])
        down_way = Gather(grid, tie(pack_lanes(down_weight), hidden_way.pair))
        down_way.first()
        query_full, both_full, proj_full = join_mixed(
            grid, mixed_blocks, mixed_way.order, *qkv_weight.shape, model
        )
        hidden_way.last(query_full)
        hidden_way.spread()
        down_way.second(query_full)
        both_full = tie(both_full, hidden_way.column, down_way.pair)
    own = dot_last(first_low, both_full).astype(jnp.bfloat16)
    if grid.square:
        query_full = tie(query_full, own, first_far[1])
    query = dot_last(first_low, query_full).astype(jnp.bfloat16)
    if grid.square:
        down_way.last(query)
        down_way.spread()
        hidden_way.cross(0)
        down_way.cross(0)
        first_far[0] = tie(first_far[0], query, down_way.column, *hidden_way.crossed)
    far, done = [], ()
    for row in range(rows):
        far.append(dot_last(first_far[row], both_full).astype(jnp.bfloat16))
        done = attend(query, own, far[row], query_ids, key_ids, row, *done)
        if row == 0 and grid.square:
            hidden_way.forward("y", done[0])
            down_way.forward("x", done[0])
            first_far[1] = tie(
                first_far[1],
                hidden_way.over_x,
                hidden_way.over_y,
                down_way.over_x,
                down_way.over_y,
                *down_way.crossed,
            )
            hidden_way.cross(1)
            hidden_way.cross(2)
    attended, level = done
    if grid.square:
        down_way.cross(1, attended, down_way.blocks[3])
        down_way.cross(2, attended, down_way.blocks[3])
        hidden_blocks = place_blocks(grid, hidden_way.core(attended), hidden_way.order)
        hidden_blocks = hidden_blocks.reshape(-1, model, model)
        down_blocks = join_down(grid, down_way.core(attended), down_way.order, *down_weight.shape)
    flat = (-1, model)
    (
        output,
        second_low,
        act_low,
        grad_pre,
        grad_middle,
        grad_proj,
        grad_attended,
        hidden_sums,
        middle_sums,
    ) = middle_block(
        stream.reshape(flat),
        attended.reshape(flat),
        cotangent.reshape(flat),
        used_rows,
        proj_full,
        hidden_blocks,
        down_blocks,
        proj_bias_full,
        gain_two,
        shift_two,
        hidden_bias_full,
        down_bias_full,
    )
    hidden_bias_grad = jnp.sum(hidden_sums, axis=0).reshape(-1)
    middle_sums = jnp.sum(middle_sums, axis=0)
    gain_two_grad, shift_two_grad = middle_sums[0], middle_sums[1]
    proj_bias_grad, down_bias_grad = middle_sums[2], middle_sums[3]
    grad_branch = jnp.where(used[..., None], cotangent, 0).reshape(flat)
    here, outer = grid.at["c"].astype(jnp.int32).reshape(1), grid.outer_count
    if grid.square:
        keep, give = tall_grad(act_low, grad_branch, here, outer, "down_weight_grad")
        down_way = Scatter(grid, keep, give, (outer, 2, 2) + keep.shape[2:])
        second_low = tie(second_low, give)
        keep, give = wide_grad(second_low, grad_pre, here, outer, "hidden_weight_grad")
        hidden_way = Scatter(grid, keep, give, (outer, -1, keep.shape[1]))
        down_way.pull(give)
        down_way.push("x", choose_dim(2))
        hidden_way.pull(down_way.sent)
        hidden_way.push("y", choose_lanes)
        grad_attended = tie(grad_attended, hidden_way.sent)
    else:
        down_grad = outer_dot(act_low, grad_branch)
        hidden_grad = outer_dot(second_low, grad_pre)
    output = output.reshape(stream.shape)
    grad_middle = grad_middle.reshape(stream.shape)
    grad_attended = grad_attended.reshape(stream.shape)

    grad_far, done = [], ()
    for row in range(rows):
        done = attend_back(
            query,
            own,
            far[row],
            attended,
            grad_attended,
            level,
            query_ids,
            key_ids,
            row,
            *done,
        )
        both_grad = done[1]
        if grid.square:
            down_way.pull(both_grad)
            hidden_way.pull(down_way.value)
            if row == 0:
                down_way.push("y", choose_dim(1))
                hidden_way.push("x", choose_lanes)
                both_grad = tie(both_grad, down_way.sent, hidden_way.sent)
            else:
                both_grad = tie(both_grad, down_way.value, hidden_way.value, *grad_far)
        share = dot_back(both_grad[row : row + 1, all_rows:], both_full).astype(jnp.bfloat16)
        grad_far.append(far_send(grid, share))
        done = (done[0], tie(both_grad, share))
    query_grad, both_grad = done
    both_flat = both_grad.reshape(-1, 2 * model)
    query_flat = query_grad.reshape(flat)
    if grid.square:
        keep, give = mixed_grad(
            first_low.reshape(flat),
            [value[0] for value in first_far],
            attended.reshape(flat),
            query_flat,
            both_flat,
            grad_proj,
            here,
            outer,
        )
        give = tie(give, *grad_far)
        mixed_way = Scatter(grid, keep, give, (outer, -1, keep.shape[1]))
        down_way.value = tie(down_way.value, give)
        hidden_way.value = tie(hidden_way.value, give)
        down_way.push("z", choose_half, 2)
        hidden_way.push("z", choose_odd, 1)
        query_grad = tie(query_grad, give, *grad_far)
        both_grad = tie(both_grad, give, *grad_far)
    else:
        first_all = [jnp.concatenate([first_low[row], first_far[row][0]]) for row in range(rows)]
        both_weight_grad = outer_dot(jnp.concatenate(first_all), both_flat)
        query_weight_grad = outer_dot(first_low.reshape(flat), query_flat)
        proj_grad = outer_dot(attended.reshape(flat), grad_proj)
    grad_first = dot_back(query_grad, query_full) + dot_back(both_grad[:, :all_rows], both_full)
    if grid.square:
        mixed_way.pull(grad_first)
        down_way.pull(mixed_way.value)
        down_way.push("z", choose_half, 1)
        hidden_way.pull(mixed_way.value)
        hidden_way.push("z", choose_half, 2)
        way_a, way_b = fork(mixed_way, 1, 8)
        way_a.push("y", choose_lanes)
        way_b.push("x", choose_odd_lanes)
        grad_first = tie(grad_first, way_a.sent, way_b.sent)
    grad_first = grad_first + jnp.concatenate(grad_far).astype(jnp.float32)
    grad_norm, gain_one_grad, shift_one_grad = layer_norm_back(
        grad_first, first_normal, first_scale, gain_one
    )
    grad_stream = (grad_middle + grad_norm).astype(jnp.bfloat16)
    skip_bias_grad = jnp.sum(grad_stream.astype(jnp.float32), axis=(0, 1))
    joined_flat, stream_flat = joined.reshape(-1, 2 * model), grad_stream.reshape(flat)
    if grid.square:
        keep, give = tall_grad(joined_flat, stream_flat, here, outer, "skip_weight_grad")
        skip_way = Scatter(grid, keep, give, (outer, 2, 2) + keep.shape[2:])
        grad_stream = tie(grad_stream, give)
    else:
        skip_weight_grad = outer_dot(joined_flat, stream_flat)
    vectors = scatter_vectors(
        grid,
        [
            skip_bias_grad,
            gain_one_grad,
            shift_one_grad,
            proj_bias_grad,
            gain_two_grad,
            shift_two_grad,
            hidden_bias_grad,
            down_bias_grad,
        ],
    )
    input_grad = dot_back(grad_stream, skip_full[:model])
    if grid.square:
        way_a.pull(input_grad)
        way_b.pull(input_grad)
        way_a.push("x", choose_lanes)
        way_b.push("y", choose_lanes)
        skip_way.pull(way_a.sent, way_b.sent)
        skip_a, skip_b = fork(skip_way, 3, 8)
        skip_a.push("x", choose_dim(2))
        skip_b.push("y", choose_dim(1))
        grad_stream = tie(grad_stream, skip_a.sent, skip_b.sent)
    skip_grad = dot_back(grad_stream, skip_full[model:])
    if grid.square:
        way_a.pull(skip_grad)
        way_b.pull(skip_grad)
        mixed_way.value = jnp.concatenate([way_a.value, way_b.value], axis=1)
        mixed_way.push("z", choose_half, 2)
        skip_a.pull(mixed_way.sent)
        skip_b.pull(mixed_way.sent)
        skip_a.push("y", choose_dim(1))
        skip_b.push("x", choose_dim(1))
        skip_a.pull()
        skip_b.pull()
        skip_way.value = jnp.concatenate([skip_a.value, skip_b.value], axis=1)
        skip_way.push("z", choose_odd, 1)
        mixed_way.pull(skip_way.sent)
        mixed_way.push("z", choose_half, 1)
        skip_way.pull(mixed_way.sent)
        skip_way.push("z", choose_half, 2)
        vectors = vectors(skip_way.sent)

        def tall_shard(way, shape):
            return unpack_lanes(wide_shard(way), *shape)

        def wide_shard(way):
            mine = tie(way.mine, skip_way.sent, mixed_way.sent)
            return (mine.astype(jnp.float32) + way.got.astype(jnp.float32))[0]

        down_shard = tall_shard(down_way, down_weight.shape)
        hidden_shard = wide_shard(hidden_way)
        skip_shard = tall_shard(skip_way, skip_weight.shape)
        mixed_shard = wide_shard(mixed_way)
        qkv_shard = mixed_shard[:, : qkv_weight.shape[1]]
        proj_shard = mixed_shard[:, qkv_weight.shape[1] :]
    else:
        down_shard = seq_scatter(down_grad)
        hidden_shard = seq_scatter(hidden_grad)
        skip_shard = seq_scatter(skip_weight_grad)
        proj_shard = seq_scatter(proj_grad)
        qkv_shard = seq_scatter(jnp.concatenate([query_weight_grad, both_weight_grad], axis=1))
        vectors = vectors()

    moved = items.moved[..., None] & (grid.seq_index == half - 1)
    results = [tie(output, skip_grad), input_grad, skip_grad]
    edge = own_rows - 16
    tails = jnp.stack([value[:, all_rows - 16 :].astype(jnp.float32) for value in results])
    tails = grid.shift(tails, half, half - 1)
    if grid.square:
        tails = tie(tails, skip_way.sent)

    def settle(place):
        own = results[place][:, :own_rows]
        tail = jnp.where(moved[:, -16:], tails[place].astype(own.dtype), own[:, edge:])
        return lax.dynamic_update_slice_in_dim(own, tail, edge, 1)

    return (
        settle(0),
        settle(1),
        settle(2),
        skip_shard,
        vectors[0],
        vectors[1],
        vectors[2],
        qkv_shard,
        proj_shard,
        vectors[3],
        vectors[4],
        vectors[5],
        hidden_shard,
        vectors[6],
        down_shard,
        vectors[7],
    )


def solution(mesh):
    return jax.shard_map(
        body,
        mesh=mesh,
        in_specs=(
            P("batch", "seq", None),
            P("batch", "seq", None),
            P("batch", "seq", None),
            P("batch", None),
            P("batch", None),
            P("batch", "seq"),
            P("seq"),
            P("seq"),
            P("seq"),
            P("batch", "seq"),
            P("batch", "seq"),
            P("seq"),
            P("seq"),
            P("seq"),
            P("batch", "seq"),
            P("seq"),
            P("batch", "seq"),
            P("seq"),
        ),
        out_specs=(
            P("batch", "seq", None),
            P("batch", "seq", None),
            P("batch", "seq", None),
            P("batch", "seq"),
            P("seq"),
            P("seq"),
            P("seq"),
            P("batch", "seq"),
            P("batch", "seq"),
            P("seq"),
            P("seq"),
            P("seq"),
            P("batch", "seq"),
            P("seq"),
            P("batch", "seq"),
            P("seq"),
        ),
        check_vma=False,
    )
```

```python
import jax
import jax.numpy as jnp
from jax import lax
from jax.experimental import pallas as pl
from jax.experimental.pallas import tpu as pltpu
from jax.sharding import PartitionSpec as P

HEADS = 16
HEAD_DIM = 72
LANES = 128
epsilon = 1e-05
masked_score = -1e30
VMEM_BYTES = 60 * 1024 * 1024
FORWARD_HEADS, BACKWARD_HEADS = 1, 2
def nt_dot(left_side, right_side):
    return lax.dot_general(
        left_side, right_side, (((1,), (1,)), ((), ())), preferred_element_type=jnp.float32
    )


def tn_dot(left_side, right_side):
    return lax.dot_general(
        left_side, right_side, (((0,), (0,)), ((), ())), preferred_element_type=jnp.float32
    )


def nn_dot(left_side, right_side):
    return lax.dot_general(
        left_side, right_side, (((1,), (0,)), ((), ())), preferred_element_type=jnp.float32
    )


def split_heads(wide, head_ref, start=0):
    rows = wide.shape[0]
    pad = jnp.zeros((rows, LANES - HEAD_DIM), wide.dtype)
    for head in range(HEADS):
        piece = wide[:, head * HEAD_DIM : (head + 1) * HEAD_DIM]
        head_ref[head, start : start + rows] = jnp.concatenate([piece, pad], axis=1)


def split_keys(own_ref, far_ref, kh, vh):
    features = own_ref.shape[2] // 2
    start = 0
    for ref in (own_ref, far_ref):
        split_heads(ref[0, :, :features], kh, start)
        split_heads(ref[0, :, features:], vh, start)
        start += ref.shape[1]


def join_heads(head_ref):
    return jnp.concatenate([head_ref[head][:, :HEAD_DIM] for head in range(HEADS)], axis=1)


def chunk_of(rows, most=4):
    for count in (most, 2, 1):
        if rows % (count * 16) == 0:
            return rows // count
    return rows


def attend_kernel(
    q_ref, own_ref, far_ref, qid_ref, kid_ref, *refs
):
    out_ref, lse_ref, qh, kh, vh, score, prob = refs[-7:]
    split_heads(q_ref[0], qh)
    split_keys(own_ref, far_ref, kh, vh)
    key_rows = kh.shape[1]
    step = chunk_of(key_rows)
    scale = HEAD_DIM ** (-0.5)
    query_ids = qid_ref[0]

    def one_head(head, score, prob):
        query = qh[head]
        top = jnp.full((1, query.shape[0]), masked_score, jnp.float32)
        for start in range(0, key_rows, step):
            part = nt_dot(kh[head, start : start + step], query) * scale
            part = jnp.where(kid_ref[0, start : start + step] == query_ids, part, masked_score)
            score[start : start + step] = part
            top = jnp.maximum(top, jnp.max(part, axis=0, keepdims=True))
        total = jnp.zeros_like(top)
        for start in range(0, key_rows, step):
            part = jnp.exp(score[start : start + step] - top)
            total = total + jnp.sum(part, axis=0, keepdims=True)
            prob[start : start + step] = part.astype(jnp.bfloat16)
        mixed = tn_dot(vh[head], prob[...]) / total
        qh[head] = mixed.T.astype(jnp.bfloat16)
        lse_ref[0, pl.ds(head, 1)] = top + jnp.log(total)

    def some_heads(index, carry):
        for lane in range(FORWARD_HEADS):
            one_head(index * FORWARD_HEADS + lane, score.at[lane], prob.at[lane])
        return carry

    lax.fori_loop(0, HEADS // FORWARD_HEADS, some_heads, 0)
    out_ref[0] = join_heads(qh)


def attend(query, own, far, query_ids, key_ids, row, *old):
    rows, width, features = query.shape
    far_rows = far.shape[1]
    key_rows = width + far_rows
    here = lambda i: (row, 0, 0)
    only = lambda i: (0, 0, 0)
    wide = pl.BlockSpec((1, width, features), here)
    levels = pl.BlockSpec((1, HEADS, width), here)
    return pl.pallas_call(
        attend_kernel,
        grid=(1,),
        in_specs=[
            wide,
            pl.BlockSpec((1, width, 2 * features), here),
            pl.BlockSpec((1, far_rows, 2 * features), only),
            pl.BlockSpec((1, 1, width), here),
            pl.BlockSpec((1, key_rows, 1), here),
        ]
        + [pl.BlockSpec(memory_space=pl.ANY)] * len(old),
        out_specs=[wide, levels],
        out_shape=[
            jax.ShapeDtypeStruct((rows, width, features), jnp.bfloat16),
            jax.ShapeDtypeStruct((rows, HEADS, width), jnp.float32),
        ],
        scratch_shapes=[
            pltpu.VMEM((HEADS, width, LANES), jnp.bfloat16),
            pltpu.VMEM((HEADS, key_rows, LANES), jnp.bfloat16),
            pltpu.VMEM((HEADS, key_rows, LANES), jnp.bfloat16),
            pltpu.VMEM((FORWARD_HEADS, key_rows, width), jnp.float32),
            pltpu.VMEM((FORWARD_HEADS, key_rows, width), jnp.bfloat16),
        ],
        input_output_aliases={5: 0, 6: 1} if old else {},
        compiler_params=pltpu.CompilerParams(vmem_limit_bytes=VMEM_BYTES),
        cost_estimate=pl.CostEstimate(
            flops=4 * HEADS * width * key_rows * LANES,
            transcendentals=HEADS * width * key_rows,
            bytes_accessed=4 * features * (width + key_rows),
        ),
        name="attend",
    )(query, own, far, query_ids, key_ids, *old)


def attend_back_kernel(
    q_ref, own_ref, far_ref, o_ref, g_ref, lse_ref, qid_ref, kid_ref, *refs
):
    dq_ref, dkv_ref, qh, kh, vh, oh, gh, prob, slope = refs[-9:]
    split_heads(q_ref[0], qh)
    features = q_ref.shape[2]
    split_keys(own_ref, far_ref, kh, vh)
    split_heads(o_ref[0], oh)
    split_heads(g_ref[0], gh)
    key_rows = kh.shape[1]
    step = chunk_of(key_rows, 2)
    scale = HEAD_DIM ** (-0.5)
    query_ids = qid_ref[0]

    def one_head(head, prob, slope):
        query = qh[head]
        grad = gh[head]
        level = lse_ref[0, pl.ds(head, 1)]
        overlap = oh[head].astype(jnp.float32) * grad.astype(jnp.float32)
        row_dot = jnp.sum(overlap.T, axis=0, keepdims=True)
        for start in range(0, key_rows, step):
            part = nt_dot(kh[head, start : start + step], query) * scale
            part = jnp.where(kid_ref[0, start : start + step] == query_ids, part, masked_score)
            soft = jnp.exp(part - level)
            prob[start : start + step] = soft.astype(jnp.bfloat16)
            turn = nt_dot(vh[head, start : start + step], grad)
            slope[start : start + step] = (soft * (turn - row_dot)).astype(jnp.bfloat16)
        value_grad = nn_dot(prob[...], grad)
        query_grad = tn_dot(kh[head], slope[...]) * scale
        key_grad = nn_dot(slope[...], query) * scale
        vh[head] = value_grad.astype(jnp.bfloat16)
        kh[head] = key_grad.astype(jnp.bfloat16)
        qh[head] = query_grad.T.astype(jnp.bfloat16)

    def some_heads(index, carry):
        for lane in range(BACKWARD_HEADS):
            one_head(index * BACKWARD_HEADS + lane, prob.at[lane], slope.at[lane])
        return carry

    lax.fori_loop(0, HEADS // BACKWARD_HEADS, some_heads, 0)
    dq_ref[0] = join_heads(qh)
    dkv_ref[0, :, :features] = join_heads(kh)
    dkv_ref[0, :, features:] = join_heads(vh)


def attend_back(
    query, own, far, mixed, grad, level, query_ids, key_ids, row, *old
):
    rows, width, features = query.shape
    far_rows = far.shape[1]
    key_rows = width + far_rows
    here = lambda i: (row, 0, 0)
    only = lambda i: (0, 0, 0)
    wide = pl.BlockSpec((1, width, features), here, pipeline_mode=pl.Buffered(1))
    return pl.pallas_call(
        attend_back_kernel,
        grid=(1,),
        in_specs=[
            wide,
            pl.BlockSpec((1, width, 2 * features), here, pipeline_mode=pl.Buffered(1)),
            pl.BlockSpec((1, far_rows, 2 * features), only, pipeline_mode=pl.Buffered(1)),
            wide,
            wide,
            pl.BlockSpec((1, HEADS, width), here),
            pl.BlockSpec((1, 1, width), here),
            pl.BlockSpec((1, key_rows, 1), here),
        ]
        + [pl.BlockSpec(memory_space=pl.ANY)] * len(old),
        out_specs=[
            pl.BlockSpec((1, width, features), here),
            pl.BlockSpec((1, key_rows, 2 * features), here),
        ],
        out_shape=[
            jax.ShapeDtypeStruct((rows, width, features), jnp.bfloat16),
            jax.ShapeDtypeStruct((rows, key_rows, 2 * features), jnp.bfloat16),
        ],
        scratch_shapes=[
            pltpu.VMEM((HEADS, width, LANES), jnp.bfloat16),
            pltpu.VMEM((HEADS, key_rows, LANES), jnp.bfloat16),
            pltpu.VMEM((HEADS, key_rows, LANES), jnp.bfloat16),
            pltpu.VMEM((HEADS, width, LANES), jnp.bfloat16),
            pltpu.VMEM((HEADS, width, LANES), jnp.bfloat16),
            pltpu.VMEM((BACKWARD_HEADS, key_rows, width), jnp.bfloat16),
            pltpu.VMEM((BACKWARD_HEADS, key_rows, width), jnp.bfloat16),
        ],
        input_output_aliases={8: 0, 9: 1} if old else {},
        compiler_params=pltpu.CompilerParams(vmem_limit_bytes=VMEM_BYTES),
        cost_estimate=pl.CostEstimate(
            flops=10 * HEADS * width * key_rows * LANES,
            transcendentals=HEADS * width * key_rows,
            bytes_accessed=8 * features * (width + key_rows),
        ),
        name="attend_back",
    )(
        query,
        own,
        far,
        mixed,
        grad,
        level,
        query_ids,
        key_ids,
        *old,
    )


def split_rows(total_ref, here, outer, keep_ref, give_ref):
    inner = total_ref.shape[0] // (2 * outer)
    for group in range(outer):
        start = group * 2 * inner
        span = slice(group * inner, (group + 1) * inner)
        keep_ref[span] = total_ref[pl.ds(pl.multiple_of(start + here * inner, 16), inner)]
        give_ref[span] = total_ref[pl.ds(pl.multiple_of(start + (1 - here) * inner, 16), inner)]


def wide_grad_kernel(outer, here_ref, left_ref, right_ref, keep_ref, give_ref, total):
    total[...] = tn_dot(left_ref[...], right_ref[...]).astype(jnp.bfloat16)
    split_rows(total, here_ref[0], outer, keep_ref, give_ref)


def wide_grad(left, right, here, outer, name):
    tokens, rows = left.shape
    blocks = right.shape[1] // rows
    half = jax.ShapeDtypeStruct((rows // 2, right.shape[1]), jnp.bfloat16)
    spec = pl.BlockSpec((rows // 2, rows), lambda j, here: (0, j))
    return pl.pallas_call(
        lambda *refs: wide_grad_kernel(outer, *refs),
        grid_spec=pltpu.PrefetchScalarGridSpec(
            num_scalar_prefetch=1,
            grid=(blocks,),
            in_specs=[
                pl.BlockSpec((tokens, rows), lambda j, here: (0, 0)),
                pl.BlockSpec((tokens, rows), lambda j, here: (0, j)),
            ],
            out_specs=[spec, spec],
            scratch_shapes=[pltpu.VMEM((rows, rows), jnp.bfloat16)],
        ),
        out_shape=[half, half],
        compiler_params=pltpu.CompilerParams(vmem_limit_bytes=VMEM_BYTES),
        cost_estimate=pl.CostEstimate(
            flops=2 * tokens * rows * right.shape[1],
            transcendentals=0,
            bytes_accessed=2 * (tokens + right.shape[1]) * rows,
        ),
        name=name,
    )(here, left, right)


def tall_grad_kernel(groups, here_ref, left_ref, right_ref, keep_ref, give_ref, total):
    total[...] = tn_dot(left_ref[...], right_ref[...]).astype(jnp.bfloat16)
    here = here_ref[0]
    inner = total.shape[0] // (2 * groups)
    columns = total.shape[1] // 4
    for group in range(groups):
        start = group * 2 * inner
        for core, out_ref in ((here, keep_ref), (1 - here, give_ref)):
            rows = total[pl.ds(pl.multiple_of(start + core * inner, 16), inner)]
            for place in range(4):
                out_ref[group, place] = pack_lanes(rows[:, place * columns : (place + 1) * columns])


def tall_grad(left, right, here, outer, name):
    tokens, model = right.shape
    blocks = left.shape[1] // model
    groups = outer // blocks
    packed = left.shape[1] // (2 * outer) * (model // 4) // LANES
    half = jax.ShapeDtypeStruct((outer, 4, packed, LANES), jnp.bfloat16)
    spec = pl.BlockSpec((groups, 4, packed, LANES), lambda i, here: (i, 0, 0, 0))
    return pl.pallas_call(
        lambda *refs: tall_grad_kernel(groups, *refs),
        grid_spec=pltpu.PrefetchScalarGridSpec(
            num_scalar_prefetch=1,
            grid=(blocks,),
            in_specs=[
                pl.BlockSpec((tokens, model), lambda i, here: (0, i)),
                pl.BlockSpec((tokens, model), lambda i, here: (0, 0)),
            ],
            out_specs=[spec, spec],
            scratch_shapes=[pltpu.VMEM((model, model), jnp.bfloat16)],
        ),
        out_shape=[half, half],
        compiler_params=pltpu.CompilerParams(vmem_limit_bytes=VMEM_BYTES),
        cost_estimate=pl.CostEstimate(
            flops=2 * tokens * model * left.shape[1],
            transcendentals=0,
            bytes_accessed=2 * (tokens + model) * left.shape[1],
        ),
        name=name,
    )(here, left, right)


def mixed_grad_kernel(
    outer, here_ref, first_ref, far_a, far_b, att_ref, query_ref, both_ref, proj_ref,
    keep_ref, give_ref, total, sums,
):
    step = pl.program_id(0)
    width = far_a.shape[0]
    span = far_a.shape[0] + first_ref.shape[0] // 2
    own = first_ref.shape[0] // 2

    @pl.when(step == 0)
    def _():
        total[0] = tn_dot(first_ref[...], query_ref[...]).astype(jnp.bfloat16)

    @pl.when((step == 1) | (step == 2))
    def _():
        sums[...] = tn_dot(first_ref[0:own], both_ref[0:own])
        sums[...] += tn_dot(far_a[...], both_ref[own:span])
        sums[...] += tn_dot(first_ref[own:], both_ref[span : span + own])
        total[step] = (sums[...] + tn_dot(far_b[...], both_ref[span + own :])).astype(jnp.bfloat16)

    @pl.when(step == 3)
    def _():
        total[3] = tn_dot(att_ref[...], proj_ref[...]).astype(jnp.bfloat16)
        here = here_ref[0]
        model = total.shape[2]
        inner = model // (2 * outer)
        cut = model * 3 // 4
        for group in range(outer):
            rows = slice(group * inner, (group + 1) * inner)
            for core, out_ref in ((here, keep_ref), (1 - here, give_ref)):
                start = pl.multiple_of((group * 2 + core) * inner, 16)
                wide = jnp.concatenate([total[k, pl.ds(start, inner)] for k in range(3)], axis=1)
                last = total[3, pl.ds(start, inner)]
                for place in range(4):
                    out_ref[rows, place * model : (place + 1) * model] = jnp.concatenate(
                        [
                            wide[:, place * cut : (place + 1) * cut],
                            last[:, place * (model - cut) : (place + 1) * (model - cut)],
                        ],
                        axis=1,
                    )


def mixed_grad(first, far, attended, query_grad, both_grad, proj_grad, here, outer):
    tokens, model = first.shape
    half = jax.ShapeDtypeStruct((model // 2, 4 * model), jnp.bfloat16)
    fixed = lambda *shape: pl.BlockSpec(
        shape, lambda j, here: (0, 0), pipeline_mode=pl.Buffered(1)
    )
    return pl.pallas_call(
        lambda *refs: mixed_grad_kernel(outer, *refs),
        grid_spec=pltpu.PrefetchScalarGridSpec(
            num_scalar_prefetch=1,
            grid=(4,),
            in_specs=[
                fixed(tokens, model),
                fixed(*far[0].shape),
                fixed(*far[1].shape),
                fixed(tokens, model),
                fixed(tokens, model),
                pl.BlockSpec(
                    (both_grad.shape[0], model),
                    lambda j, here: (0, jnp.minimum(jnp.maximum(j - 1, 0), 1)),
                ),
                fixed(tokens, model),
            ],
            out_specs=[fixed(model // 2, 4 * model), fixed(model // 2, 4 * model)],
            scratch_shapes=[
                pltpu.VMEM((4, model, model), jnp.bfloat16),
                pltpu.VMEM((model, model), jnp.float32),
            ],
        ),
        out_shape=[half, half],
        compiler_params=pltpu.CompilerParams(vmem_limit_bytes=VMEM_BYTES),
        cost_estimate=pl.CostEstimate(
            flops=2 * model * model * (2 * tokens + 2 * both_grad.shape[0]),
            transcendentals=0,
            bytes_accessed=2 * model * (6 * tokens + 2 * both_grad.shape[0] + 4 * model),
        ),
        name="mixed_weight_grad",
    )(here, first, far[0], far[1], attended, query_grad, both_grad, proj_grad)


def column_chunks(width):
    cut = width // 256 // 2 * 256
    return ((0, cut), (cut, width)) if cut else ((0, width),)


def middle_kernel(
    stream_ref, att_ref, cot_ref, used_ref, proj_ref, hidden_ref, down_ref,
    proj_bias_ref, gain_ref, shift_ref, hidden_bias_ref, down_bias_ref,
    out_ref, second_ref, act_ref, pre_ref, middle_grad_ref, proj_grad_ref, att_grad_ref,
    hidden_sum_ref, sums_ref,
    low, normal, scale, branch, total, back,
):
    step = pl.program_id(1)
    steps = pl.num_programs(1)

    @pl.when(step == 0)
    def _():
        middle = stream_ref[...] + nn_dot(att_ref[...], proj_ref[...]) + proj_bias_ref[...]
        centred = middle - jnp.mean(middle, axis=-1, keepdims=True)
        inverse = lax.rsqrt(jnp.mean(centred * centred, axis=-1, keepdims=True) + epsilon)
        unit = centred * inverse
        normal[...] = unit
        scale[...] = inverse
        second = (unit * gain_ref[...] + shift_ref[...]).astype(jnp.bfloat16)
        low[...] = second
        second_ref[...] = second
        branch[...] = (cot_ref[...].astype(jnp.float32) * used_ref[...]).astype(jnp.bfloat16)
        total[...] = middle + down_bias_ref[...]
        back[...] = jnp.zeros_like(back)

    for start, stop in column_chunks(hidden_ref.shape[2]):
        pre_act = nn_dot(low[...], hidden_ref[0, :, start:stop]) + hidden_bias_ref[0, :, start:stop]
        grad_act = nt_dot(branch[...], down_ref[0, start:stop])
        below = 0.5 + 0.5 * lax.erf(pre_act * (0.5**0.5))
        density = jnp.exp(-0.5 * pre_act * pre_act) * ((2.0 * jnp.pi) ** -0.5)
        act = (pre_act * below).astype(jnp.bfloat16)
        grad_pre = (grad_act * (below + pre_act * density)).astype(jnp.bfloat16)
        act_ref[:, start:stop] = act
        pre_ref[:, start:stop] = grad_pre
        hidden_sum_ref[0, 0, :, start:stop] = jnp.sum(
            grad_pre.astype(jnp.float32), axis=0, keepdims=True
        )
        total[...] += nn_dot(act, down_ref[0, start:stop])
        back[...] += nt_dot(grad_pre, hidden_ref[0, :, start:stop])

    @pl.when(step == steps - 1)
    def _():
        out_ref[...] = total[...].astype(jnp.bfloat16)
        grad = back[...]
        unit = normal[...]
        part = grad * gain_ref[...]
        mean_part = jnp.mean(part, axis=-1, keepdims=True)
        mean_both = jnp.mean(part * unit, axis=-1, keepdims=True)
        grad_out = cot_ref[...].astype(jnp.float32) * used_ref[...]
        grad_middle = grad_out + (part - mean_part - unit * mean_both) * scale[...]
        middle_grad_ref[...] = grad_middle
        grad_low = grad_middle.astype(jnp.bfloat16)
        proj_grad_ref[...] = grad_low
        att_grad_ref[...] = nt_dot(grad_low, proj_ref[...]).astype(jnp.bfloat16)
        sums_ref[0, 0:1] = jnp.sum(grad * unit, axis=0, keepdims=True)
        sums_ref[0, 1:2] = jnp.sum(grad, axis=0, keepdims=True)
        sums_ref[0, 2:3] = jnp.sum(grad_low.astype(jnp.float32), axis=0, keepdims=True)
        sums_ref[0, 3:4] = jnp.sum(grad_out, axis=0, keepdims=True)


def token_block(tokens):
    return tokens // 4 if tokens % 64 == 0 else tokens


def middle_block(
    stream, attended, cotangent, used, proj, hidden, down, proj_bias, gain, shift, hidden_bias,
    down_bias,
):
    tokens, model = stream.shape
    steps = hidden.shape[0]
    rows = token_block(tokens)
    blocks = tokens // rows
    by_rows = pl.BlockSpec((rows, model), lambda i, s: (i, 0))
    by_step = pl.BlockSpec((rows, model), lambda i, s: (i, s))
    vector = pl.BlockSpec((1, model), lambda i, s: (0, 0))
    low_rows = jax.ShapeDtypeStruct((tokens, model), jnp.bfloat16)
    low_steps = jax.ShapeDtypeStruct((tokens, steps * model), jnp.bfloat16)
    flops = 2 * tokens * model * model * (4 * steps + 2)
    return pl.pallas_call(
        middle_kernel,
        grid=(blocks, steps),
        in_specs=[
            by_rows,
            by_rows,
            by_rows,
            pl.BlockSpec((rows, 1), lambda i, s: (i, 0)),
            pl.BlockSpec((model, model), lambda i, s: (0, 0), pipeline_mode=pl.Buffered(1)),
            pl.BlockSpec((1, model, model), lambda i, s: (s, 0, 0)),
            pl.BlockSpec((1, model, model), lambda i, s: (s, 0, 0)),
            vector,
            vector,
            vector,
            pl.BlockSpec((1, 1, model), lambda i, s: (s, 0, 0)),
            vector,
        ],
        out_specs=[
            by_rows,
            by_rows,
            by_step,
            by_step,
            by_rows,
            by_rows,
            by_rows,
            pl.BlockSpec((1, 1, 1, model), lambda i, s: (i, s, 0, 0)),
            pl.BlockSpec((1, 4, model), lambda i, s: (i, 0, 0)),
        ],
        out_shape=[
            low_rows,
            low_rows,
            low_steps,
            low_steps,
            jax.ShapeDtypeStruct((tokens, model), jnp.float32),
            low_rows,
            low_rows,
            jax.ShapeDtypeStruct((blocks, steps, 1, model), jnp.float32),
            jax.ShapeDtypeStruct((blocks, 4, model), jnp.float32),
        ],
        scratch_shapes=[
            pltpu.VMEM((rows, model), jnp.bfloat16),
            pltpu.VMEM((rows, model), jnp.float32),
            pltpu.VMEM((rows, 1), jnp.float32),
            pltpu.VMEM((rows, model), jnp.bfloat16),
            pltpu.VMEM((rows, model), jnp.float32),
            pltpu.VMEM((rows, model), jnp.float32),
        ],
        compiler_params=pltpu.CompilerParams(vmem_limit_bytes=VMEM_BYTES),
        cost_estimate=pl.CostEstimate(
            flops=flops,
            transcendentals=2 * tokens * model * steps,
            bytes_accessed=2 * tokens * model * (2 * steps + 12) + 4 * model * model * steps * blocks,
        ),
        name="middle_block",
    )(
        stream,
        attended,
        cotangent,
        used,
        proj,
        hidden,
        down,
        proj_bias[None],
        gain[None],
        shift[None],
        hidden_bias.reshape(steps, 1, model),
        down_bias[None],
    )


def layer_norm(stream, norm_gain, norm_shift):
    centred = stream - jnp.mean(stream, axis=-1, keepdims=True)
    scale = lax.rsqrt(jnp.mean(centred * centred, axis=-1, keepdims=True) + epsilon)
    normal = centred * scale
    return (normal * norm_gain + norm_shift).astype(jnp.bfloat16), normal, scale


def layer_norm_back(grad, normal, scale, norm_gain):
    part = grad * norm_gain
    mean_part = jnp.mean(part, axis=-1, keepdims=True)
    mean_both = jnp.mean(part * normal, axis=-1, keepdims=True)
    gain_grad = jnp.sum(grad * normal, axis=(0, 1))
    shift_grad = jnp.sum(grad, axis=(0, 1))
    return (part - mean_part - normal * mean_both) * scale, gain_grad, shift_grad


def outer_dot(left_side, right_side):
    return lax.dot_general(
        left_side, right_side, (((0,), (0,)), ((), ())), preferred_element_type=jnp.bfloat16
    )


def dot_last(left_side, right_side):
    return lax.dot_general(
        left_side, right_side, (((2,), (0,)), ((), ())), preferred_element_type=jnp.float32
    )


def dot_back(left_side, right_side):
    return lax.dot_general(
        left_side, right_side, (((2,), (1,)), ((), ())), preferred_element_type=jnp.float32
    )


def dot_tokens(left_side, right_side):
    return lax.dot_general(
        left_side, right_side, (((0, 1), (0, 1)), ((), ())), preferred_element_type=jnp.bfloat16
    )


class Grid:
    def __init__(self):
        self.batch_count = lax.axis_size("batch")
        self.seq_count = lax.axis_size("seq")
        self.seq_index = lax.axis_index("seq")
        batch_index = lax.axis_index("batch")
        self.outer_count = self.batch_count // 2
        self.square = self.seq_count == 4 and self.outer_count == 4
        self.at = {
            "z": batch_index // 2,
            "c": batch_index % 2,
            "y": self.seq_index // 2,
            "x": self.seq_index % 2,
        }

    def index(self, z, c, s):
        return (z * 2 + c) * self.seq_count + s

    def send(self, value, axis, turn=0):
        pairs = []
        for z in range(self.outer_count):
            for c in range(2):
                for s in range(self.seq_count):
                    far_z, far_c, far_s = z, c, s
                    if axis == "z":
                        far_z = z ^ turn
                    elif axis == "c":
                        far_c = 1 - c
                    elif axis == "y":
                        far_s = s ^ 2
                    else:
                        far_s = s ^ 1
                    pairs.append((self.index(z, c, s), self.index(far_z, far_c, far_s)))
        return lax.ppermute(value, ("batch", "seq"), pairs)

    def shift(self, value, source, target):
        pairs = [
            (b * self.seq_count + source, b * self.seq_count + target)
            for b in range(self.batch_count)
        ]
        return lax.ppermute(value, ("batch", "seq"), pairs)


def tie(value, *others):
    return lax.optimization_barrier((value, *others))[0]


def square_gather(grid, shard):
    over_x = grid.send(shard, "x")
    found = jnp.stack([shard, over_x, grid.send(shard, "y"), grid.send(over_x, "y")])
    return jnp.stack(
        [
            lax.dynamic_index_in_dim(found, grid.seq_index ^ place, 0, keepdims=False)
            for place in range(4)
        ]
    )


def pack_lanes(shard):
    rows, columns = shard.shape
    whole = columns // LANES
    rest = columns - whole * LANES
    pieces = [shard[:, k * LANES : (k + 1) * LANES] for k in range(whole)]
    if rest:
        fold = LANES // rest
        step = rows // fold
        last = [shard[k * step : (k + 1) * step, whole * LANES :] for k in range(fold)]
        pieces.append(jnp.concatenate(last, axis=1))
    return jnp.concatenate(pieces, axis=0)


def unpack_lanes(packed, rows, columns):
    whole = columns // LANES
    rest = columns - whole * LANES
    pieces = [packed[k * rows : (k + 1) * rows] for k in range(whole)]
    if rest:
        fold = LANES // rest
        last = packed[whole * rows : whole * rows + rows // fold]
        pieces.append(
            jnp.concatenate([last[:, k * rest : (k + 1) * rest] for k in range(fold)], axis=0)
        )
    return jnp.concatenate(pieces, axis=1)


def rows_kernel(rows, columns, turn_ref, to_ref, *refs):
    blocks, out_ref, found = refs[:8], refs[8], refs[9]
    for block in range(8):
        found[to_ref[block]] = blocks[block][...]
    for core in range(2):
        wide = [unpack_lanes(found[core * 4 + place], rows, columns) for place in range(4)]
        out_ref[core * rows : (core + 1) * rows] = jnp.concatenate(wide, axis=1)


def mixed_kernel(columns, turn_ref, to_ref, *refs):
    blocks, query_ref, both_ref, proj_ref, found = refs[:8], refs[8], refs[9], refs[10], refs[11]
    rows, model = found.shape[1:]
    for block in range(8):
        found[to_ref[block]] = blocks[block][...]
    for core in range(2):
        span = slice(core * rows, (core + 1) * rows)
        parts = [found[core * 4 + place] for place in range(4)]
        wide = jnp.concatenate([part[:, :columns] for part in parts], axis=1)
        query_ref[span] = wide[:, :model]
        both_ref[span] = wide[:, model:]
        proj_ref[span] = jnp.concatenate([part[:, columns:] for part in parts], axis=1)


def swap_bits(value):
    return ((value & 1) << 1) | (value >> 1)


def assemble(grid, blocks, order, piece, kernel, widths, rows, name):
    outer = grid.outer_count
    turns = grid.at["z"] ^ jnp.arange(4, dtype=jnp.int32)
    if order[1] == 2:
        turns = swap_bits(turns)
    block = jnp.arange(8, dtype=jnp.int32)
    places = (grid.at["c"] ^ (block >> 2)) * 4 + (grid.seq_index ^ (block & 3))
    shapes = [jax.ShapeDtypeStruct((outer * 2 * rows, w), jnp.bfloat16) for w in widths]
    return pl.pallas_call(
        kernel,
        grid_spec=pltpu.PrefetchScalarGridSpec(
            num_scalar_prefetch=2,
            grid=(outer,),
            in_specs=[pl.BlockSpec(piece, lambda z, turn, to: (turn[z], 0))] * 8,
            out_specs=[pl.BlockSpec((2 * rows, w), lambda z, turn, to: (z, 0)) for w in widths],
            scratch_shapes=[pltpu.VMEM((8,) + piece, jnp.bfloat16)],
        ),
        out_shape=shapes,
        compiler_params=pltpu.CompilerParams(vmem_limit_bytes=VMEM_BYTES),
        cost_estimate=pl.CostEstimate(
            flops=0,
            transcendentals=0,
            bytes_accessed=8 * outer * rows * sum(widths),
        ),
        name=name,
    )(turns, places, *blocks)


def place_kernel(block_count, outer_count, to_ref, *refs):
    blocks, out_ref, sems = refs[:block_count], refs[block_count], refs[block_count + 1]
    rows = out_ref.shape[1]
    copies = []
    for block in range(block_count):
        for turn in range(outer_count):
            slot = block * outer_count + turn
            copies.append(
                pltpu.make_async_copy(
                    blocks[block].at[pl.ds(turn * rows, rows)], out_ref.at[to_ref[slot]], sems.at[slot]
                )
            )
    for copy in copies:
        copy.start()
    for copy in copies:
        copy.wait()


def place_blocks(grid, blocks, order):
    outer = grid.outer_count
    rows, columns = blocks[0].shape[0] // outer, blocks[0].shape[1]
    spot = jnp.arange(8 * outer, dtype=jnp.int32)
    core, place = grid.at["c"] ^ (spot >> 4), grid.seq_index ^ (spot >> 2 & 3)
    turn = spot & 3
    if order[1] == 2:
        turn = swap_bits(turn)
    slots = (place * outer + (grid.at["z"] ^ turn)) * 2 + core
    count = 8 * outer
    return pl.pallas_call(
        lambda *refs: place_kernel(8, outer, *refs),
        grid_spec=pltpu.PrefetchScalarGridSpec(
            num_scalar_prefetch=1,
            grid=(1,),
            in_specs=[pl.BlockSpec(memory_space=pl.ANY)] * 8,
            out_specs=pl.BlockSpec((count, rows, columns), lambda i, to: (0, 0, 0)),
            scratch_shapes=[pltpu.SemaphoreType.DMA((count,))],
        ),
        compiler_params=pltpu.CompilerParams(vmem_limit_bytes=VMEM_BYTES),
        out_shape=jax.ShapeDtypeStruct((count, rows, columns), blocks[0].dtype),
        cost_estimate=pl.CostEstimate(
            flops=0, transcendentals=0, bytes_accessed=4 * count * rows * columns
        ),
        name="place_blocks",
    )(slots, *blocks)


class Gather:
    def __init__(self, grid, piece):
        self.grid, self.piece, self.crossed = grid, piece, []

    def direct(self, *extra):
        self.order = [0, 1, 2, 3]
        parts = [self.piece] + [self.grid.send(self.piece, "z", turn) for turn in (1, 2, 3)]
        self.column = jnp.concatenate(parts + list(extra), axis=0)

    def first(self):
        self.order = [0, 2, 1, 3]
        self.far = self.grid.send(self.piece, "z", 2)

    def second(self, *after):
        piece = tie(self.piece, *after) if after else self.piece
        self.pair = jnp.concatenate([piece, self.far], axis=0)
        self.far = self.grid.send(self.pair, "z", 1)

    def last(self, *after):
        pair = tie(self.pair, *after) if after else self.pair
        self.column = jnp.concatenate([pair, self.far], axis=0)

    def spread(self):
        self.over_x = self.grid.send(self.column, "x")
        self.over_y = self.grid.send(self.column, "y")

    def forward(self, axis, *after):
        value = self.over_x if axis == "y" else self.over_y
        if after:
            value = tie(value, *after)
            if axis == "y":
                self.over_x = value
            else:
                self.over_y = value
        self.blocks = [self.column, self.over_x, self.over_y, self.grid.send(value, axis)]

    def cross(self, at, *after):
        block = (self.column, self.over_x, self.over_y)[at]
        block = tie(block, *after) if after else block
        self.crossed.append(self.grid.send(block, "c"))

    def core(self, *after):
        block = tie(self.blocks[3], *self.crossed[1:], *after)
        return self.blocks + self.crossed + [self.grid.send(block, "c")]


def split_vectors(joint, widths):
    result, start = [], 0
    for width in widths:
        result.append(joint[:, start : start + width].reshape(-1).astype(jnp.float32))
        start += width
    return result


def gather_plain(matrices, vectors):
    joint = lax.all_gather(jnp.concatenate(vectors), "seq", axis=0)
    wide = [
        lax.all_gather(
            lax.all_gather(shard, "batch", axis=0, tiled=True), "seq", axis=1, tiled=True
        )
        for shard in matrices
    ]
    return split_vectors(joint, [vector.shape[0] for vector in vectors]), wide


def hidden_columns(hidden_full, model):
    return jnp.stack(jnp.split(hidden_full, hidden_full.shape[1] // model, axis=1))


def gather_skip(grid, skip_weight, vectors):
    joint = jnp.concatenate(vectors)
    short = -joint.shape[0] % (8 * LANES)
    extra = jnp.pad(joint, (0, short)).reshape(-1, LANES)
    rows, columns = skip_weight.shape
    piece = pack_lanes(skip_weight)
    way = Gather(grid, piece)
    way.direct(extra)
    way.spread()
    way.forward("y")
    for at in range(3):
        way.cross(at)
    found = jnp.stack([block[-extra.shape[0] :].reshape(-1) for block in way.blocks])
    joint = jnp.stack(
        [
            lax.dynamic_index_in_dim(found, grid.seq_index ^ place, 0, keepdims=False)
            for place in range(4)
        ]
    )
    (skip_full,) = assemble(
        grid,
        way.core(),
        way.order,
        piece.shape,
        lambda *refs: rows_kernel(rows, columns, *refs),
        [4 * columns],
        rows,
        "join_skip",
    )
    return way, split_vectors(joint, [vector.shape[0] for vector in vectors]), skip_full


def join_mixed(grid, blocks, order, rows, columns, model):
    return assemble(
        grid,
        blocks,
        order,
        (rows, model),
        lambda *refs: mixed_kernel(columns, *refs),
        [model, 2 * model, model],
        rows,
        "join_mixed",
    )


def join_down(grid, blocks, order, rows, columns):
    packed = rows * columns // LANES
    (full,) = assemble(
        grid,
        blocks,
        order,
        (packed, LANES),
        lambda *refs: rows_kernel(rows, columns, *refs),
        [4 * columns],
        rows,
        "join_down",
    )
    return full.reshape(-1, 4 * columns, 4 * columns)


def add_low(mine, other):
    return (mine.astype(jnp.float32) + other.astype(jnp.float32)).astype(jnp.bfloat16)


class Scatter:
    def __init__(self, grid, keep, give, view):
        self.grid, self.mine, self.sent, self.view = grid, keep, give, view
        self.got = grid.send(give, "c")

    def push(self, axis, choose, turn=0):
        here = self.grid.at[axis]
        if turn:
            here = here // turn % 2
        self.mine, self.sent = choose(self.value, here), choose(self.value, 1 - here)
        self.got = self.grid.send(self.sent, axis, turn)

    def pull(self, *after):
        mine = tie(self.mine, *after) if after else self.mine
        self.value = add_low(mine, self.got)
        if self.view is not None:
            self.value, self.view = self.value.reshape(self.view), None
        return self.value


def fork(way, dim, align):
    whole = way.value.shape[dim]
    cut = -(-whole // (2 * align)) * align
    ways = []
    for start, stop in ((0, cut), (cut, whole)):
        branch = object.__new__(Scatter)
        branch.grid, branch.view = way.grid, None
        branch.value = lax.slice_in_dim(way.value, start, stop, axis=dim)
        ways.append(branch)
    return ways


def choose_dim(dim):
    return lambda value, at: lax.dynamic_index_in_dim(value, at, dim, keepdims=False)


def choose_half(value, at):
    half = value.shape[0] // 2
    return lax.dynamic_slice_in_dim(value, at * half, half, 0)


def choose_odd(value, at):
    pairs = value.reshape((2, 2) + value.shape[1:])
    return lax.dynamic_index_in_dim(pairs, at, 1, keepdims=False)


def choose_lanes(value, at):
    half = value.shape[-1] // 2
    return lax.dynamic_slice_in_dim(value, at * half, half, value.ndim - 1)


def choose_odd_lanes(value, at):
    part = value.shape[-1] // 4
    pieces = [
        lax.dynamic_slice_in_dim(value, (2 * k + at) * part, part, value.ndim - 1) for k in range(2)
    ]
    return jnp.concatenate(pieces, axis=-1)


def seq_scatter(value):
    value = lax.psum_scatter(value, "seq", scatter_dimension=1, tiled=True)
    return lax.psum_scatter(value, "batch", scatter_dimension=0, tiled=True).astype(jnp.float32)


def scatter_vectors(grid, vectors):
    joint = jnp.concatenate(vectors)
    if grid.square:
        joint = lax.all_gather(joint.reshape(-1, LANES), ("batch", "seq"))
    else:
        joint = lax.psum(joint, ("batch", "seq"))[None]
    return lambda *after: own_columns(grid, tie(joint, *after), vectors)


def own_columns(grid, joint, vectors):
    joint = jnp.sum(joint, axis=0).reshape(-1)
    result, start = [], 0
    for vector in vectors:
        width = vector.shape[0] // grid.seq_count
        result.append(lax.dynamic_slice_in_dim(joint, start + grid.seq_index * width, width))
        start += vector.shape[0]
    return result


class Items:
    def __init__(self, grid, segments, occupied, own_rows, all_rows):
        self.grid = grid
        self.segments, self.occupied = segments, occupied
        self.own_rows, self.all_rows = own_rows, all_rows
        self.halo_rows = all_rows - own_rows
        self.border = own_rows * (grid.seq_count // 2)
        tail = slice(self.border - self.halo_rows, self.border)
        self.moved = (segments[:, tail] == segments[:, self.border : self.border + 1]) & (
            occupied[:, tail] > 0
        )

    def of(self, seq_index):
        half = self.grid.seq_count // 2
        start = seq_index * self.own_rows
        rows = self.segments.shape[0]
        segment = lax.dynamic_slice(self.segments, (0, start), (rows, self.own_rows))
        used = lax.dynamic_slice(self.occupied, (0, start), (rows, self.own_rows)) > 0
        gone = jnp.pad(self.moved, ((0, 0), (self.own_rows - self.halo_rows, 0)))
        used = used & ~(gone & (seq_index == half - 1))
        halo_used = self.moved & (seq_index == half)
        halo_segment = self.segments[:, self.border - self.halo_rows : self.border]
        segment = jnp.concatenate([segment, halo_segment], axis=1)
        used = jnp.concatenate([used, halo_used], axis=1)
        alone = 1024 + seq_index * self.all_rows + jnp.arange(self.all_rows, dtype=jnp.int32)
        return jnp.where(used, segment, alone[None]), used


def far_gather(grid, value):
    rows, width, features = value.shape
    half = grid.seq_count // 2
    if half == 2:
        return [grid.send(value[row : row + 1], "x") for row in range(rows)]
    whole = lax.all_gather(value, "seq", axis=0)
    start = grid.seq_index // half * half
    whole = lax.dynamic_slice_in_dim(whole, start, half, 0)
    whole = whole.transpose(1, 0, 2, 3).reshape(rows, half * width, features)
    return [whole[row : row + 1] for row in range(rows)]


def far_ids(grid, items):
    half = grid.seq_count // 2
    if half == 2:
        return items.of(grid.seq_index ^ 1)[0]
    start = grid.seq_index // half * half
    ids = [
        jnp.where(start + part == grid.seq_index, -1, items.of(start + part)[0])
        for part in range(half)
    ]
    return jnp.concatenate(ids, axis=1)


def far_send(grid, value):
    half = grid.seq_count // 2
    if half == 2:
        return grid.send(value, "x")
    split = value.reshape(half, -1, value.shape[2])
    whole = jnp.zeros((grid.seq_count,) + split.shape[1:], jnp.bfloat16)
    start = grid.seq_index // half * half
    whole = lax.dynamic_update_slice_in_dim(whole, split, start, 0)
    return lax.psum_scatter(whole, "seq", scatter_dimension=0)[None]


def body(
    inputs,
    skip_inputs,
    out_cotangent,
    segments,
    occupied,
    skip_weight,
    skip_bias,
    first_gain,
    first_shift,
    qkv_weight,
    proj_weight,
    proj_bias,
    second_gain,
    second_shift,
    hidden_weight,
    hidden_bias,
    down_weight,
    down_bias,
):
    grid = Grid()
    own_rows, model = inputs.shape[1], inputs.shape[2]
    all_rows = -(-(own_rows + 16) // 32) * 32
    halo_rows = all_rows - own_rows
    half = grid.seq_count // 2
    vectors = [
        skip_bias,
        first_gain,
        first_shift,
        proj_bias,
        second_gain,
        second_shift,
        hidden_bias,
        down_bias,
    ]
    if grid.square:
        skip_way, vectors, skip_full = gather_skip(grid, skip_weight, vectors)
        mixed_piece = jnp.concatenate([qkv_weight, proj_weight], axis=1)
        mixed_way = Gather(grid, tie(mixed_piece, skip_way.column))
        mixed_way.first()
        mixed_way.second(skip_way.over_x, skip_way.over_y)
        mixed_way.last()
        mixed_way.spread()
        mixed_way.forward("y")
        for at in range(3):
            mixed_way.cross(at)
    else:
        vectors, wide = gather_plain(
            [skip_weight, qkv_weight, proj_weight, hidden_weight, down_weight], vectors
        )
        skip_full, qkv_full, proj_full, hidden_full, down_full = wide
        query_full, both_full = qkv_full[:, :model], qkv_full[:, model:]
        hidden_blocks = hidden_columns(hidden_full, model)
        down_blocks = down_full.reshape(-1, model, model)
    (
        skip_bias_full,
        gain_one,
        shift_one,
        proj_bias_full,
        gain_two,
        shift_two,
        hidden_bias_full,
        down_bias_full,
    ) = vectors
    joined_inputs = inputs
    if grid.square:
        joined_inputs = tie(inputs, skip_way.column)
        segments = tie(segments, skip_way.column)
    items = Items(grid, segments, occupied, own_rows, all_rows)
    query_ids, used = items.of(grid.seq_index)
    key_ids = jnp.concatenate([query_ids, far_ids(grid, items)], axis=1)
    tails = jnp.stack([v[:, own_rows - halo_rows :] for v in (inputs, skip_inputs, out_cotangent)])
    halo = grid.shift(tails, half - 1, half)
    first_tokens = jnp.concatenate([joined_inputs, halo[0]], axis=1)
    second_tokens = jnp.concatenate([skip_inputs, halo[1]], axis=1)
    query_ids, key_ids = query_ids[:, None, :], key_ids[:, :, None]
    used_rows = used.astype(jnp.float32).reshape(-1, 1)
    joined = jnp.concatenate([first_tokens, second_tokens], axis=2)
    joined, query_ids, key_ids, used_rows = lax.optimization_barrier(
        (joined, query_ids, key_ids, used_rows)
    )
    cotangent = jnp.concatenate([out_cotangent, halo[2]], axis=1)

    stream = dot_last(joined, skip_full) + skip_bias_full
    if grid.square:
        stream = tie(stream, mixed_way.crossed[0])
    first_low, first_normal, first_scale = layer_norm(stream, gain_one, shift_one)
    rows = inputs.shape[0]
    first_far = far_gather(grid, first_low)
    if grid.square:
        hidden_way = Gather(grid, tie(hidden_weight, stream))
        hidden_way.first()
        mixed_blocks = mixed_way.core(hidden_way.far)
        hidden_way.second(mixed_way.blocks[3])
        down_way = Gather(grid, tie(pack_lanes(down_weight), hidden_way.pair))
        down_way.first()
        query_full, both_full, proj_full = join_mixed(
            grid, mixed_blocks, mixed_way.order, *qkv_weight.shape, model
        )
        hidden_way.last(query_full)
        hidden_way.spread()
        down_way.second(query_full)
        both_full = tie(both_full, first_far[0], hidden_way.column, down_way.pair)
    own = dot_last(first_low, both_full).astype(jnp.bfloat16)
    if grid.square:
        query_full = tie(query_full, own, first_far[1])
    query = dot_last(first_low, query_full).astype(jnp.bfloat16)
    if grid.square:
        down_way.last(query)
        down_way.spread()
        hidden_way.cross(0)
        down_way.cross(0)
        first_far[0] = tie(first_far[0], query, down_way.column, *hidden_way.crossed)
    far, done = [], ()
    for row in range(rows):
        far.append(dot_last(first_far[row], both_full).astype(jnp.bfloat16))
        done = attend(query, own, far[row], query_ids, key_ids, row, *done)
        if row == 0 and grid.square:
            hidden_way.forward("y", done[0])
            down_way.forward("x", done[0])
            first_far[1] = tie(
                first_far[1],
                hidden_way.over_x,
                hidden_way.over_y,
                down_way.over_x,
                down_way.over_y,
                *down_way.crossed,
            )
            hidden_way.cross(1)
            hidden_way.cross(2)
    attended, level = done
    if grid.square:
        down_way.cross(1, attended, down_way.blocks[3])
        down_way.cross(2, attended, down_way.blocks[3])
        hidden_blocks = place_blocks(grid, hidden_way.core(attended), hidden_way.order)
        hidden_blocks = hidden_blocks.reshape(-1, model, model)
        down_blocks = join_down(grid, down_way.core(attended), down_way.order, *down_weight.shape)
    flat = (-1, model)
    (
        output,
        second_low,
        act_low,
        grad_pre,
        grad_middle,
        grad_proj,
        grad_attended,
        hidden_sums,
        middle_sums,
    ) = middle_block(
        stream.reshape(flat),
        attended.reshape(flat),
        cotangent.reshape(flat),
        used_rows,
        proj_full,
        hidden_blocks,
        down_blocks,
        proj_bias_full,
        gain_two,
        shift_two,
        hidden_bias_full,
        down_bias_full,
    )
    hidden_bias_grad = jnp.sum(hidden_sums, axis=0).reshape(-1)
    middle_sums = jnp.sum(middle_sums, axis=0)
    gain_two_grad, shift_two_grad = middle_sums[0], middle_sums[1]
    proj_bias_grad, down_bias_grad = middle_sums[2], middle_sums[3]
    grad_branch = jnp.where(used[..., None], cotangent, 0).reshape(flat)
    here, outer = grid.at["c"].astype(jnp.int32).reshape(1), grid.outer_count
    if grid.square:
        keep, give = tall_grad(act_low, grad_branch, here, outer, "down_weight_grad")
        down_way = Scatter(grid, keep, give, (outer, 2, 2) + keep.shape[2:])
        second_low = tie(second_low, give)
        keep, give = wide_grad(second_low, grad_pre, here, outer, "hidden_weight_grad")
        hidden_way = Scatter(grid, keep, give, (outer, -1, keep.shape[1]))
        down_way.pull(give)
        down_way.push("x", choose_dim(2))
        hidden_way.pull(down_way.sent)
        hidden_way.push("y", choose_lanes)
        grad_attended = tie(grad_attended, hidden_way.sent)
    else:
        down_grad = outer_dot(act_low, grad_branch)
        hidden_grad = outer_dot(second_low, grad_pre)
    output = output.reshape(stream.shape)
    grad_middle = grad_middle.reshape(stream.shape)
    grad_attended = grad_attended.reshape(stream.shape)

    grad_far, done = [], ()
    for row in range(rows):
        done = attend_back(
            query,
            own,
            far[row],
            attended,
            grad_attended,
            level,
            query_ids,
            key_ids,
            row,
            *done,
        )
        both_grad = done[1]
        if grid.square:
            down_way.pull(both_grad)
            hidden_way.pull(down_way.value)
            if row == 0:
                down_way.push("y", choose_dim(1))
                hidden_way.push("x", choose_lanes)
                both_grad = tie(both_grad, down_way.sent, hidden_way.sent)
            else:
                both_grad = tie(both_grad, down_way.value, hidden_way.value, *grad_far)
        share = dot_back(both_grad[row : row + 1, all_rows:], both_full).astype(jnp.bfloat16)
        grad_far.append(far_send(grid, share))
        done = (done[0], tie(both_grad, share))
    query_grad, both_grad = done
    both_flat = both_grad.reshape(-1, 2 * model)
    query_flat = query_grad.reshape(flat)
    if grid.square:
        keep, give = mixed_grad(
            first_low.reshape(flat),
            [value[0] for value in first_far],
            attended.reshape(flat),
            query_flat,
            both_flat,
            grad_proj,
            here,
            outer,
        )
        give = tie(give, *grad_far)
        mixed_way = Scatter(grid, keep, give, (outer, -1, keep.shape[1]))
        down_way.value = tie(down_way.value, give)
        hidden_way.value = tie(hidden_way.value, give)
        down_way.push("z", choose_half, 2)
        hidden_way.push("z", choose_odd, 1)
        query_grad = tie(query_grad, give, *grad_far)
        both_grad = tie(both_grad, give, *grad_far)
    else:
        first_all = [jnp.concatenate([first_low[row], first_far[row][0]]) for row in range(rows)]
        both_weight_grad = outer_dot(jnp.concatenate(first_all), both_flat)
        query_weight_grad = outer_dot(first_low.reshape(flat), query_flat)
        proj_grad = outer_dot(attended.reshape(flat), grad_proj)
    grad_first = dot_back(query_grad, query_full) + dot_back(both_grad[:, :all_rows], both_full)
    if grid.square:
        mixed_way.pull(grad_first)
        down_way.pull(mixed_way.value)
        down_way.push("z", choose_half, 1)
        hidden_way.pull(mixed_way.value)
        hidden_way.push("z", choose_half, 2)
        way_a, way_b = fork(mixed_way, 1, 8)
        way_a.push("y", choose_lanes)
        way_b.push("x", choose_odd_lanes)
        grad_first = tie(grad_first, way_a.sent, way_b.sent)
    grad_first = grad_first + jnp.concatenate(grad_far).astype(jnp.float32)
    grad_norm, gain_one_grad, shift_one_grad = layer_norm_back(
        grad_first, first_normal, first_scale, gain_one
    )
    grad_stream = (grad_middle + grad_norm).astype(jnp.bfloat16)
    skip_bias_grad = jnp.sum(grad_stream.astype(jnp.float32), axis=(0, 1))
    joined_flat, stream_flat = joined.reshape(-1, 2 * model), grad_stream.reshape(flat)
    if grid.square:
        keep, give = tall_grad(joined_flat, stream_flat, here, outer, "skip_weight_grad")
        skip_way = Scatter(grid, keep, give, (outer, 2, 2) + keep.shape[2:])
        grad_stream = tie(grad_stream, give)
    else:
        skip_weight_grad = outer_dot(joined_flat, stream_flat)
    vectors = scatter_vectors(
        grid,
        [
            skip_bias_grad,
            gain_one_grad,
            shift_one_grad,
            proj_bias_grad,
            gain_two_grad,
            shift_two_grad,
            hidden_bias_grad,
            down_bias_grad,
        ],
    )
    input_grad = dot_back(grad_stream, skip_full[:model])
    if grid.square:
        way_a.pull(input_grad)
        way_b.pull(input_grad)
        way_a.push("x", choose_lanes)
        way_b.push("y", choose_lanes)
        skip_way.pull(way_a.sent, way_b.sent)
        skip_a, skip_b = fork(skip_way, 3, 8)
        skip_a.push("x", choose_dim(2))
        skip_b.push("y", choose_dim(1))
        grad_stream = tie(grad_stream, skip_a.sent, skip_b.sent)
    skip_grad = dot_back(grad_stream, skip_full[model:])
    if grid.square:
        way_a.pull(skip_grad)
        way_b.pull(skip_grad)
        mixed_way.value = jnp.concatenate([way_a.value, way_b.value], axis=1)
        mixed_way.push("z", choose_half, 2)
        skip_a.pull(mixed_way.sent)
        skip_b.pull(mixed_way.sent)
        skip_a.push("y", choose_dim(1))
        skip_b.push("x", choose_dim(1))
        skip_a.pull()
        skip_b.pull()
        skip_way.value = jnp.concatenate([skip_a.value, skip_b.value], axis=1)
        skip_way.push("z", choose_odd, 1)
        mixed_way.pull(skip_way.sent)
        mixed_way.push("z", choose_half, 1)
        skip_way.pull(mixed_way.sent)
        skip_way.push("z", choose_half, 2)
        vectors = vectors(skip_way.sent)

        def tall_shard(way, shape):
            return unpack_lanes(wide_shard(way), *shape)

        def wide_shard(way):
            mine = tie(way.mine, skip_way.sent, mixed_way.sent)
            return (mine.astype(jnp.float32) + way.got.astype(jnp.float32))[0]

        down_shard = tall_shard(down_way, down_weight.shape)
        hidden_shard = wide_shard(hidden_way)
        skip_shard = tall_shard(skip_way, skip_weight.shape)
        mixed_shard = wide_shard(mixed_way)
        qkv_shard = mixed_shard[:, : qkv_weight.shape[1]]
        proj_shard = mixed_shard[:, qkv_weight.shape[1] :]
    else:
        down_shard = seq_scatter(down_grad)
        hidden_shard = seq_scatter(hidden_grad)
        skip_shard = seq_scatter(skip_weight_grad)
        proj_shard = seq_scatter(proj_grad)
        qkv_shard = seq_scatter(jnp.concatenate([query_weight_grad, both_weight_grad], axis=1))
        vectors = vectors()

    moved = items.moved[..., None] & (grid.seq_index == half - 1)
    results = [tie(output, skip_grad), input_grad, skip_grad]
    edge = own_rows - 16
    tails = jnp.stack([value[:, all_rows - 16 :].astype(jnp.float32) for value in results])
    tails = grid.shift(tails, half, half - 1)
    if grid.square:
        tails = tie(tails, skip_way.sent)

    def settle(place):
        own = results[place][:, :own_rows]
        tail = jnp.where(moved[:, -16:], tails[place].astype(own.dtype), own[:, edge:])
        return lax.dynamic_update_slice_in_dim(own, tail, edge, 1)

    return (
        settle(0),
        settle(1),
        settle(2),
        skip_shard,
        vectors[0],
        vectors[1],
        vectors[2],
        qkv_shard,
        proj_shard,
        vectors[3],
        vectors[4],
        vectors[5],
        hidden_shard,
        vectors[6],
        down_shard,
        vectors[7],
    )


def solution(mesh):
    return jax.shard_map(
        body,
        mesh=mesh,
        in_specs=(
            P("batch", "seq", None),
            P("batch", "seq", None),
            P("batch", "seq", None),
            P("batch", None),
            P("batch", None),
            P("batch", "seq"),
            P("seq"),
            P("seq"),
            P("seq"),
            P("batch", "seq"),
            P("batch", "seq"),
            P("seq"),
            P("seq"),
            P("seq"),
            P("batch", "seq"),
            P("seq"),
            P("batch", "seq"),
            P("seq"),
        ),
        out_specs=(
            P("batch", "seq", None),
            P("batch", "seq", None),
            P("batch", "seq", None),
            P("batch", "seq"),
            P("seq"),
            P("seq"),
            P("seq"),
            P("batch", "seq"),
            P("batch", "seq"),
            P("seq"),
            P("seq"),
            P("seq"),
            P("batch", "seq"),
            P("seq"),
            P("batch", "seq"),
            P("seq"),
        ),
        check_vma=False,
    )
```
